32 devices in a mesh: samp: 8 (over z, x), snp: 4 (over y, core).
Axes of the slice: x: 2, y: 2, z: 4, core: 2. Of those that a mesh axis runs over, the one named last changes fastest.
Arguments:
- genotype: bfloat16 [16384, 1024], P('samp', 'snp'), may hold values from -60 to 60
- phenotype: float32 [16384], P('samp'), may hold values from -6 to 6
- residual: float32 [16384], P('samp'), may hold values from -6 to 6
- sign_flips: int32 [16384, 127], P('samp'), may hold values from -1 to 1, as said below
- weights: bfloat16 [128, 49, 128], P('snp'), may hold values from -0.5 to 0.5
- member: int32 [128, 49], P('snp'), may hold values 0 or 1
- gene_start: int32 [128], P('snp'), may hold values from 0 to 1023, as said below
- gene_end: int32 [128], P('snp'), may hold values from 1 to 1024, as said below
Outputs:
- z_scores: float32 [128, 49, 128], P('snp')
The draws below stay inside these ranges and needn't reach their ends.
Inputs may be any that keep to these rules, and one draw needn't show every extreme that they name: `sign_flips`: each entry is -1 or 1. `gene_start`: gene g's start lies among the SNPs of block g // 32 of 256 SNPs, at or past (g % 32) * (8) within it and before the next such mark, except that the last gene starts at 1023; the first gene starts at 0. gene_end - gene_start lies between 1 and 128 and reaches 128 in every block of genes except possibly the last; gene_end is at most 1024, and the last gene ends at 1024.
All inputs are finite; a program needn't handle non-finite values. No bound on the sum of `member` on one device may be relied on, other than what follows from the above.
Results may differ from the reference program's by a relative error of at most 0.0041.
Values may be sent and summed in bfloat16 or wider, within the bound.
A program may use at most 64 MiB of HBM per device.

```python
import jax
import jax.numpy as jnp
from jax import lax

SNP_DEV = 256
GENE_DEV = 32
WIN = 128
TISSUE = 49
FLIPS = 127
SAMPLES = 16384
SNPS = 1024
GENES = 128


def draw_genotype(key, part):
    key_base, key_row, key_col = jax.random.split(key, 3)
    row_pos = jnp.arange(SAMPLES, dtype=jnp.float32)[:, None] / (SAMPLES - 1)
    row_scale = 10.0 ** jax.random.uniform(key_row, (SAMPLES, 1)) * (1.0 + 2.0 * row_pos)
    col_scale = 0.5 + 1.5 * jax.random.uniform(key_col, (1, SNPS))
    values = jnp.clip(jax.random.normal(key_base, (SAMPLES, SNPS)), -4.0, 4.0)
    return (0.2 * values * row_scale * col_scale).astype(jnp.bfloat16)


def draw_sign_flips(key, part):
    coins = jax.random.randint(jax.random.fold_in(key, 3), (SAMPLES, FLIPS), 0, 2)
    return (2 * coins - 1).astype(jnp.int32)


def gene_windows(key):
    key_place, key_span = jax.random.split(jax.random.fold_in(key, 11), 2)
    spacing = SNP_DEV // GENE_DEV
    gene_ids = jnp.arange(GENES, dtype=jnp.int32)
    block_index = gene_ids // GENE_DEV
    slot_index = gene_ids % GENE_DEV
    first_snp = block_index * SNP_DEV + slot_index * spacing + jax.random.randint(key_place, (GENES,), 0, spacing)
    first_snp = jnp.where(gene_ids == 0, 0, first_snp)
    first_snp = jnp.where(gene_ids == GENES - 1, SNPS - 1, first_snp)
    length = jax.random.randint(key_span, (GENES,), WIN // 4, WIN + 1)
    length = jnp.where(slot_index == GENE_DEV - 1, WIN, length)
    last_snp = jnp.minimum(first_snp + length, SNPS)
    return (first_snp.astype(jnp.int32), last_snp.astype(jnp.int32))


def draw_gene_start(key, part):
    return gene_windows(key)[0]


def draw_gene_end(key, part):
    return gene_windows(key)[1]


def with_ends(drawn, rng, least, top_value):
    shape = drawn.shape
    place = [jax.random.randint(jax.random.fold_in(rng, axis), (), 0, shape[axis]) for axis in range(len(shape))]
    drawn = drawn.at[tuple(place)].set(least)
    longest = shape.index(max(shape))
    place[longest] = (place[longest] + 1) % shape[longest]
    return drawn.at[tuple(place)].set(top_value)


def steps_of(own_key, dims, cuts, low, top_value):
    level, own = 1.0, jax.random.fold_in(own_key, 6)
    for position, shards_of in cuts:
        heights = jnp.exp(jax.random.uniform(jax.random.fold_in(own, position), (shards_of,), jnp.float32, low / len(cuts), top_value / len(cuts)))
        level = level * jnp.repeat(heights, dims[position] // shards_of).reshape([-1 if axis == position else 1 for axis in range(len(dims))])
    return level


def noise(stream_key, extent, scale, limit, cuts=(), kind=jnp.bfloat16):
    drawn = scale * jax.random.normal(stream_key, extent, jnp.float32)
    if cuts:
        drawn = drawn * steps_of(stream_key, extent, cuts, -0.22, 0.18)
    return jnp.clip(drawn, -limit, limit).astype(kind)


def setup_inputs(seed: int = 0) -> dict:
    arg_keys = jax.random.split(jax.random.key(seed), 9)
    genotype = draw_genotype(jax.random.fold_in(arg_keys[8], 71), 0)
    phenotype = noise(arg_keys[1], (SAMPLES,), 1.0, 6.0, ((0, 8),), jnp.float32)
    residual = noise(arg_keys[2], (SAMPLES,), 1.0, 6.0, ((0, 8),), jnp.float32)
    sign_flips = draw_sign_flips(jax.random.fold_in(arg_keys[8], 71), 0)
    weights = noise(arg_keys[4], (GENES, TISSUE, WIN), WIN ** -0.5, 0.5, ((0, 4),))
    member = with_ends((jax.random.randint(arg_keys[5], (GENES, TISSUE), 0, 4) < 3).astype(jnp.int32), jax.random.fold_in(arg_keys[5], 1), 0, 1)
    gene_start = draw_gene_start(jax.random.fold_in(arg_keys[8], 71), 0)
    gene_end = draw_gene_end(jax.random.fold_in(arg_keys[8], 71), 0)
    return {"genotype": genotype, "phenotype": phenotype, "residual": residual, "sign_flips": sign_flips, "weights": weights, "member": member, "gene_start": gene_start, "gene_end": gene_end}


def reference(genotype, phenotype, residual, sign_flips, weights, member, gene_start, gene_end):
    sample_total = genotype.shape[0]
    padded = jnp.pad(genotype, ((0, 0), (0, WIN)))
    labels = jnp.concatenate([phenotype[:, None], residual[:, None] * sign_flips.astype(jnp.float32)], axis=1)
    labels = lax.optimization_barrier(labels.astype(jnp.bfloat16)).astype(jnp.float32)
    sum_lab = lax.optimization_barrier(jnp.sum(labels, axis=0))
    window_pos = jnp.arange(WIN, dtype=jnp.int32)
    scale_root = jnp.sqrt(jnp.asarray(sample_total, dtype=jnp.float32))

    def one_gene(items):
        gene_wts, gene_mem, gene_first, gene_last = items
        window = lax.dynamic_slice_in_dim(padded, gene_first.astype(jnp.int32), WIN, 1).astype(jnp.float32)
        inside_mask = (window_pos < gene_last - gene_first).astype(jnp.float32)
        window_wts = gene_wts.astype(jnp.float32) * gene_mem.astype(jnp.float32)[:, None] * inside_mask[None, :]
        predicted = jnp.dot(window, window_wts.T, precision=lax.Precision.HIGHEST)
        predicted = lax.optimization_barrier(predicted.astype(jnp.bfloat16)).astype(jnp.float32)
        sum_pred = lax.optimization_barrier(jnp.sum(predicted, axis=0))
        sum_sq = lax.optimization_barrier(jnp.sum(predicted * predicted, axis=0))
        cross_prod = jnp.dot(predicted.T, labels, precision=lax.Precision.HIGHEST)
        col_mean = sum_pred / sample_total
        col_spread = jnp.sqrt(sum_sq / sample_total - col_mean * col_mean + 1e-06)
        return (cross_prod - col_mean[:, None] * sum_lab[None, :]) / (col_spread[:, None] * scale_root)
    return lax.map(one_gene, (weights, member, gene_start, gene_end))
```

```python
import functools

import jax
import jax.numpy as jnp
from jax import lax
from jax.experimental import pallas as pl
from jax.experimental.pallas import tpu as pltpu
from jax.sharding import PartitionSpec as P

MESH = pl.DeviceIdType.MESH
TILE = 16
PARTS = 4
VMEM_LIMIT = 24 * 1024 * 1024


def across(left, right):
    return lax.dot_general(left, right, (((0,), (0,)), ((), ())), preferred_element_type=jnp.float32)


def iotas(rows, cols):
    return (
        lax.broadcasted_iota(jnp.int32, (rows, cols), 0),
        lax.broadcasted_iota(jnp.int32, (rows, cols), 1),
    )


def share_of(rows, count):
    per = -(-rows // (count * TILE)) * TILE
    while rows % per:
        per += TILE
    return per


def square_of(rows):
    tiles, width = rows.shape
    return jnp.concatenate([rows, jnp.zeros((width - tiles, width), jnp.float32)], axis=0)


def sums_kernel(
    count, ring, window,
    geno, phen, resid, flips, starts, ends, member, weights,
    near_out, far_out, corner_out, placed_out,
    phen_v, resid_v, starts_v, ends_v, member_v, weights_v,
    geno_v, flips_v, halo_v, labels_v,
    main_s, main_r, main_p, main_g,
    corner_s, corner_r, corner_p, corner_g,
    tail_v, tail_sums, sums_s, sums_r, sums_t, cols_v,
    load_sem, flip_sem, small_sem, halo_ss, halo_rs,
    ms_ss, ms_rs, mg_ss, mg_rs, cs_ss, cs_rs, cg_ss, cg_rs,
    sm_ss, sm_rs, tl_ss, tl_rs,
):
    me = lax.axis_index("samp")
    mine = lax.axis_index("snp")
    has_before = mine > 0
    has_after = mine < ring - 1
    before = jnp.maximum(mine - 1, 0)
    after = jnp.minimum(mine + 1, ring - 1)
    samples, snps = geno_v.shape
    blocks = snps // window
    part = samples // PARTS
    owners, per = corner_g.shape[0], corner_g.shape[1]
    inverse = 1.0 / (samples * count)

    def peers(body):
        if count <= 16:
            for dist in range(1, count):
                body(dist)
        else:
            def step(dist, carry):
                body(dist)
                return carry
            lax.fori_loop(1, count, step, 0)

    def ahead(dist):
        return lax.rem(me + dist, count)

    def behind(dist):
        return lax.rem(me + count - dist, count)

    barrier = pltpu.get_barrier_semaphore()
    peers(lambda dist: pl.semaphore_signal(
        barrier, inc=1, device_id=(ahead(dist), mine), device_id_type=MESH))

    @pl.when(has_before)
    def _():
        pl.semaphore_signal(barrier, inc=1, device_id=(me, before), device_id_type=MESH)

    @pl.when(has_after)
    def _():
        pl.semaphore_signal(barrier, inc=1, device_id=(me, after), device_id_type=MESH)

    small = [
        pltpu.make_async_copy(src, dst, small_sem.at[i])
        for i, (src, dst) in enumerate((
            (resid, resid_v), (phen, phen_v), (starts, starts_v), (ends, ends_v),
            (member, member_v), (weights, weights_v),
        ))
    ]
    loads, flip_loads = [], []
    for copy in small[:2]:
        copy.start()
    for i in range(PARTS):
        rows = pl.ds(i * part, part)
        loads.append(pltpu.make_async_copy(geno.at[rows], geno_v.at[rows], load_sem.at[i]))
        flip_loads.append(pltpu.make_async_copy(flips.at[rows], flips_v.at[rows], flip_sem.at[i]))
        flip_loads[i].start()
        loads[i].start()
    for copy in small[2:]:
        copy.start()

    flip_count = flips_v.shape[1]
    for copy in small[:2]:
        copy.wait()
    phen_cols = square_of(phen_v[...]).T
    resid_cols = square_of(resid_v[...]).T
    lanes = phen_v.shape[1]
    for i in range(PARTS):
        flip_loads[i].wait()
        for t in range(i * part // lanes, (i + 1) * part // lanes):
            rows = pl.ds(t * lanes, lanes)
            signs = flips_v[rows, :].astype(jnp.float32)
            labels_v[rows, pl.ds(0, flip_count)] = (signs * resid_cols[:, t:t + 1]).astype(jnp.bfloat16)
            labels_v[rows, pl.ds(flip_count, 1)] = phen_cols[:, t:t + 1].astype(jnp.bfloat16)

    both = has_before & has_after

    @pl.when(both)
    def _():
        pl.semaphore_wait(barrier, count + 1)

    @pl.when(jnp.logical_not(both))
    def _():
        pl.semaphore_wait(barrier, count if ring > 1 else count - 1)

    def remote(src, dst, ss, rs, device):
        return pltpu.make_async_remote_copy(
            src_ref=src, dst_ref=dst, send_sem=ss, recv_sem=rs,
            device_id=device, device_id_type=MESH)

    halos = []
    for i in range(PARTS):
        rows = pl.ds(i * part, part)
        halos.append(remote(
            geno.at[rows, pl.ds(0, window)], halo_v.at[rows],
            halo_ss.at[i], halo_rs.at[i], (me, before)))

    @pl.when(has_before)
    def _():
        for copy in halos:
            copy.start()

    def guarded(index, body):
        if owners == count:
            body()
        else:
            pl.when(index < owners)(body)

    class Exchange:
        def __init__(self, send, got, piece, full, ss, rs, gss, grs):
            self.send, self.got, self.piece, self.full = send, got, piece, full
            self.ss, self.rs, self.gss, self.grs = ss, rs, gss, grs

        def scatter_copy(self, dist):
            return remote(
                self.send.at[ahead(dist)], self.got.at[dist],
                self.ss.at[dist], self.rs.at[dist], (ahead(dist), mine))

        def gather_copy(self, dist, slot):
            return remote(
                self.piece, self.full.at[slot],
                self.gss.at[dist], self.grs.at[dist], (ahead(dist), mine))

        def scatter(self):
            peers(lambda dist: guarded(ahead(dist), lambda: self.scatter_copy(dist).start()))

        def reduce(self, finish):
            def owner():
                total = self.send[me].astype(jnp.float32)
                if count <= 16:
                    for dist in range(1, count):
                        self.scatter_copy(dist).wait_recv()
                        total += self.got[dist].astype(jnp.float32)
                else:
                    def step(dist, total):
                        self.scatter_copy(dist).wait_recv()
                        return total + self.got[dist].astype(jnp.float32)
                    total = lax.fori_loop(1, count, step, total)
                self.piece[...] = finish(total).astype(self.piece.dtype)
                peers(lambda dist: self.gather_copy(dist, me).start())
                self.full[me] = self.piece[...]
            guarded(me, owner)

        def gather_wait(self):
            peers(lambda dist: guarded(
                behind(dist), lambda: self.gather_copy(dist, behind(dist)).wait_recv()))

        def sends_wait(self):
            peers(lambda dist: guarded(ahead(dist), lambda: self.scatter_copy(dist).wait_send()))
            guarded(me, lambda: peers(lambda dist: self.gather_copy(dist, me).wait_send()))

    main = [
        Exchange(
            main_s.at[b], main_r.at[b], main_p.at[b], main_g.at[b],
            ms_ss.at[b], ms_rs.at[b], mg_ss.at[b], mg_rs.at[b])
        for b in range(blocks)
    ]
    edge = Exchange(corner_s, corner_r, corner_p, corner_g, cs_ss, cs_rs, cg_ss, cg_rs)

    for i in range(PARTS):
        loads[i].wait()
    own = geno_v[...]
    labels = labels_v[...]
    with_labels = across(own, labels)
    gram = across(own, own)
    ones = jnp.ones((8, samples), jnp.bfloat16)
    col_sums = jnp.dot(ones, own, preferred_element_type=jnp.float32)
    lab_sums = jnp.dot(ones, labels, preferred_element_type=jnp.float32)
    row8, _ = iotas(8, window)
    sums = jnp.where(row8 == blocks, lab_sums, 0.0)
    for b in range(blocks):
        sums = jnp.where(row8 == b, col_sums[:, b * window:(b + 1) * window], sums)
    sums_s[...] = sums

    def sums_copy(dist):
        return remote(sums_s, sums_r.at[dist], sm_ss.at[dist], sm_rs.at[dist], (ahead(dist), mine))

    peers(lambda dist: sums_copy(dist).start())
    row, col = iotas(window, window)
    for b in range(blocks):
        low, mid, high = b * window, (b + 1) * window, (b + 2) * window
        beyond = gram[low:mid, mid:high] if b < blocks - 1 else 0.0
        band = jnp.where(col >= row, gram[low:mid, low:mid], beyond)
        main_s[b, :, pl.ds(0, per), :] = with_labels[low:mid].astype(jnp.bfloat16).reshape(owners, per, window)
        main_s[b, :, pl.ds(per, per), :] = band.astype(jnp.bfloat16).reshape(owners, per, window)
        main[b].scatter()

    for copy in small[2:]:
        copy.wait()
    place(mine * snps, starts_v, ends_v, member_v, weights_v, placed_out)

    total = sums_s[...]
    if count <= 16:
        for dist in range(1, count):
            sums_copy(dist).wait_recv()
            total += sums_r[dist]
    else:
        def step(dist, total):
            sums_copy(dist).wait_recv()
            return total + sums_r[dist]
        total = lax.fori_loop(1, count, step, total)
    sums_t[...] = total
    cols_v[...] = square_of(total).T
    tail_copies = [remote(sums_t, tail_sums, tl_ss.at[0], tl_rs.at[0], (me, before))]

    @pl.when(has_before)
    def _():
        tail_copies[0].start()

    my_rows = pl.ds(pl.multiple_of(me * per, per), per) if owners == count else pl.ds(
        pl.multiple_of(jnp.minimum(me, owners - 1) * per, per), per)
    row_of, col_of = iotas(per, window)
    row_of = row_of + me * per

    def mean_col(b):
        return cols_v[my_rows, :][:, b:b + 1] * inverse

    def finish_main(b):
        def finish(total):
            at = mean_col(b)
            scored = total[:per] - at * sums_t[blocks:blocks + 1, :]
            scored = pltpu.roll(scored, 1, 1)
            mean_row = sums_t[b:b + 1, :] * inverse
            if b < blocks - 1:
                mean_row = jnp.where(col_of >= row_of, mean_row, sums_t[b + 1:b + 2, :] * inverse)
            value = total[per:] * inverse - at * mean_row
            value = jnp.where(col_of == row_of, value, 2.0 * value)
            if b == blocks - 1:
                value = jnp.where(col_of >= row_of, value, 0.0)
            return jnp.concatenate([scored, value], axis=0)
        return finish

    for b in range(blocks):
        main[b].reduce(finish_main(b))

    last = snps - window

    @pl.when(has_after)
    def _():
        corner = jnp.zeros((window, window), jnp.float32)
        for i in range(PARTS):
            rows = pl.ds(i * part, part)
            halos[i].wait_recv()
            corner += across(geno_v[rows, pl.ds(last, window)], halo_v[rows, :])
        corner_s[...] = corner.astype(jnp.bfloat16).reshape(owners, per, window)
        edge.scatter()

    main[0].gather_wait()
    tail_copies.append(remote(main_g.at[0], tail_v, tl_ss.at[1], tl_rs.at[1], (me, before)))

    @pl.when(has_before)
    def _():
        tail_copies[1].start()

    def finish_edge(total):
        value = total * inverse - mean_col(blocks - 1) * (tail_sums[0:1, :] * inverse)
        return jnp.where(col_of < row_of, 2.0 * value, 0.0)

    @pl.when(has_after)
    def _():
        tail_copies[0].wait_recv()
        edge.reduce(finish_edge)

    for b in range(1, blocks):
        main[b].gather_wait()
    near_out[...] = main_g[...]

    @pl.when(has_after)
    def _():
        edge.gather_wait()
        corner_out[...] = corner_g[...]
        tail_copies[1].wait_recv()
        far_out[...] = tail_v[...]

    @pl.when(jnp.logical_not(has_after))
    def _():
        corner_out[...] = jnp.zeros_like(corner_out)
        far_out[...] = jnp.zeros_like(far_out)

    @pl.when(has_before)
    def _():
        for copy in halos + tail_copies:
            copy.wait_send()
    peers(lambda dist: sums_copy(dist).wait_send())
    for exchange in main:
        exchange.sends_wait()
    pl.when(has_after)(edge.sends_wait)


def place(offset, starts, ends, member, weights, placed):
    tissues, genes, window = weights.shape
    blocks = placed.shape[0]
    per_block = genes // blocks
    spacing = window // per_block
    gene_row, gene_col = iotas(genes, genes)

    def upright(row_ref):
        spread = jnp.broadcast_to(row_ref[...].astype(jnp.float32), (genes, genes))
        picked = jnp.where(gene_row == gene_col, spread, 0.0)
        return jnp.sum(picked, axis=1, keepdims=True).astype(jnp.int32)

    first, past = upright(starts), upright(ends)
    gene, lane = iotas(genes, window)
    inside = (lane < past - first).astype(jnp.float32)
    within = first - offset - (gene // per_block) * window
    extra = within - (gene % per_block) * spacing
    owned = member[...].astype(jnp.float32)
    for t in range(tissues):
        values = weights[t].astype(jnp.float32) * owned[:, t:t + 1] * inside
        bit = 1
        while bit < spacing:
            values = jnp.where((extra & bit) != 0, pltpu.roll(values, bit, 1), values)
            bit *= 2
        for b in range(blocks):
            genes_of = slice(b * per_block, (b + 1) * per_block)
            turned = pltpu.roll(values[genes_of], 0, 1, stride=spacing, stride_axis=0)
            kept = lane[genes_of] >= within[genes_of]
            rows = pl.ds(t * per_block, per_block)
            placed[b, rows, pl.ds(0, window)] = jnp.where(kept, turned, 0.0).astype(jnp.bfloat16)
            placed[b, rows, pl.ds(window, window)] = jnp.where(kept, 0.0, turned).astype(jnp.bfloat16)


def reduced_sums(genotype, phenotype, residual, sign_flips, starts, ends, member, weights):
    samples, snps = genotype.shape
    tissues, genes, window = weights.shape
    count, ring = lax.axis_size("samp"), lax.axis_size("snp")
    blocks = snps // window
    per = share_of(window, count)
    owners = window // per
    half, wide = jnp.bfloat16, jnp.float32
    dma = pltpu.SemaphoreType.DMA
    vmem = pl.BlockSpec(memory_space=pltpu.VMEM)
    hbm = pl.BlockSpec(memory_space=pltpu.HBM)
    operands = (
        genotype, phenotype.reshape(-1, window), residual.reshape(-1, window), sign_flips,
        starts.reshape(1, genes), ends.reshape(1, genes), member, weights,
    )
    return pl.pallas_call(
        functools.partial(sums_kernel, count, ring, window),
        out_shape=(
            jax.ShapeDtypeStruct((blocks, owners, 2 * per, window), half),
            jax.ShapeDtypeStruct((owners, 2 * per, window), half),
            jax.ShapeDtypeStruct((owners, per, window), half),
            jax.ShapeDtypeStruct((blocks, tissues * genes // blocks, 2 * window), half),
        ),
        in_specs=[hbm] * 8,
        out_specs=(vmem,) * 4,
        scratch_shapes=[pltpu.VMEM(x.shape, x.dtype) for x in operands[1:3] + operands[4:]] + [
            pltpu.VMEM((samples, snps), half),
            pltpu.VMEM(sign_flips.shape, jnp.int32),
            pltpu.VMEM((samples, window), half),
            pltpu.VMEM((samples, window), half),
            pltpu.VMEM((blocks, owners, 2 * per, window), half),
            pltpu.VMEM((blocks, count, 2 * per, window), half),
            pltpu.VMEM((blocks, 2 * per, window), half),
            pltpu.VMEM((blocks, owners, 2 * per, window), half),
            pltpu.VMEM((owners, per, window), half),
            pltpu.VMEM((count, per, window), half),
            pltpu.VMEM((per, window), half),
            pltpu.VMEM((owners, per, window), half),
            pltpu.VMEM((owners, 2 * per, window), half),
            pltpu.VMEM((8, window), wide),
            pltpu.VMEM((8, window), wide),
            pltpu.VMEM((count, 8, window), wide),
            pltpu.VMEM((8, window), wide),
            pltpu.VMEM((window, window), wide),
            dma((PARTS,)), dma((PARTS,)), dma((6,)), dma((PARTS,)), dma((PARTS,)),
            dma((blocks, count)), dma((blocks, count)), dma((blocks, count)), dma((blocks, count)),
            dma((count,)), dma((count,)), dma((count,)), dma((count,)),
            dma((count,)), dma((count,)), dma((2,)), dma((2,)),
        ],
        compiler_params=pltpu.CompilerParams(
            collective_id=0, has_side_effects=True, vmem_limit_bytes=VMEM_LIMIT),
        name="sums",
    )(*(pltpu.with_memory_space_constraint(x, pltpu.HBM) for x in operands))


def scores_kernel(sample_total, near, far, corner, placed, out_hbm, out, sem):
    tissues, genes, window = out.shape
    blocks = placed.shape[0]
    per_block = genes // blocks
    per = corner.shape[1]
    row, col = iotas(window, window)
    root = 1.0 / (sample_total ** 0.5)

    def piece(ref, at):
        return ref[:, pl.ds(at, per), :].reshape(window, window)

    def source(b):
        return near.at[b] if b < blocks else far

    def masked(keep, value):
        return jnp.where(keep, value.astype(jnp.float32), 0.0).astype(jnp.bfloat16)

    labelled = [piece(source(b), 0) for b in range(blocks + 1)]
    banded = [piece(source(b), per) for b in range(blocks + 1)]
    diagonal = [masked(col >= row, band) for band in banded]
    beside = [masked(col < row, band) for band in banded[:blocks - 1]] + [piece(corner, 0)]
    nothing = jnp.zeros((window, window), jnp.bfloat16)
    pairs, bands = [], []
    for b in range(blocks):
        pairs.append(jnp.concatenate([labelled[b], labelled[b + 1]], axis=0))
        bands.append(jnp.concatenate([
            jnp.concatenate([diagonal[b], beside[b]], axis=1),
            jnp.concatenate([nothing, diagonal[b + 1]], axis=1),
        ], axis=0))

    copies = []
    step = next(n for n in range(min(7, tissues), 0, -1) if tissues % n == 0)
    for t in range(0, tissues, step):
        for b in range(blocks):
            half = placed[b, pl.ds(t * per_block, step * per_block), :]
            top = jnp.dot(half, pairs[b], preferred_element_type=jnp.float32)
            square = jnp.dot(half, bands[b], preferred_element_type=jnp.float32)
            variance = jnp.sum(square * half.astype(jnp.float32), axis=1, keepdims=True)
            scale = lax.rsqrt(jnp.maximum(variance, 0.0) + 1e-06) * root
            out[pl.ds(t, step), pl.ds(b * per_block, per_block), :] = (top * scale).reshape(step, per_block, window)
        part = pl.ds(t, step)
        copies.append(pltpu.make_async_copy(out.at[part], out_hbm.at[part], sem.at[t // step]))
        copies[-1].start()
    for copy in copies:
        copy.wait()


def on_device(genotype, phenotype, residual, sign_flips, weights, member, gene_start, gene_end):
    by_tissue = weights.transpose(1, 0, 2)
    near, far, corner, placed = reduced_sums(
        genotype, phenotype, residual, sign_flips, gene_start, gene_end, member, by_tissue)
    vmem = pl.BlockSpec(memory_space=pltpu.VMEM)
    scores = pl.pallas_call(
        functools.partial(scores_kernel, genotype.shape[0] * lax.axis_size("samp")),
        out_shape=jax.ShapeDtypeStruct(by_tissue.shape, jnp.float32),
        in_specs=[vmem] * 4,
        out_specs=pl.BlockSpec(memory_space=pltpu.HBM),
        scratch_shapes=[
            pltpu.VMEM(by_tissue.shape, jnp.float32),
            pltpu.SemaphoreType.DMA((by_tissue.shape[0],)),
        ],
        compiler_params=pltpu.CompilerParams(vmem_limit_bytes=VMEM_LIMIT),
        name="scores",
    )(near, far, corner, placed)
    return scores.transpose(1, 0, 2)


def solution(mesh):
    return jax.shard_map(
        on_device,
        mesh=mesh,
        in_specs=(
            P("samp", "snp"),
            P("samp"),
            P("samp"),
            P("samp", None),
            P("snp", None, None),
            P("snp", None),
            P("snp"),
            P("snp"),
        ),
        out_specs=P("snp", None, None),
        check_vma=False,
    )
```

```python
import functools

import jax
import jax.numpy as jnp
from jax import lax
from jax.experimental import pallas as pl
from jax.experimental.pallas import tpu as pltpu
from jax.sharding import PartitionSpec as P

MESH = pl.DeviceIdType.MESH
TILE = 16
PARTS = 4
VMEM_LIMIT = 24 * 1024 * 1024


def across(left, right):
    return lax.dot_general(left, right, (((0,), (0,)), ((), ())), preferred_element_type=jnp.float32)


def iotas(rows, cols):
    return (
        lax.broadcasted_iota(jnp.int32, (rows, cols), 0),
        lax.broadcasted_iota(jnp.int32, (rows, cols), 1),
    )


def share_of(rows, count):
    per = -(-rows // (count * TILE)) * TILE
    while rows % per:
        per += TILE
    return per


def square_of(rows):
    tiles, width = rows.shape
    return jnp.concatenate([rows, jnp.zeros((width - tiles, width), jnp.float32)], axis=0)


def sums_kernel(
    count, ring, window,
    geno, phen, resid, flips, starts, ends, member, weights,
    near_out, far_out, corner_out, placed_out,
    phen_v, resid_v, starts_v, ends_v, member_v, weights_v,
    data_v, flips_v, halo_v,
    main_s, main_r, main_p, main_g,
    late_s, late_r, tail_v, tail_sums, sums_s, sums_r, sums_t, cols_v,
    load_sem, flip_sem, small_sem, halo_ss, halo_rs,
    ms_ss, ms_rs, mg_ss, mg_rs, lt_ss, lt_rs, td_ss, td_rs,
    sm_ss, sm_rs, tl_ss, tl_rs,
):
    me = lax.axis_index("samp")
    mine = lax.axis_index("snp")
    has_before = mine > 0
    has_after = mine < ring - 1
    odd = lax.rem(mine, 2) == 1
    even = lax.rem(mine, 2) == 0
    before = jnp.maximum(mine - 1, 0)
    after = jnp.minimum(mine + 1, ring - 1)
    samples = data_v.shape[0]
    owners, bands, per, _ = main_g.shape
    blocks = bands // 2
    snps = blocks * window
    part = samples // PARTS
    inverse = 1.0 / (samples * count)

    def peers(body, first=1):
        if count <= 16:
            for dist in range(first, count):
                body(dist)
        else:
            def step(dist, carry):
                body(dist)
                return carry
            lax.fori_loop(first, count, step, 0)

    def collect(wait, got, total):
        if count <= 16:
            for dist in range(1, count):
                wait(dist)
                total += got[dist].astype(jnp.float32)
            return total

        def step(dist, total):
            wait(dist)
            return total + got[dist].astype(jnp.float32)
        return lax.fori_loop(1, count, step, total)

    def ahead(dist):
        return lax.rem(me + dist, count)

    def behind(dist):
        return lax.rem(me + count - dist, count)

    barrier = pltpu.get_barrier_semaphore()

    def greet(dist, other):
        pl.semaphore_signal(barrier, inc=1, device_id=(ahead(dist), other), device_id_type=MESH)

    peers(lambda dist: greet(dist, mine))
    pl.when(has_before & even)(lambda: peers(lambda dist: greet(dist, before), 0))
    pl.when(has_before & odd)(lambda: greet(0, before))
    pl.when(has_after & odd)(lambda: peers(lambda dist: greet(dist, after), 0))
    pl.when(has_after & even)(lambda: greet(0, after))

    small = [
        pltpu.make_async_copy(src, dst, small_sem.at[i])
        for i, (src, dst) in enumerate((
            (resid, resid_v), (phen, phen_v), (starts, starts_v), (ends, ends_v),
            (member, member_v), (weights, weights_v),
        ))
    ]
    loads, flip_loads = [], []
    for copy in small[:2]:
        copy.start()
    for i in range(PARTS):
        rows = pl.ds(i * part, part)
        loads.append(pltpu.make_async_copy(
            geno.at[rows], data_v.at[rows, pl.ds(0, snps)], load_sem.at[i]))
        flip_loads.append(pltpu.make_async_copy(flips.at[rows], flips_v.at[rows], flip_sem.at[i]))
        flip_loads[i].start()
        loads[i].start()
    for copy in small[2:]:
        copy.start()

    for copy in small[:2]:
        copy.wait()
    phen_cols = square_of(phen_v[...]).T
    resid_cols = square_of(resid_v[...]).T
    lanes = phen_v.shape[1]
    for i in range(PARTS):
        flip_loads[i].wait()
        for t in range(i * part // lanes, (i + 1) * part // lanes):
            rows = pl.ds(t * lanes, lanes)
            signs = flips_v[rows, :].astype(jnp.float32)
            labels = jnp.concatenate([signs * resid_cols[:, t:t + 1], phen_cols[:, t:t + 1]], axis=1)
            data_v[rows, pl.ds(snps, window)] = labels.astype(jnp.bfloat16)

    from_before = jnp.where(has_before, jnp.where(even, count, 1), 0)
    from_after = jnp.where(has_after, jnp.where(even, 1, count), 0)
    pl.semaphore_wait(barrier, count - 1 + from_before + from_after)

    def remote(src, dst, ss, rs, device):
        return pltpu.make_async_remote_copy(
            src_ref=src, dst_ref=dst, send_sem=ss, recv_sem=rs,
            device_id=device, device_id_type=MESH)

    halos = []
    for i in range(PARTS):
        rows = pl.ds(i * part, part)
        halos.append(remote(
            geno.at[rows, pl.ds(0, window)], halo_v.at[rows],
            halo_ss.at[i], halo_rs.at[i], (me, before)))

    @pl.when(has_before)
    def _():
        for copy in halos:
            copy.start()

    def guarded(index, body):
        if owners == count:
            body()
        else:
            pl.when(index < owners)(body)

    def scatter_copy(dist):
        return remote(
            main_s.at[ahead(dist)], main_r.at[dist], ms_ss.at[dist], ms_rs.at[dist], (ahead(dist), mine))

    def gather_copy(dist, slot):
        return remote(main_p, main_g.at[slot], mg_ss.at[dist], mg_rs.at[dist], (ahead(dist), mine))

    def direct_copy(dist, slot):
        return remote(
            main_p.at[pl.ds(0, 2)], tail_v.at[slot], td_ss.at[dist], td_rs.at[dist], (ahead(dist), before))

    def sums_copy(dist):
        return remote(sums_s, sums_r.at[dist], sm_ss.at[dist], sm_rs.at[dist], (ahead(dist), mine))

    def late_copy(dist):
        return remote(late_s, late_r.at[dist], lt_ss.at[dist], lt_rs.at[dist], (ahead(dist), mine))

    tail_copies = [
        remote(sums_t, tail_sums, tl_ss.at[0], tl_rs.at[0], (me, before)),
        remote(main_g.at[:, pl.ds(0, 2)], tail_v, tl_ss.at[1], tl_rs.at[1], (me, before)),
    ]

    for i in range(PARTS):
        loads[i].wait()
    data = data_v[...]
    left = jnp.concatenate([data[:, :snps], jnp.ones((samples, 8), jnp.bfloat16)], axis=1)
    products = across(left, data)
    row8, _ = iotas(8, window)
    sums = jnp.zeros((8, window), jnp.float32)
    for b in range(blocks + 1):
        sums = jnp.where(row8 == b, products[snps:, b * window:(b + 1) * window], sums)
    sums_s[...] = sums
    peers(lambda dist: sums_copy(dist).start())
    row, col = iotas(window, window)
    for b in range(blocks):
        low, mid, high = b * window, (b + 1) * window, (b + 2) * window
        beyond = products[low:mid, mid:high] if b < blocks - 1 else 0.0
        band = jnp.where(col >= row, products[low:mid, low:mid], beyond)
        main_s[:, 2 * b] = products[low:mid, snps:].astype(jnp.bfloat16).reshape(owners, per, window)
        main_s[:, 2 * b + 1] = band.astype(jnp.bfloat16).reshape(owners, per, window)
    peers(lambda dist: guarded(ahead(dist), lambda: scatter_copy(dist).start()))

    half = window // 2
    half_row, half_col = iotas(half, window)

    def corner():
        for copy in halos:
            copy.wait_recv()
        product = across(data_v[:, pl.ds(snps - window, window)], halo_v[...])
        turned = pltpu.roll(product, half, 1)[:half]
        folded = jnp.where(half_col - half > half_row, product.T[half:], turned)
        late_s[...] = jnp.where(half_col < half, product[half:], folded).astype(jnp.bfloat16)
        peers(lambda dist: late_copy(dist).start())

    pl.when(has_after & even)(corner)

    for copy in small[2:]:
        copy.wait()
    place(mine * snps, starts_v, ends_v, member_v, weights_v, placed_out)

    sums_t[...] = collect(lambda dist: sums_copy(dist).wait_recv(), sums_r, sums_s[...])
    cols_v[...] = square_of(sums_t[...]).T
    pl.when(has_before)(lambda: tail_copies[0].start())

    def owner():
        total = collect(
            lambda dist: scatter_copy(dist).wait_recv(), main_r, main_s[me].astype(jnp.float32))
        row_of, col_of = iotas(per, window)
        row_of = row_of + me * per
        columns = cols_v[pl.ds(pl.multiple_of(me * per, per), per), :] * inverse
        for b in range(blocks):
            at = columns[:, b:b + 1]
            scored = total[2 * b] - at * sums_t[blocks:blocks + 1, :]
            main_p[2 * b] = pltpu.roll(scored, 1, 1).astype(main_p.dtype)
            mean_row = sums_t[b:b + 1, :] * inverse
            if b < blocks - 1:
                mean_row = jnp.where(col_of >= row_of, mean_row, sums_t[b + 1:b + 2, :] * inverse)
            value = total[2 * b + 1] * inverse - at * mean_row
            value = jnp.where(col_of == row_of, value, 2.0 * value)
            main_p[2 * b + 1] = value.astype(main_p.dtype)
        peers(lambda dist: gather_copy(dist, me).start())
        pl.when(has_before & even)(lambda: peers(lambda dist: direct_copy(dist, me).start(), 0))
        main_g[me] = main_p[...]
    guarded(me, owner)

    pl.when(has_after & odd)(corner)

    peers(lambda dist: guarded(
        behind(dist), lambda: gather_copy(dist, behind(dist)).wait_recv()))
    pl.when(has_before & odd)(lambda: tail_copies[1].start())
    near_out[...] = main_g[...]

    @pl.when(has_after)
    def _():
        folded = collect(
            lambda dist: late_copy(dist).wait_recv(), late_r, late_s[...].astype(jnp.float32))
        tail_copies[0].wait_recv()
        mirrored = jnp.concatenate([folded, folded], axis=0).T
        product = jnp.concatenate([
            pltpu.roll(folded, half, 1), jnp.where(half_col < half, folded, mirrored[half:])], axis=0)
        value = product * inverse - (cols_v[:, blocks - 1:blocks] * inverse) * (tail_sums[0:1, :] * inverse)
        corner_out[...] = jnp.where(col < row, 2.0 * value, 0.0).astype(corner_out.dtype)

        pl.when(even)(lambda: tail_copies[1].wait_recv())
        pl.when(odd)(lambda: peers(lambda dist: guarded(
            behind(dist), lambda: direct_copy(dist, behind(dist)).wait_recv()), 0))
        far_out[...] = tail_v[...]

    @pl.when(jnp.logical_not(has_after))
    def _():
        corner_out[...] = jnp.zeros_like(corner_out)
        far_out[...] = jnp.zeros_like(far_out)

    @pl.when(has_before)
    def _():
        for copy in halos:
            copy.wait_send()
        tail_copies[0].wait_send()
        pl.when(odd)(lambda: tail_copies[1].wait_send())
        pl.when(even)(lambda: guarded(
            me, lambda: peers(lambda dist: direct_copy(dist, me).wait_send(), 0)))
    peers(lambda dist: sums_copy(dist).wait_send())
    peers(lambda dist: guarded(ahead(dist), lambda: scatter_copy(dist).wait_send()))
    guarded(me, lambda: peers(lambda dist: gather_copy(dist, me).wait_send()))
    pl.when(has_after)(lambda: peers(lambda dist: late_copy(dist).wait_send()))


def place(offset, starts, ends, member, weights, placed):
    tissues, genes, window = weights.shape
    blocks = placed.shape[0]
    per_block = genes // blocks
    gene_row, gene_col = iotas(genes, genes)

    def upright(row_ref):
        spread = jnp.broadcast_to(row_ref[...].astype(jnp.float32), (genes, genes))
        picked = jnp.where(gene_row == gene_col, spread, 0.0)
        return jnp.sum(picked, axis=1, keepdims=True).astype(jnp.int32)

    first, past = upright(starts), upright(ends)
    gene, lane = iotas(genes, window)
    inside = lane < past - first
    within = first - offset - (gene // per_block) * window
    owned = member[...]
    for t in range(tissues):
        kept = inside & (owned[:, t:t + 1] != 0)
        weights[t] = jnp.where(kept, weights[t].astype(jnp.float32), 0.0).astype(weights.dtype)
    near = lane >= within
    source = (lane - within) & (window - 1)
    for t in range(tissues):
        turned = jnp.take_along_axis(weights[t].astype(jnp.float32), source, axis=1)
        head = jnp.where(near, turned, 0.0).astype(placed.dtype)
        rest = jnp.where(near, 0.0, turned).astype(placed.dtype)
        rows = pl.ds(t * per_block, per_block)
        for b in range(blocks):
            genes_of = slice(b * per_block, (b + 1) * per_block)
            placed[b, rows, pl.ds(0, window)] = head[genes_of]
            placed[b, rows, pl.ds(window, window)] = rest[genes_of]


def reduced_sums(genotype, phenotype, residual, sign_flips, starts, ends, member, weights):
    samples, snps = genotype.shape
    tissues, genes, window = weights.shape
    count, ring = lax.axis_size("samp"), lax.axis_size("snp")
    blocks = snps // window
    per = share_of(window, count)
    owners = window // per
    half, wide = jnp.bfloat16, jnp.float32
    dma = pltpu.SemaphoreType.DMA
    vmem = pl.BlockSpec(memory_space=pltpu.VMEM)
    hbm = pl.BlockSpec(memory_space=pltpu.HBM)
    operands = (
        genotype, phenotype.reshape(-1, window), residual.reshape(-1, window), sign_flips,
        starts.reshape(1, genes), ends.reshape(1, genes), member, weights,
    )
    return pl.pallas_call(
        functools.partial(sums_kernel, count, ring, window),
        out_shape=(
            jax.ShapeDtypeStruct((owners, 2 * blocks, per, window), half),
            jax.ShapeDtypeStruct((owners, 2, per, window), half),
            jax.ShapeDtypeStruct((window, window), half),
            jax.ShapeDtypeStruct((blocks, tissues * genes // blocks, 2 * window), half),
        ),
        in_specs=[hbm] * 8,
        out_specs=(vmem,) * 4,
        scratch_shapes=[pltpu.VMEM(x.shape, x.dtype) for x in operands[1:3] + operands[4:]] + [
            pltpu.VMEM((samples, snps + window), half),
            pltpu.VMEM(sign_flips.shape, jnp.int32),
            pltpu.VMEM((samples, window), half),
            pltpu.VMEM((owners, 2 * blocks, per, window), half),
            pltpu.VMEM((count, 2 * blocks, per, window), half),
            pltpu.VMEM((2 * blocks, per, window), half),
            pltpu.VMEM((owners, 2 * blocks, per, window), half),
            pltpu.VMEM((window // 2, window), half),
            pltpu.VMEM((count, window // 2, window), half),
            pltpu.VMEM((owners, 2, per, window), half),
            pltpu.VMEM((8, window), wide),
            pltpu.VMEM((8, window), wide),
            pltpu.VMEM((count, 8, window), wide),
            pltpu.VMEM((8, window), wide),
            pltpu.VMEM((window, window), wide),
            dma((PARTS,)), dma((PARTS,)), dma((6,)), dma((PARTS,)), dma((PARTS,)),
            dma((count,)), dma((count,)), dma((count,)), dma((count,)),
            dma((count,)), dma((count,)), dma((count,)), dma((count,)),
            dma((count,)), dma((count,)), dma((2,)), dma((2,)),
        ],
        compiler_params=pltpu.CompilerParams(
            collective_id=0, has_side_effects=True, vmem_limit_bytes=VMEM_LIMIT),
        name="sums",
    )(*(pltpu.with_memory_space_constraint(x, pltpu.HBM) for x in operands))


def scores_kernel(sample_total, near, far, corner, placed, out_hbm, out, sem):
    tissues, genes, window = out.shape
    blocks = placed.shape[0]
    per_block = genes // blocks
    row, col = iotas(window, window)
    root = 1.0 / (sample_total ** 0.5)

    def piece(b, kind):
        ref, at = (near, 2 * b) if b < blocks else (far, 0)
        return ref[:, at + kind].reshape(window, window)

    def masked(keep, value):
        return jnp.where(keep, value.astype(jnp.float32), 0.0).astype(jnp.bfloat16)

    labelled = [piece(b, 0) for b in range(blocks + 1)]
    banded = [piece(b, 1) for b in range(blocks + 1)]
    diagonal = [masked(col >= row, band) for band in banded]
    beside = [masked(col < row, band) for band in banded[:blocks - 1]] + [corner[...]]
    nothing = jnp.zeros((window, window), jnp.bfloat16)
    pairs, bands = [], []
    for b in range(blocks):
        pairs.append(jnp.concatenate([labelled[b], labelled[b + 1]], axis=0))
        bands.append(jnp.concatenate([
            jnp.concatenate([diagonal[b], beside[b]], axis=1),
            jnp.concatenate([nothing, diagonal[b + 1]], axis=1),
        ], axis=0))

    copies = []
    step = next(n for n in range(min(7, tissues), 0, -1) if tissues % n == 0)
    for t in range(0, tissues, step):
        for b in range(blocks):
            half = placed[b, pl.ds(t * per_block, step * per_block), :]
            top = jnp.dot(half, pairs[b], preferred_element_type=jnp.float32)
            square = jnp.dot(half, bands[b], preferred_element_type=jnp.float32)
            variance = jnp.sum(square * half.astype(jnp.float32), axis=1, keepdims=True)
            scale = lax.rsqrt(jnp.maximum(variance, 0.0) + 1e-06) * root
            out[pl.ds(t, step), pl.ds(b * per_block, per_block), :] = (top * scale).reshape(step, per_block, window)
        part = pl.ds(t, step)
        copies.append(pltpu.make_async_copy(out.at[part], out_hbm.at[part], sem.at[t // step]))
        copies[-1].start()
    for copy in copies:
        copy.wait()


def on_device(genotype, phenotype, residual, sign_flips, weights, member, gene_start, gene_end):
    by_tissue = weights.transpose(1, 0, 2)
    near, far, corner, placed = reduced_sums(
        genotype, phenotype, residual, sign_flips, gene_start, gene_end, member, by_tissue)
    vmem = pl.BlockSpec(memory_space=pltpu.VMEM)
    scores = pl.pallas_call(
        functools.partial(scores_kernel, genotype.shape[0] * lax.axis_size("samp")),
        out_shape=jax.ShapeDtypeStruct(by_tissue.shape, jnp.float32),
        in_specs=[vmem] * 4,
        out_specs=pl.BlockSpec(memory_space=pltpu.HBM),
        scratch_shapes=[
            pltpu.VMEM(by_tissue.shape, jnp.float32),
            pltpu.SemaphoreType.DMA((by_tissue.shape[0],)),
        ],
        compiler_params=pltpu.CompilerParams(vmem_limit_bytes=VMEM_LIMIT),
        name="scores",
    )(near, far, corner, placed)
    return scores.transpose(1, 0, 2)


def solution(mesh):
    return jax.shard_map(
        on_device,
        mesh=mesh,
        in_specs=(
            P("samp", "snp"),
            P("samp"),
            P("samp"),
            P("samp", None),
            P("snp", None, None),
            P("snp", None),
            P("snp"),
            P("snp"),
        ),
        out_specs=P("snp", None, None),
        check_vma=False,
    )
```

```python
import functools

import jax
import jax.numpy as jnp
from jax import lax
from jax.experimental import pallas as pl
from jax.experimental.pallas import tpu as pltpu
from jax.sharding import PartitionSpec as P

MESH = pl.DeviceIdType.MESH
TILE = 16
PARTS = 4
VMEM_LIMIT = 24 * 1024 * 1024


def across(left, right):
    return lax.dot_general(left, right, (((0,), (0,)), ((), ())), preferred_element_type=jnp.float32)


def iotas(rows, cols):
    return (
        lax.broadcasted_iota(jnp.int32, (rows, cols), 0),
        lax.broadcasted_iota(jnp.int32, (rows, cols), 1),
    )


def share_of(rows, count):
    per = -(-rows // (count * TILE)) * TILE
    while rows % per:
        per += TILE
    return per


def square_of(rows):
    tiles, width = rows.shape
    return jnp.concatenate([rows, jnp.zeros((width - tiles, width), jnp.float32)], axis=0)


def sums_kernel(
    count, ring, window,
    geno, phen, resid, flips, starts, ends, member, weights,
    near_out, far_out, corner_out, placed_out,
    phen_v, resid_v, starts_v, ends_v, member_v, weights_v,
    data_v, flips_v, halo_v, back_v,
    main_s, main_r, main_p, main_g,
    late_s, late_r, back_s, back_r, fold_v, tail_v, tail_sums, sums_s, sums_r, sums_t, cols_v,
    load_sem, flip_sem, small_sem, halo_ss, halo_rs,
    ms_ss, ms_rs, mg_ss, mg_rs, lt_ss, lt_rs, bc_ss, bc_rs, td_ss, td_rs,
    sm_ss, sm_rs, tl_ss, tl_rs, bk_ss, bk_rs,
):
    me = lax.axis_index("samp")
    mine = lax.axis_index("snp")
    has_before = mine > 0
    has_after = mine < ring - 1
    odd = lax.rem(mine, 2) == 1
    even = lax.rem(mine, 2) == 0
    before = jnp.maximum(mine - 1, 0)
    after = jnp.minimum(mine + 1, ring - 1)
    samples = data_v.shape[0]
    owners, bands, per, _ = main_g.shape
    blocks = bands // 2
    snps = blocks * window
    part = samples // PARTS
    inverse = 1.0 / (samples * count)

    def peers(body, first=1):
        if count <= 16:
            for dist in range(first, count):
                body(dist)
        else:
            def step(dist, carry):
                body(dist)
                return carry
            lax.fori_loop(first, count, step, 0)

    def collect(wait, got, total):
        if count <= 16:
            for dist in range(1, count):
                wait(dist)
                total += got[dist].astype(jnp.float32)
            return total

        def step(dist, total):
            wait(dist)
            return total + got[dist].astype(jnp.float32)
        return lax.fori_loop(1, count, step, total)

    def ahead(dist):
        return lax.rem(me + dist, count)

    def behind(dist):
        return lax.rem(me + count - dist, count)

    barrier = pltpu.get_barrier_semaphore()

    def greet(dist, other):
        pl.semaphore_signal(barrier, inc=1, device_id=(ahead(dist), other), device_id_type=MESH)

    peers(lambda dist: greet(dist, mine))
    pl.when(has_before & even)(lambda: peers(lambda dist: greet(dist, before), 0))
    pl.when(has_before & odd)(lambda: greet(0, before))
    pl.when(has_after & odd)(lambda: peers(lambda dist: greet(dist, after), 0))
    pl.when(has_after & even)(lambda: greet(0, after))

    small = [
        pltpu.make_async_copy(src, dst, small_sem.at[i])
        for i, (src, dst) in enumerate((
            (resid, resid_v), (phen, phen_v), (starts, starts_v), (ends, ends_v),
            (member, member_v), (weights, weights_v),
        ))
    ]
    loads, flip_loads = [], []
    for copy in small[:2]:
        copy.start()
    for i in range(PARTS):
        rows = pl.ds(i * part, part)
        loads.append(pltpu.make_async_copy(
            geno.at[rows], data_v.at[rows, pl.ds(0, snps)], load_sem.at[i]))
        flip_loads.append(pltpu.make_async_copy(flips.at[rows], flips_v.at[rows], flip_sem.at[i]))
        flip_loads[i].start()
        loads[i].start()
    for copy in small[2:]:
        copy.start()

    for copy in small[:2]:
        copy.wait()
    phen_cols = square_of(phen_v[...]).T
    resid_cols = square_of(resid_v[...]).T
    lanes = phen_v.shape[1]
    for i in range(PARTS):
        flip_loads[i].wait()
        for t in range(i * part // lanes, (i + 1) * part // lanes):
            rows = pl.ds(t * lanes, lanes)
            signs = flips_v[rows, :].astype(jnp.float32)
            labels = jnp.concatenate([signs * resid_cols[:, t:t + 1], phen_cols[:, t:t + 1]], axis=1)
            data_v[rows, pl.ds(snps, window)] = labels.astype(jnp.bfloat16)

    from_before = jnp.where(has_before, jnp.where(even, count, 1), 0)
    from_after = jnp.where(has_after, jnp.where(even, 1, count), 0)
    pl.semaphore_wait(barrier, count - 1 + from_before + from_after)

    def remote(src, dst, ss, rs, device):
        return pltpu.make_async_remote_copy(
            src_ref=src, dst_ref=dst, send_sem=ss, recv_sem=rs,
            device_id=device, device_id_type=MESH)

    halos = []
    for i in range(PARTS):
        rows = pl.ds(i * part, part)
        halos.append(remote(
            geno.at[rows, pl.ds(0, window)], halo_v.at[rows],
            halo_ss.at[i], halo_rs.at[i], (me, before)))

    half_parts = PARTS // 2
    split = half_parts * part
    back = remote(
        geno.at[pl.ds(split, samples - split), pl.ds(snps - window, window)], back_v,
        bk_ss.at[0], bk_rs.at[0], (me, after))

    @pl.when(has_before)
    def _():
        for copy in halos[:half_parts]:
            copy.start()

    @pl.when(has_before & odd)
    def _():
        for copy in halos[half_parts:]:
            copy.start()

    pl.when(has_after & odd)(back.start)

    def guarded(index, body):
        if owners == count:
            body()
        else:
            pl.when(index < owners)(body)

    def scatter_copy(dist):
        return remote(
            main_s.at[ahead(dist)], main_r.at[dist], ms_ss.at[dist], ms_rs.at[dist], (ahead(dist), mine))

    def gather_copy(dist, slot):
        return remote(main_p, main_g.at[slot], mg_ss.at[dist], mg_rs.at[dist], (ahead(dist), mine))

    def direct_copy(dist, slot):
        return remote(
            main_p.at[pl.ds(0, 2)], tail_v.at[slot], td_ss.at[dist], td_rs.at[dist], (ahead(dist), before))

    def sums_copy(dist):
        return remote(sums_s, sums_r.at[dist], sm_ss.at[dist], sm_rs.at[dist], (ahead(dist), mine))

    def late_copy(dist):
        return remote(late_s, late_r.at[dist], lt_ss.at[dist], lt_rs.at[dist], (ahead(dist), mine))

    def back_copy(dist):
        return remote(back_s, back_r.at[dist], bc_ss.at[dist], bc_rs.at[dist], (ahead(dist), before))

    tail_copies = [
        remote(sums_t, tail_sums, tl_ss.at[0], tl_rs.at[0], (me, before)),
        remote(main_g.at[:, pl.ds(0, 2)], tail_v, tl_ss.at[1], tl_rs.at[1], (me, before)),
    ]

    for i in range(PARTS):
        loads[i].wait()
    data = data_v[...]
    left = jnp.concatenate([data[:, :snps], jnp.ones((samples, 8), jnp.bfloat16)], axis=1)
    products = across(left, data)
    row8, _ = iotas(8, window)
    sums = jnp.zeros((8, window), jnp.float32)
    for b in range(blocks + 1):
        sums = jnp.where(row8 == b, products[snps:, b * window:(b + 1) * window], sums)
    sums_s[...] = sums
    peers(lambda dist: sums_copy(dist).start())
    row, col = iotas(window, window)
    for b in range(blocks):
        low, mid, high = b * window, (b + 1) * window, (b + 2) * window
        beyond = products[low:mid, mid:high] if b < blocks - 1 else 0.0
        band = jnp.where(col >= row, products[low:mid, low:mid], beyond)
        main_s[:, 2 * b] = products[low:mid, snps:].astype(jnp.bfloat16).reshape(owners, per, window)
        main_s[:, 2 * b + 1] = band.astype(jnp.bfloat16).reshape(owners, per, window)
    peers(lambda dist: guarded(ahead(dist), lambda: scatter_copy(dist).start()))

    half = window // 2
    half_row, half_col = iotas(half, window)

    def fold(product):
        turned = pltpu.roll(product, half, 1)[:half]
        folded = jnp.where(half_col - half > half_row, product.T[half:], turned)
        return jnp.where(half_col < half, product[half:], folded).astype(jnp.bfloat16)

    def corner(count_of_parts):
        for copy in halos[:count_of_parts]:
            copy.wait_recv()
        rows = pl.ds(0, count_of_parts * part)
        late_s[...] = fold(across(data_v[rows, pl.ds(snps - window, window)], halo_v[rows, :]))
        peers(lambda dist: late_copy(dist).start())

    pl.when(has_after & even)(lambda: corner(PARTS))

    for copy in small[2:]:
        copy.wait()
    place(mine * snps, starts_v, ends_v, member_v, weights_v, placed_out)

    @pl.when(has_before & even)
    def _():
        back.wait_recv()
        back_s[...] = fold(across(back_v[...], data_v[pl.ds(split, samples - split), pl.ds(0, window)]))
        peers(lambda dist: back_copy(dist).start(), 0)

    sums_t[...] = collect(lambda dist: sums_copy(dist).wait_recv(), sums_r, sums_s[...])
    cols_v[...] = square_of(sums_t[...]).T
    pl.when(has_before)(lambda: tail_copies[0].start())

    def owner():
        total = collect(
            lambda dist: scatter_copy(dist).wait_recv(), main_r, main_s[me].astype(jnp.float32))
        row_of, col_of = iotas(per, window)
        row_of = row_of + me * per
        columns = cols_v[pl.ds(pl.multiple_of(me * per, per), per), :] * inverse
        for b in range(blocks):
            at = columns[:, b:b + 1]
            scored = total[2 * b] - at * sums_t[blocks:blocks + 1, :]
            main_p[2 * b] = pltpu.roll(scored, 1, 1).astype(main_p.dtype)
            mean_row = sums_t[b:b + 1, :] * inverse
            if b < blocks - 1:
                mean_row = jnp.where(col_of >= row_of, mean_row, sums_t[b + 1:b + 2, :] * inverse)
            value = total[2 * b + 1] * inverse - at * mean_row
            value = jnp.where(col_of == row_of, value, 2.0 * value)
            main_p[2 * b + 1] = value.astype(main_p.dtype)
        peers(lambda dist: gather_copy(dist, me).start())
        pl.when(has_before & even)(lambda: peers(lambda dist: direct_copy(dist, me).start(), 0))
        main_g[me] = main_p[...]
    guarded(me, owner)

    pl.when(has_after & odd)(lambda: corner(half_parts))

    peers(lambda dist: guarded(
        behind(dist), lambda: gather_copy(dist, behind(dist)).wait_recv()))
    pl.when(has_before & odd)(lambda: tail_copies[1].start())
    near_out[...] = main_g[...]

    @pl.when(has_after)
    def _():
        fold_v[...] = collect(
            lambda dist: late_copy(dist).wait_recv(), late_r, late_s[...].astype(jnp.float32))

        @pl.when(odd)
        def _():
            back_copy(0).wait_recv()
            fold_v[...] += collect(
                lambda dist: back_copy(dist).wait_recv(), back_r, back_r[0].astype(jnp.float32))

        folded = fold_v[...]
        tail_copies[0].wait_recv()
        mirrored = jnp.concatenate([folded, folded], axis=0).T
        product = jnp.concatenate([
            pltpu.roll(folded, half, 1), jnp.where(half_col < half, folded, mirrored[half:])], axis=0)
        value = product * inverse - (cols_v[:, blocks - 1:blocks] * inverse) * (tail_sums[0:1, :] * inverse)
        corner_out[...] = jnp.where(col < row, 2.0 * value, 0.0).astype(corner_out.dtype)

        pl.when(even)(lambda: tail_copies[1].wait_recv())
        pl.when(odd)(lambda: peers(lambda dist: guarded(
            behind(dist), lambda: direct_copy(dist, behind(dist)).wait_recv()), 0))
        far_out[...] = tail_v[...]

    @pl.when(jnp.logical_not(has_after))
    def _():
        corner_out[...] = jnp.zeros_like(corner_out)
        far_out[...] = jnp.zeros_like(far_out)

    @pl.when(has_before)
    def _():
        for copy in halos[:half_parts]:
            copy.wait_send()
        tail_copies[0].wait_send()

        @pl.when(odd)
        def _():
            for copy in halos[half_parts:]:
                copy.wait_send()
            tail_copies[1].wait_send()

        pl.when(even)(lambda: peers(lambda dist: back_copy(dist).wait_send(), 0))
        pl.when(even)(lambda: guarded(
            me, lambda: peers(lambda dist: direct_copy(dist, me).wait_send(), 0)))
    pl.when(has_after & odd)(back.wait_send)
    peers(lambda dist: sums_copy(dist).wait_send())
    peers(lambda dist: guarded(ahead(dist), lambda: scatter_copy(dist).wait_send()))
    guarded(me, lambda: peers(lambda dist: gather_copy(dist, me).wait_send()))
    pl.when(has_after)(lambda: peers(lambda dist: late_copy(dist).wait_send()))


def place(offset, starts, ends, member, weights, placed):
    tissues, genes, window = weights.shape
    blocks = placed.shape[0]
    per_block = genes // blocks
    gene_row, gene_col = iotas(genes, genes)

    def upright(row_ref):
        spread = jnp.broadcast_to(row_ref[...].astype(jnp.float32), (genes, genes))
        picked = jnp.where(gene_row == gene_col, spread, 0.0)
        return jnp.sum(picked, axis=1, keepdims=True).astype(jnp.int32)

    first, past = upright(starts), upright(ends)
    gene, lane = iotas(genes, window)
    inside = lane < past - first
    within = first - offset - (gene // per_block) * window
    owned = member[...]
    for t in range(tissues):
        kept = inside & (owned[:, t:t + 1] != 0)
        weights[t] = jnp.where(kept, weights[t].astype(jnp.float32), 0.0).astype(weights.dtype)
    near = lane >= within
    source = (lane - within) & (window - 1)
    for t in range(tissues):
        turned = jnp.take_along_axis(weights[t].astype(jnp.float32), source, axis=1)
        head = jnp.where(near, turned, 0.0).astype(placed.dtype)
        rest = jnp.where(near, 0.0, turned).astype(placed.dtype)
        rows = pl.ds(t * per_block, per_block)
        for b in range(blocks):
            genes_of = slice(b * per_block, (b + 1) * per_block)
            placed[b, rows, pl.ds(0, window)] = head[genes_of]
            placed[b, rows, pl.ds(window, window)] = rest[genes_of]


def reduced_sums(genotype, phenotype, residual, sign_flips, starts, ends, member, weights):
    samples, snps = genotype.shape
    tissues, genes, window = weights.shape
    count, ring = lax.axis_size("samp"), lax.axis_size("snp")
    blocks = snps // window
    per = share_of(window, count)
    owners = window // per
    half, wide = jnp.bfloat16, jnp.float32
    dma = pltpu.SemaphoreType.DMA
    vmem = pl.BlockSpec(memory_space=pltpu.VMEM)
    hbm = pl.BlockSpec(memory_space=pltpu.HBM)
    operands = (
        genotype, phenotype.reshape(-1, window), residual.reshape(-1, window), sign_flips,
        starts.reshape(1, genes), ends.reshape(1, genes), member, weights,
    )
    return pl.pallas_call(
        functools.partial(sums_kernel, count, ring, window),
        out_shape=(
            jax.ShapeDtypeStruct((owners, 2 * blocks, per, window), half),
            jax.ShapeDtypeStruct((owners, 2, per, window), half),
            jax.ShapeDtypeStruct((window, window), half),
            jax.ShapeDtypeStruct((blocks, tissues * genes // blocks, 2 * window), half),
        ),
        in_specs=[hbm] * 8,
        out_specs=(vmem,) * 4,
        scratch_shapes=[pltpu.VMEM(x.shape, x.dtype) for x in operands[1:3] + operands[4:]] + [
            pltpu.VMEM((samples, snps + window), half),
            pltpu.VMEM(sign_flips.shape, jnp.int32),
            pltpu.VMEM((samples, window), half),
            pltpu.VMEM((samples - samples // PARTS * (PARTS // 2), window), half),
            pltpu.VMEM((owners, 2 * blocks, per, window), half),
            pltpu.VMEM((count, 2 * blocks, per, window), half),
            pltpu.VMEM((2 * blocks, per, window), half),
            pltpu.VMEM((owners, 2 * blocks, per, window), half),
            pltpu.VMEM((window // 2, window), half),
            pltpu.VMEM((count, window // 2, window), half),
            pltpu.VMEM((window // 2, window), half),
            pltpu.VMEM((count, window // 2, window), half),
            pltpu.VMEM((window // 2, window), wide),
            pltpu.VMEM((owners, 2, per, window), half),
            pltpu.VMEM((8, window), wide),
            pltpu.VMEM((8, window), wide),
            pltpu.VMEM((count, 8, window), wide),
            pltpu.VMEM((8, window), wide),
            pltpu.VMEM((window, window), wide),
            dma((PARTS,)), dma((PARTS,)), dma((6,)), dma((PARTS,)), dma((PARTS,)),
            dma((count,)), dma((count,)), dma((count,)), dma((count,)),
            dma((count,)), dma((count,)), dma((count,)), dma((count,)),
            dma((count,)), dma((count,)), dma((count,)), dma((count,)),
            dma((2,)), dma((2,)), dma((1,)), dma((1,)),
        ],
        compiler_params=pltpu.CompilerParams(
            collective_id=0, has_side_effects=True, vmem_limit_bytes=VMEM_LIMIT),
        name="sums",
    )(*(pltpu.with_memory_space_constraint(x, pltpu.HBM) for x in operands))


def scores_kernel(sample_total, near, far, corner, placed, out_hbm, out, sem):
    tissues, genes, window = out.shape
    blocks = placed.shape[0]
    per_block = genes // blocks
    row, col = iotas(window, window)
    root = 1.0 / (sample_total ** 0.5)

    def piece(b, kind):
        ref, at = (near, 2 * b) if b < blocks else (far, 0)
        return ref[:, at + kind].reshape(window, window)

    def masked(keep, value):
        return jnp.where(keep, value.astype(jnp.float32), 0.0).astype(jnp.bfloat16)

    labelled = [piece(b, 0) for b in range(blocks + 1)]
    banded = [piece(b, 1) for b in range(blocks + 1)]
    diagonal = [masked(col >= row, band) for band in banded]
    beside = [masked(col < row, band) for band in banded[:blocks - 1]] + [corner[...]]
    nothing = jnp.zeros((window, window), jnp.bfloat16)
    pairs, bands = [], []
    for b in range(blocks):
        pairs.append(jnp.concatenate([labelled[b], labelled[b + 1]], axis=0))
        bands.append(jnp.concatenate([
            jnp.concatenate([diagonal[b], beside[b]], axis=1),
            jnp.concatenate([nothing, diagonal[b + 1]], axis=1),
        ], axis=0))

    copies = []
    step = next(n for n in range(min(7, tissues), 0, -1) if tissues % n == 0)
    for t in range(0, tissues, step):
        for b in range(blocks):
            half = placed[b, pl.ds(t * per_block, step * per_block), :]
            top = jnp.dot(half, pairs[b], preferred_element_type=jnp.float32)
            square = jnp.dot(half, bands[b], preferred_element_type=jnp.float32)
            variance = jnp.sum(square * half.astype(jnp.float32), axis=1, keepdims=True)
            scale = lax.rsqrt(jnp.maximum(variance, 0.0) + 1e-06) * root
            out[pl.ds(t, step), pl.ds(b * per_block, per_block), :] = (top * scale).reshape(step, per_block, window)
        part = pl.ds(t, step)
        copies.append(pltpu.make_async_copy(out.at[part], out_hbm.at[part], sem.at[t // step]))
        copies[-1].start()
    for copy in copies:
        copy.wait()


def on_device(genotype, phenotype, residual, sign_flips, weights, member, gene_start, gene_end):
    by_tissue = weights.transpose(1, 0, 2)
    near, far, corner, placed = reduced_sums(
        genotype, phenotype, residual, sign_flips, gene_start, gene_end, member, by_tissue)
    vmem = pl.BlockSpec(memory_space=pltpu.VMEM)
    scores = pl.pallas_call(
        functools.partial(scores_kernel, genotype.shape[0] * lax.axis_size("samp")),
        out_shape=jax.ShapeDtypeStruct(by_tissue.shape, jnp.float32),
        in_specs=[vmem] * 4,
        out_specs=pl.BlockSpec(memory_space=pltpu.HBM),
        scratch_shapes=[
            pltpu.VMEM(by_tissue.shape, jnp.float32),
            pltpu.SemaphoreType.DMA((by_tissue.shape[0],)),
        ],
        compiler_params=pltpu.CompilerParams(vmem_limit_bytes=VMEM_LIMIT),
        name="scores",
    )(near, far, corner, placed)
    return scores.transpose(1, 0, 2)


def solution(mesh):
    return jax.shard_map(
        on_device,
        mesh=mesh,
        in_specs=(
            P("samp", "snp"),
            P("samp"),
            P("samp"),
            P("samp", None),
            P("snp", None, None),
            P("snp", None),
            P("snp"),
            P("snp"),
        ),
        out_specs=P("snp", None, None),
        check_vma=False,
    )
```

```python
import functools

import jax
import jax.numpy as jnp
from jax import lax
from jax.experimental import pallas as pl
from jax.experimental.pallas import tpu as pltpu
from jax.sharding import PartitionSpec as P

MESH = pl.DeviceIdType.MESH
TILE = 16
PARTS = 4
HALVES = 2
VMEM_LIMIT = 24 * 1024 * 1024


def across(left, right):
    return lax.dot_general(left, right, (((0,), (0,)), ((), ())), preferred_element_type=jnp.float32)


def iotas(rows, cols):
    return (
        lax.broadcasted_iota(jnp.int32, (rows, cols), 0),
        lax.broadcasted_iota(jnp.int32, (rows, cols), 1),
    )


def share_of(rows, count):
    per = -(-rows // (count * TILE)) * TILE
    while rows % per:
        per += TILE
    return per


def square_of(rows):
    tiles, width = rows.shape
    return jnp.concatenate([rows, jnp.zeros((width - tiles, width), jnp.float32)], axis=0)


def sums_kernel(
    count, ring, window,
    geno, phen, resid, flips, starts, ends, member, weights,
    near_out, far_out, corner_out, placed_out,
    phen_v, resid_v, starts_v, ends_v, member_v, weights_v,
    data_v, flips_v, halo_v, back_v,
    main_s, main_r, main_p, main_g,
    late_s, late_r, back_s, back_r, fold_v, tail_v,
    sums_s, sums_r, sums_t, cols_v, near_v, next_v,
    load_sem, flip_sem, small_sem, halo_ss, halo_rs,
    ms_ss, ms_rs, mg_ss, mg_rs, lt_ss, lt_rs, bc_ss, bc_rs, td_ss, td_rs,
    sm_ss, sm_rs, st_ss, st_rs, bk_ss, bk_rs,
):
    me = lax.axis_index("samp")
    mine = lax.axis_index("snp")
    parity = lax.rem(mine, 2)
    odd, even = parity == 1, parity == 0
    has_before, has_after = mine > 0, mine < ring - 1
    before = jnp.maximum(mine - 1, 0)
    after = jnp.minimum(mine + 1, ring - 1)
    beyond = jnp.minimum(mine + 2, ring - 1)
    keeper = mine + 1 - parity
    partner = mine + 1 - 2 * parity
    slot = 1 - parity
    samples = data_v.shape[0]
    owners, bands, per, _ = main_g.shape
    blocks = bands // 2
    snps = blocks * window
    part = samples // PARTS
    split = samples // HALVES
    inverse = 1.0 / (samples * count)

    def peers(body, first=1):
        if count <= 16:
            for dist in range(first, count):
                body(dist)
        else:
            def step(dist, carry):
                body(dist)
                return carry
            lax.fori_loop(first, count, step, 0)

    def group(body):
        pl.when(even)(lambda: body(0))
        peers(body)

    def collect(wait, got, total, first=1):
        if count <= 16:
            for dist in range(first, count):
                wait(dist)
                total += got[dist].astype(jnp.float32)
            return total

        def step(dist, total):
            wait(dist)
            return total + got[dist].astype(jnp.float32)
        return lax.fori_loop(first, count, step, total)

    def ahead(dist):
        return lax.rem(me + dist, count)

    def behind(dist):
        return lax.rem(me + count - dist, count)

    small = [
        pltpu.make_async_copy(src, dst, small_sem.at[i])
        for i, (src, dst) in enumerate((
            (resid, resid_v), (phen, phen_v), (starts, starts_v), (ends, ends_v),
            (member, member_v), (weights, weights_v),
        ))
    ]
    flip_loads = []
    for copy in small[:2]:
        copy.start()
    for i in range(PARTS):
        rows = pl.ds(i * part, part)
        flip_loads.append(pltpu.make_async_copy(flips.at[rows], flips_v.at[rows], flip_sem.at[i]))
        flip_loads[i].start()
    load = pltpu.make_async_copy(geno, data_v.at[:, pl.ds(0, snps)], load_sem.at[0])
    load.start()

    barrier = pltpu.get_barrier_semaphore()

    def greet(dist, other):
        pl.semaphore_signal(barrier, inc=1, device_id=(ahead(dist), other), device_id_type=MESH)

    peers(lambda dist: greet(dist, mine))
    peers(lambda dist: greet(dist, partner), 0)
    pl.when(has_before & even)(lambda: greet(0, before))

    @pl.when(has_after & odd)
    def _():
        peers(lambda dist: greet(dist, after), 0)
        peers(lambda dist: greet(dist, beyond), 0)

    for copy in small[2:]:
        copy.start()

    for copy in small[:2]:
        copy.wait()
    phen_cols = square_of(phen_v[...]).T
    resid_cols = square_of(resid_v[...]).T
    lanes = phen_v.shape[1]
    for i in range(PARTS):
        flip_loads[i].wait()
        for t in range(i * part // lanes, (i + 1) * part // lanes):
            rows = pl.ds(t * lanes, lanes)
            signs = flips_v[rows, :].astype(jnp.float32)
            labels = jnp.concatenate([signs * resid_cols[:, t:t + 1], phen_cols[:, t:t + 1]], axis=1)
            data_v[rows, pl.ds(snps, window)] = labels.astype(jnp.bfloat16)

    load.wait()
    data = data_v[...]
    left = jnp.concatenate([data[:, :snps], jnp.ones((samples, 8), jnp.bfloat16)], axis=1)
    products = across(left, data)
    row8, _ = iotas(8, window)
    sums = jnp.zeros((8, window), jnp.float32)
    for b in range(blocks + 1):
        sums = jnp.where(row8 == b, products[snps:, b * window:(b + 1) * window], sums)
    sums_s[...] = sums
    row, col = iotas(window, window)
    for b in range(blocks):
        low, mid, high = b * window, (b + 1) * window, (b + 2) * window
        other = products[low:mid, mid:high] if b < blocks - 1 else 0.0
        band = jnp.where(col >= row, products[low:mid, low:mid], other)
        main_s[:, 2 * b] = products[low:mid, snps:].astype(jnp.bfloat16).reshape(owners, per, window)
        main_s[:, 2 * b + 1] = band.astype(jnp.bfloat16).reshape(owners, per, window)

    def remote(src, dst, ss, rs, device):
        return pltpu.make_async_remote_copy(
            src_ref=src, dst_ref=dst, send_sem=ss, recv_sem=rs,
            device_id=device, device_id_type=MESH)

    halos = []
    for i in range(HALVES):
        rows = pl.ds(i * split, split)
        halos.append(remote(
            geno.at[rows, pl.ds(0, window)], halo_v.at[rows],
            halo_ss.at[i], halo_rs.at[i], (me, before)))
    back = remote(
        geno.at[pl.ds(split, samples - split), pl.ds(snps - window, window)], back_v,
        bk_ss.at[0], bk_rs.at[0], (me, after))

    def guarded(index, body):
        if owners == count:
            body()
        else:
            pl.when(index < owners)(body)

    def sums_copy(dist):
        return remote(
            sums_s, sums_r.at[slot, dist], sm_ss.at[dist], sm_rs.at[slot, dist], (ahead(dist), keeper))

    def scatter_copy(dist):
        return remote(
            main_s.at[ahead(dist)], main_r.at[slot, dist],
            ms_ss.at[dist], ms_rs.at[slot, dist], (ahead(dist), keeper))

    def gather_copy(s, dist, place):
        return remote(
            main_p.at[s], main_g.at[place], mg_ss.at[s, dist], mg_rs.at[dist],
            (ahead(dist), jnp.maximum(mine - s, 0)))

    def direct_copy(s, dist, place):
        return remote(
            main_p.at[s, pl.ds(0, 2)], tail_v.at[place], td_ss.at[s, dist], td_rs.at[dist],
            (ahead(dist), jnp.maximum(mine - 1 - s, 0)))

    def late_copy(dist):
        return remote(late_s, late_r.at[dist], lt_ss.at[dist], lt_rs.at[dist], (ahead(dist), mine))

    def back_copy(dist):
        return remote(back_s, back_r.at[dist], bc_ss.at[dist], bc_rs.at[dist], (ahead(dist), before))

    stats = [
        remote(sums_t.at[1], near_v, st_ss.at[0], st_rs.at[0], (me, before)),
        remote(sums_t.at[0], next_v, st_ss.at[1], st_rs.at[1], (me, before)),
        remote(sums_t.at[1], next_v, st_ss.at[2], st_rs.at[2], (me, jnp.maximum(mine - 2, 0))),
    ]
    further = odd & (mine > 1)

    pl.semaphore_wait(
        barrier,
        2 * count - 1 + jnp.where(has_before & even, count, 0)
        + jnp.where(has_after & odd, 1, 0) + jnp.where(further, count, 0))
    pl.when(has_before)(halos[0].start)

    @pl.when(has_before & odd)
    def _():
        for copy in halos[1:]:
            copy.start()

    pl.when(has_after & odd)(back.start)
    group(lambda dist: sums_copy(dist).start())
    group(lambda dist: guarded(ahead(dist), lambda: scatter_copy(dist).start()))

    half = window // 2
    half_row, half_col = iotas(half, window)

    def fold(product):
        turned = pltpu.roll(product, half, 1)[:half]
        folded = jnp.where(half_col - half > half_row, product.T[half:], turned)
        return jnp.where(half_col < half, product[half:], folded).astype(jnp.bfloat16)

    def corner(arrived):
        for copy in halos[:arrived]:
            copy.wait_recv()
        rows = pl.ds(0, arrived * split)
        late_s[...] = fold(across(data_v[rows, pl.ds(snps - window, window)], halo_v[rows, :]))
        peers(lambda dist: late_copy(dist).start())

    pl.when(even)(lambda: corner(HALVES))

    for copy in small[2:]:
        copy.wait()
    place(mine * snps, starts_v, ends_v, member_v, weights_v, placed_out)

    @pl.when(has_before & even)
    def _():
        back.wait_recv()
        back_s[...] = fold(across(back_v[...], data_v[pl.ds(split, samples - split), pl.ds(0, window)]))
        peers(lambda dist: back_copy(dist).start(), 0)

    def settle(s):
        sums_t[s] = collect(
            lambda dist: remote(
                sums_s, sums_r.at[s, dist], sm_ss.at[dist], sm_rs.at[s, dist],
                (ahead(dist), partner)).wait_recv(),
            sums_r.at[s], sums_s[...] if s == 0 else jnp.zeros_like(sums_s), 1 - s)
        cols_v[s] = square_of(sums_t[s]).T

    def own(s):
        def body():
            total = collect(
                lambda dist: remote(
                    main_s.at[0], main_r.at[s, dist], ms_ss.at[dist], ms_rs.at[s, dist],
                    (ahead(dist), partner)).wait_recv(),
                main_r.at[s],
                main_s[me].astype(jnp.float32) if s == 0 else jnp.zeros(main_p.shape[1:], jnp.float32), 1 - s)
            row_of, col_of = iotas(per, window)
            row_of = row_of + me * per
            columns = cols_v[s, pl.ds(pl.multiple_of(me * per, per), per), :] * inverse
            for b in range(blocks):
                at = columns[:, b:b + 1]
                scored = total[2 * b] - at * sums_t[s, blocks:blocks + 1, :]
                main_p[s, 2 * b] = pltpu.roll(scored, 1, 1).astype(main_p.dtype)
                mean_row = sums_t[s, b:b + 1, :] * inverse
                if b < blocks - 1:
                    mean_row = jnp.where(col_of >= row_of, mean_row, sums_t[s, b + 1:b + 2, :] * inverse)
                value = total[2 * b + 1] * inverse - at * mean_row
                value = jnp.where(col_of == row_of, value, 2.0 * value)
                main_p[s, 2 * b + 1] = value.astype(main_p.dtype)
            peers(lambda dist: gather_copy(s, dist, me).start(), 1 - s)
            if s == 0:
                peers(lambda dist: direct_copy(s, dist, me).start(), 0)
                main_g[me] = main_p[s]
            else:
                pl.when(further)(lambda: peers(lambda dist: direct_copy(s, dist, me).start(), 0))
        guarded(me, body)

    @pl.when(odd)
    def _():
        for s in range(2):
            settle(s)
        stats[0].start()
        stats[1].start()
        pl.when(further)(stats[2].start)
        for s in range(2):
            own(s)

    pl.when(has_after & odd)(lambda: corner(1))

    @pl.when(has_after)
    def _():
        @pl.when(even)
        def _():
            stats[0].wait_recv()
            stats[1].wait_recv()

        @pl.when(odd)
        def _():
            near_v[...] = sums_t[0]
            stats[2].wait_recv()

        fold_v[...] = collect(
            lambda dist: late_copy(dist).wait_recv(), late_r, late_s[...].astype(jnp.float32))

        @pl.when(odd)
        def _():
            fold_v[...] = collect(lambda dist: back_copy(dist).wait_recv(), back_r, fold_v[...], 0)

        folded = fold_v[...]
        mirrored = jnp.concatenate([folded, folded], axis=0).T
        product = jnp.concatenate([
            pltpu.roll(folded, half, 1), jnp.where(half_col < half, folded, mirrored[half:])], axis=0)
        mean_col = square_of(near_v[...]).T[:, blocks - 1:blocks] * inverse
        value = product * inverse - mean_col * (next_v[0:1, :] * inverse)
        corner_out[...] = jnp.where(col < row, 2.0 * value, 0.0).astype(corner_out.dtype)

    group(lambda dist: guarded(
        behind(dist), lambda: gather_copy(0, dist, behind(dist)).wait_recv()))
    near_out[...] = main_g[...]

    @pl.when(has_after)
    def _():
        peers(lambda dist: guarded(
            behind(dist), lambda: direct_copy(0, dist, behind(dist)).wait_recv()), 0)
        far_out[...] = tail_v[...]

    @pl.when(jnp.logical_not(has_after))
    def _():
        corner_out[...] = jnp.zeros_like(corner_out)
        far_out[...] = jnp.zeros_like(far_out)

    pl.when(has_before)(halos[0].wait_send)
    pl.when(has_before & even)(lambda: peers(lambda dist: back_copy(dist).wait_send(), 0))
    pl.when(has_after & odd)(back.wait_send)
    pl.when(has_after)(lambda: peers(lambda dist: late_copy(dist).wait_send()))
    group(lambda dist: sums_copy(dist).wait_send())
    group(lambda dist: guarded(ahead(dist), lambda: scatter_copy(dist).wait_send()))

    @pl.when(odd)
    def _():
        for copy in halos[1:]:
            copy.wait_send()
        stats[0].wait_send()
        stats[1].wait_send()
        pl.when(further)(stats[2].wait_send)

        def sent():
            for s in range(2):
                peers(lambda dist: gather_copy(s, dist, me).wait_send(), 1 - s)
            peers(lambda dist: direct_copy(0, dist, me).wait_send(), 0)
            pl.when(further)(lambda: peers(lambda dist: direct_copy(1, dist, me).wait_send(), 0))
        guarded(me, sent)


def place(offset, starts, ends, member, weights, placed):
    tissues, genes, window = weights.shape
    blocks = placed.shape[0]
    per_block = genes // blocks
    gene_row, gene_col = iotas(genes, genes)

    def upright(row_ref):
        spread = jnp.broadcast_to(row_ref[...].astype(jnp.float32), (genes, genes))
        picked = jnp.where(gene_row == gene_col, spread, 0.0)
        return jnp.sum(picked, axis=1, keepdims=True).astype(jnp.int32)

    first, past = upright(starts), upright(ends)
    gene, lane = iotas(genes, window)
    inside = lane < past - first
    within = first - offset - (gene // per_block) * window
    owned = member[...]
    for t in range(tissues):
        kept = inside & (owned[:, t:t + 1] != 0)
        weights[t] = jnp.where(kept, weights[t].astype(jnp.float32), 0.0).astype(weights.dtype)
    near = lane >= within
    source = (lane - within) & (window - 1)
    for t in range(tissues):
        turned = jnp.take_along_axis(weights[t].astype(jnp.float32), source, axis=1)
        head = jnp.where(near, turned, 0.0).astype(placed.dtype)
        rest = jnp.where(near, 0.0, turned).astype(placed.dtype)
        rows = pl.ds(t * per_block, per_block)
        for b in range(blocks):
            genes_of = slice(b * per_block, (b + 1) * per_block)
            placed[b, rows, pl.ds(0, window)] = head[genes_of]
            placed[b, rows, pl.ds(window, window)] = rest[genes_of]


def reduced_sums(genotype, phenotype, residual, sign_flips, starts, ends, member, weights):
    samples, snps = genotype.shape
    tissues, genes, window = weights.shape
    count, ring = lax.axis_size("samp"), lax.axis_size("snp")
    blocks = snps // window
    per = share_of(window, count)
    owners = window // per
    half, wide = jnp.bfloat16, jnp.float32
    dma = pltpu.SemaphoreType.DMA
    vmem = pl.BlockSpec(memory_space=pltpu.VMEM)
    hbm = pl.BlockSpec(memory_space=pltpu.HBM)
    operands = (
        genotype, phenotype.reshape(-1, window), residual.reshape(-1, window), sign_flips,
        starts.reshape(1, genes), ends.reshape(1, genes), member, weights,
    )
    return pl.pallas_call(
        functools.partial(sums_kernel, count, ring, window),
        out_shape=(
            jax.ShapeDtypeStruct((owners, 2 * blocks, per, window), half),
            jax.ShapeDtypeStruct((owners, 2, per, window), half),
            jax.ShapeDtypeStruct((window, window), half),
            jax.ShapeDtypeStruct((blocks, tissues * genes // blocks, 2 * window), half),
        ),
        in_specs=[hbm] * 8,
        out_specs=(vmem,) * 4,
        scratch_shapes=[pltpu.VMEM(x.shape, x.dtype) for x in operands[1:3] + operands[4:]] + [
            pltpu.VMEM((samples, snps + window), half),
            pltpu.VMEM(sign_flips.shape, jnp.int32),
            pltpu.VMEM((samples, window), half),
            pltpu.VMEM((samples - samples // HALVES, window), half),
            pltpu.VMEM((owners, 2 * blocks, per, window), half),
            pltpu.VMEM((2, count, 2 * blocks, per, window), half),
            pltpu.VMEM((2, 2 * blocks, per, window), half),
            pltpu.VMEM((owners, 2 * blocks, per, window), half),
            pltpu.VMEM((window // 2, window), half),
            pltpu.VMEM((count, window // 2, window), half),
            pltpu.VMEM((window // 2, window), half),
            pltpu.VMEM((count, window // 2, window), half),
            pltpu.VMEM((window // 2, window), wide),
            pltpu.VMEM((owners, 2, per, window), half),
            pltpu.VMEM((8, window), wide),
            pltpu.VMEM((2, count, 8, window), wide),
            pltpu.VMEM((2, 8, window), wide),
            pltpu.VMEM((2, window, window), wide),
            pltpu.VMEM((8, window), wide),
            pltpu.VMEM((8, window), wide),
            dma((1,)), dma((PARTS,)), dma((6,)), dma((HALVES,)), dma((HALVES,)),
            dma((count,)), dma((2, count)), dma((2, count)), dma((count,)),
            dma((count,)), dma((count,)), dma((count,)), dma((count,)), dma((2, count)), dma((count,)),
            dma((count,)), dma((2, count)), dma((3,)), dma((3,)), dma((1,)), dma((1,)),
        ],
        compiler_params=pltpu.CompilerParams(
            collective_id=0, has_side_effects=True, vmem_limit_bytes=VMEM_LIMIT),
        name="sums",
    )(*(pltpu.with_memory_space_constraint(x, pltpu.HBM) for x in operands))


def scores_kernel(sample_total, near, far, corner, placed, out_hbm, out, sem):
    tissues, genes, window = out.shape
    blocks = placed.shape[0]
    per_block = genes // blocks
    row, col = iotas(window, window)
    root = 1.0 / (sample_total ** 0.5)

    def piece(b, kind):
        ref, at = (near, 2 * b) if b < blocks else (far, 0)
        return ref[:, at + kind].reshape(window, window)

    def masked(keep, value):
        return jnp.where(keep, value.astype(jnp.float32), 0.0).astype(jnp.bfloat16)

    labelled = [piece(b, 0) for b in range(blocks + 1)]
    banded = [piece(b, 1) for b in range(blocks + 1)]
    diagonal = [masked(col >= row, band) for band in banded]
    beside = [masked(col < row, band) for band in banded[:blocks - 1]] + [corner[...]]
    nothing = jnp.zeros((window, window), jnp.bfloat16)
    pairs, bands = [], []
    for b in range(blocks):
        pairs.append(jnp.concatenate([labelled[b], labelled[b + 1]], axis=0))
        bands.append(jnp.concatenate([
            jnp.concatenate([diagonal[b], beside[b]], axis=1),
            jnp.concatenate([nothing, diagonal[b + 1]], axis=1),
        ], axis=0))

    copies = []
    step = next(n for n in range(min(7, tissues), 0, -1) if tissues % n == 0)
    for t in range(0, tissues, step):
        for b in range(blocks):
            half = placed[b, pl.ds(t * per_block, step * per_block), :]
            top = jnp.dot(half, pairs[b], preferred_element_type=jnp.float32)
            square = jnp.dot(half, bands[b], preferred_element_type=jnp.float32)
            variance = jnp.sum(square * half.astype(jnp.float32), axis=1, keepdims=True)
            scale = lax.rsqrt(jnp.maximum(variance, 0.0) + 1e-06) * root
            out[pl.ds(t, step), pl.ds(b * per_block, per_block), :] = (top * scale).reshape(step, per_block, window)
        part = pl.ds(t, step)
        copies.append(pltpu.make_async_copy(out.at[part], out_hbm.at[part], sem.at[t // step]))
        copies[-1].start()
    for copy in copies:
        copy.wait()


def on_device(genotype, phenotype, residual, sign_flips, weights, member, gene_start, gene_end):
    by_tissue = weights.transpose(1, 0, 2)
    near, far, corner, placed = reduced_sums(
        genotype, phenotype, residual, sign_flips, gene_start, gene_end, member, by_tissue)
    vmem = pl.BlockSpec(memory_space=pltpu.VMEM)
    scores = pl.pallas_call(
        functools.partial(scores_kernel, genotype.shape[0] * lax.axis_size("samp")),
        out_shape=jax.ShapeDtypeStruct(by_tissue.shape, jnp.float32),
        in_specs=[vmem] * 4,
        out_specs=pl.BlockSpec(memory_space=pltpu.HBM),
        scratch_shapes=[
            pltpu.VMEM(by_tissue.shape, jnp.float32),
            pltpu.SemaphoreType.DMA((by_tissue.shape[0],)),
        ],
        compiler_params=pltpu.CompilerParams(vmem_limit_bytes=VMEM_LIMIT),
        name="scores",
    )(near, far, corner, placed)
    return scores.transpose(1, 0, 2)


def solution(mesh):
    return jax.shard_map(
        on_device,
        mesh=mesh,
        in_specs=(
            P("samp", "snp"),
            P("samp"),
            P("samp"),
            P("samp", None),
            P("snp", None, None),
            P("snp", None),
            P("snp"),
            P("snp"),
        ),
        out_specs=P("snp", None, None),
        check_vma=False,
    )
```

```python
import functools

import jax
import jax.numpy as jnp
from jax import lax
from jax.experimental import pallas as pl
from jax.experimental.pallas import tpu as pltpu
from jax.sharding import PartitionSpec as P

MESH = pl.DeviceIdType.MESH
TILE = 16
PARTS = 4
HALVES = 2
VMEM_LIMIT = 24 * 1024 * 1024


def across(left, right):
    return lax.dot_general(left, right, (((0,), (0,)), ((), ())), preferred_element_type=jnp.float32)


def iotas(rows, cols):
    return (
        lax.broadcasted_iota(jnp.int32, (rows, cols), 0),
        lax.broadcasted_iota(jnp.int32, (rows, cols), 1),
    )


def share_of(rows, count):
    per = -(-rows // (count * TILE)) * TILE
    while rows % per:
        per += TILE
    return per


def square_of(rows):
    tiles, width = rows.shape
    return jnp.concatenate([rows, jnp.zeros((width - tiles, width), jnp.float32)], axis=0)


def sums_kernel(
    count, ring, window,
    geno, phen, resid, flips, starts, ends, member, weights,
    near_out, far_out, corner_out, placed_out,
    phen_v, resid_v, starts_v, ends_v, member_v, weights_v,
    data_v, flips_v, halo_v, back_v,
    main_s, main_r, main_p, main_g,
    late_s, late_r, back_s, back_r, fold_v, tail_v,
    sums_s, sums_r, sums_t, cols_v, near_v, next_v,
    load_sem, flip_sem, small_sem, halo_ss, halo_rs,
    ms_ss, ms_rs, mg_ss, mg_rs, lt_ss, lt_rs, bc_ss, bc_rs, td_ss, td_rs,
    sm_ss, sm_rs, st_ss, st_rs, bk_ss, bk_rs, fw_ss, fw_rs,
):
    me = lax.axis_index("samp")
    mine = lax.axis_index("snp")
    parity = lax.rem(mine, 2)
    odd, even = parity == 1, parity == 0
    has_before, has_after = mine > 0, mine < ring - 1
    before = jnp.maximum(mine - 1, 0)
    after = jnp.minimum(mine + 1, ring - 1)
    beyond = jnp.minimum(mine + 2, ring - 1)
    keeper = mine + 1 - parity
    partner = mine + 1 - 2 * parity
    slot = 1 - parity
    samples = data_v.shape[0]
    blocks, owners, _, per, _ = main_g.shape
    snps = blocks * window
    part = samples // PARTS
    split = samples // HALVES
    inverse = 1.0 / (samples * count)

    def peers(body, first=1):
        if count <= 16:
            for dist in range(first, count):
                body(dist)
        else:
            def step(dist, carry):
                body(dist)
                return carry
            lax.fori_loop(first, count, step, 0)

    def group(body):
        pl.when(even)(lambda: body(0))
        peers(body)

    def collect(wait, got, total, first=1):
        if count <= 16:
            for dist in range(first, count):
                wait(dist)
                total += got[dist].astype(jnp.float32)
            return total

        def step(dist, total):
            wait(dist)
            return total + got[dist].astype(jnp.float32)
        return lax.fori_loop(first, count, step, total)

    def ahead(dist):
        return lax.rem(me + dist, count)

    def behind(dist):
        return lax.rem(me + count - dist, count)

    small = [
        pltpu.make_async_copy(src, dst, small_sem.at[i])
        for i, (src, dst) in enumerate((
            (resid, resid_v), (phen, phen_v), (starts, starts_v), (ends, ends_v),
            (member, member_v), (weights, weights_v),
        ))
    ]
    flip_loads = []
    for copy in small[:2]:
        copy.start()
    for i in range(PARTS):
        rows = pl.ds(i * part, part)
        flip_loads.append(pltpu.make_async_copy(flips.at[rows], flips_v.at[rows], flip_sem.at[i]))
        flip_loads[i].start()
    load = pltpu.make_async_copy(geno, data_v.at[:, pl.ds(0, snps)], load_sem.at[0])
    load.start()

    barrier = pltpu.get_barrier_semaphore()

    def greet(dist, other):
        pl.semaphore_signal(barrier, inc=1, device_id=(ahead(dist), other), device_id_type=MESH)

    peers(lambda dist: greet(dist, mine))
    peers(lambda dist: greet(dist, partner), 0)
    pl.when(has_before & even)(lambda: greet(0, before))

    @pl.when(has_after & odd)
    def _():
        peers(lambda dist: greet(dist, after), 0)
        peers(lambda dist: greet(dist, beyond), 0)

    for copy in small[2:]:
        copy.start()

    for copy in small[:2]:
        copy.wait()
    phen_cols = square_of(phen_v[...]).T
    resid_cols = square_of(resid_v[...]).T
    lanes = phen_v.shape[1]
    for i in range(PARTS):
        flip_loads[i].wait()
        for t in range(i * part // lanes, (i + 1) * part // lanes):
            rows = pl.ds(t * lanes, lanes)
            signs = flips_v[rows, :].astype(jnp.float32)
            labels = jnp.concatenate([signs * resid_cols[:, t:t + 1], phen_cols[:, t:t + 1]], axis=1)
            data_v[rows, pl.ds(snps, window)] = labels.astype(jnp.bfloat16)

    load.wait()
    data = data_v[...]
    left = jnp.concatenate([data[:, :snps], jnp.ones((samples, 8), jnp.bfloat16)], axis=1)
    products = across(left, data)
    row8, _ = iotas(8, window)
    sums = jnp.zeros((8, window), jnp.float32)
    for b in range(blocks + 1):
        sums = jnp.where(row8 == b, products[snps:, b * window:(b + 1) * window], sums)
    sums_s[...] = sums
    row, col = iotas(window, window)
    for b in range(blocks):
        low, mid, high = b * window, (b + 1) * window, (b + 2) * window
        other = products[low:mid, mid:high] if b < blocks - 1 else 0.0
        band = jnp.where(col >= row, products[low:mid, low:mid], other)
        main_s[b, :, 0] = products[low:mid, snps:].astype(jnp.bfloat16).reshape(owners, per, window)
        main_s[b, :, 1] = band.astype(jnp.bfloat16).reshape(owners, per, window)

    def remote(src, dst, ss, rs, device):
        return pltpu.make_async_remote_copy(
            src_ref=src, dst_ref=dst, send_sem=ss, recv_sem=rs,
            device_id=device, device_id_type=MESH)

    halos = []
    for i in range(HALVES):
        rows = pl.ds(i * split, split)
        halos.append(remote(
            geno.at[rows, pl.ds(0, window)], halo_v.at[rows],
            halo_ss.at[i], halo_rs.at[i], (me, before)))
    back = remote(
        geno.at[pl.ds(split, samples - split), pl.ds(snps - window, window)], back_v,
        bk_ss.at[0], bk_rs.at[0], (me, after))

    def guarded(index, body):
        if owners == count:
            body()
        else:
            pl.when(index < owners)(body)

    def sums_copy(dist):
        return remote(
            sums_s, sums_r.at[slot, dist], sm_ss.at[dist], sm_rs.at[slot, dist], (ahead(dist), keeper))

    def scatter_copy(b, dist):
        return remote(
            main_s.at[b, ahead(dist)], main_r.at[slot, b, dist],
            ms_ss.at[b, dist], ms_rs.at[slot, b, dist], (ahead(dist), keeper))

    def gather_copy(s, b, dist, place):
        return remote(
            main_p.at[s, b], main_g.at[b, place], mg_ss.at[s, b, dist], mg_rs.at[b, dist],
            (ahead(dist), jnp.maximum(mine - s, 0)))

    def direct_copy(dist, place):
        return remote(
            main_p.at[1, 0], tail_v.at[place], td_ss.at[dist], td_rs.at[dist],
            (ahead(dist), jnp.maximum(mine - 2, 0)))

    forward = remote(main_g.at[0], tail_v, fw_ss.at[0], fw_rs.at[0], (me, before))

    def late_copy(dist):
        return remote(late_s, late_r.at[dist], lt_ss.at[dist], lt_rs.at[dist], (ahead(dist), mine))

    def back_copy(dist):
        return remote(back_s, back_r.at[dist], bc_ss.at[dist], bc_rs.at[dist], (ahead(dist), before))

    stats = [
        remote(sums_t.at[1], near_v, st_ss.at[0], st_rs.at[0], (me, before)),
        remote(sums_t.at[0], next_v, st_ss.at[1], st_rs.at[1], (me, before)),
        remote(sums_t.at[1], next_v, st_ss.at[2], st_rs.at[2], (me, jnp.maximum(mine - 2, 0))),
    ]
    further = odd & (mine > 1)

    pl.semaphore_wait(
        barrier,
        2 * count - 1 + jnp.where(has_before & even, count, 0)
        + jnp.where(has_after & odd, 1, 0) + jnp.where(further, count, 0))
    pl.when(has_before)(halos[0].start)

    @pl.when(has_before & odd)
    def _():
        for copy in halos[1:]:
            copy.start()

    pl.when(has_after & odd)(back.start)
    group(lambda dist: sums_copy(dist).start())
    for b in range(blocks):
        group(lambda dist: guarded(ahead(dist), lambda: scatter_copy(b, dist).start()))

    half = window // 2
    half_row, half_col = iotas(half, window)

    def fold(product):
        turned = pltpu.roll(product, half, 1)[:half]
        folded = jnp.where(half_col - half > half_row, product.T[half:], turned)
        return jnp.where(half_col < half, product[half:], folded).astype(jnp.bfloat16)

    def corner(arrived):
        for copy in halos[:arrived]:
            copy.wait_recv()
        rows = pl.ds(0, arrived * split)
        late_s[...] = fold(across(data_v[rows, pl.ds(snps - window, window)], halo_v[rows, :]))
        peers(lambda dist: late_copy(dist).start())

    pl.when(even)(lambda: corner(HALVES))

    for copy in small[2:]:
        copy.wait()
    place(mine * snps, starts_v, ends_v, member_v, weights_v, placed_out)

    @pl.when(has_before & even)
    def _():
        back.wait_recv()
        back_s[...] = fold(across(back_v[...], data_v[pl.ds(split, samples - split), pl.ds(0, window)]))
        peers(lambda dist: back_copy(dist).start(), 0)

    def settle(s):
        sums_t[s] = collect(
            lambda dist: remote(
                sums_s, sums_r.at[s, dist], sm_ss.at[dist], sm_rs.at[s, dist],
                (ahead(dist), partner)).wait_recv(),
            sums_r.at[s], sums_s[...] if s == 0 else jnp.zeros_like(sums_s), 1 - s)
        cols_v[s] = square_of(sums_t[s]).T

    def own(s, b):
        def body():
            total = collect(
                lambda dist: remote(
                    main_s.at[b, 0], main_r.at[s, b, dist], ms_ss.at[b, dist], ms_rs.at[s, b, dist],
                    (ahead(dist), partner)).wait_recv(),
                main_r.at[s, b],
                main_s[b, me].astype(jnp.float32) if s == 0 else jnp.zeros(main_p.shape[2:], jnp.float32), 1 - s)
            row_of, col_of = iotas(per, window)
            row_of = row_of + me * per
            at = cols_v[s, pl.ds(pl.multiple_of(me * per, per), per), :][:, b:b + 1] * inverse
            scored = total[0] - at * sums_t[s, blocks:blocks + 1, :]
            main_p[s, b, 0] = pltpu.roll(scored, 1, 1).astype(main_p.dtype)
            mean_row = sums_t[s, b:b + 1, :] * inverse
            if b < blocks - 1:
                mean_row = jnp.where(col_of >= row_of, mean_row, sums_t[s, b + 1:b + 2, :] * inverse)
            value = total[1] * inverse - at * mean_row
            value = jnp.where(col_of == row_of, value, 2.0 * value)
            main_p[s, b, 1] = value.astype(main_p.dtype)
            if s == 1 and b == 0:
                pl.when(further)(lambda: peers(lambda dist: direct_copy(dist, me).start(), 0))
            peers(lambda dist: gather_copy(s, b, dist, me).start(), 1 - s)
            if s == 0:
                main_g[b, me] = main_p[s, b]
        guarded(me, body)

    @pl.when(odd)
    def _():
        for s in range(2):
            settle(s)
        stats[0].start()
        stats[1].start()
        pl.when(further)(stats[2].start)
        for s in (1, 0):
            own(s, 0)

    pl.when(has_after & odd)(lambda: corner(1))

    @pl.when(odd)
    def _():
        for b in range(1, blocks):
            for s in (1, 0):
                own(s, b)

    def gathered(b):
        group(lambda dist: guarded(
            behind(dist), lambda: gather_copy(0, b, dist, behind(dist)).wait_recv()))

    gathered(0)
    pl.when(odd)(forward.start)

    @pl.when(has_after)
    def _():
        @pl.when(even)
        def _():
            stats[0].wait_recv()
            stats[1].wait_recv()

        @pl.when(odd)
        def _():
            near_v[...] = sums_t[0]
            stats[2].wait_recv()

        fold_v[...] = collect(
            lambda dist: late_copy(dist).wait_recv(), late_r, late_s[...].astype(jnp.float32))

        @pl.when(odd)
        def _():
            fold_v[...] = collect(lambda dist: back_copy(dist).wait_recv(), back_r, fold_v[...], 0)

        folded = fold_v[...]
        mirrored = jnp.concatenate([folded, folded], axis=0).T
        product = jnp.concatenate([
            pltpu.roll(folded, half, 1), jnp.where(half_col < half, folded, mirrored[half:])], axis=0)
        mean_col = square_of(near_v[...]).T[:, blocks - 1:blocks] * inverse
        value = product * inverse - mean_col * (next_v[0:1, :] * inverse)
        corner_out[...] = jnp.where(col < row, 2.0 * value, 0.0).astype(corner_out.dtype)

    for b in range(1, blocks):
        gathered(b)
    near_out[...] = main_g[...]

    @pl.when(has_after)
    def _():
        pl.when(even)(forward.wait_recv)
        pl.when(odd)(lambda: peers(lambda dist: guarded(
            behind(dist), lambda: direct_copy(dist, behind(dist)).wait_recv()), 0))
        far_out[...] = tail_v[...]

    @pl.when(jnp.logical_not(has_after))
    def _():
        corner_out[...] = jnp.zeros_like(corner_out)
        far_out[...] = jnp.zeros_like(far_out)

    pl.when(has_before)(halos[0].wait_send)
    pl.when(has_before & even)(lambda: peers(lambda dist: back_copy(dist).wait_send(), 0))
    pl.when(has_after & odd)(back.wait_send)
    pl.when(has_after)(lambda: peers(lambda dist: late_copy(dist).wait_send()))
    group(lambda dist: sums_copy(dist).wait_send())
    for b in range(blocks):
        group(lambda dist: guarded(ahead(dist), lambda: scatter_copy(b, dist).wait_send()))

    @pl.when(odd)
    def _():
        for copy in halos[1:]:
            copy.wait_send()
        stats[0].wait_send()
        stats[1].wait_send()
        pl.when(further)(stats[2].wait_send)

        forward.wait_send()

        def sent():
            for b in range(blocks):
                for s in range(2):
                    peers(lambda dist: gather_copy(s, b, dist, me).wait_send(), 1 - s)
            pl.when(further)(lambda: peers(lambda dist: direct_copy(dist, me).wait_send(), 0))
        guarded(me, sent)


def place(offset, starts, ends, member, weights, placed):
    tissues, genes, window = weights.shape
    blocks = placed.shape[0]
    per_block = genes // blocks
    gene_row, gene_col = iotas(genes, genes)

    def upright(row_ref):
        spread = jnp.broadcast_to(row_ref[...].astype(jnp.float32), (genes, genes))
        picked = jnp.where(gene_row == gene_col, spread, 0.0)
        return jnp.sum(picked, axis=1, keepdims=True).astype(jnp.int32)

    first, past = upright(starts), upright(ends)
    gene, lane = iotas(genes, window)
    inside = lane < past - first
    within = first - offset - (gene // per_block) * window
    owned = member[...]
    for t in range(tissues):
        kept = inside & (owned[:, t:t + 1] != 0)
        weights[t] = jnp.where(kept, weights[t].astype(jnp.float32), 0.0).astype(weights.dtype)
    near = lane >= within
    source = (lane - within) & (window - 1)
    for t in range(tissues):
        turned = jnp.take_along_axis(weights[t].astype(jnp.float32), source, axis=1)
        head = jnp.where(near, turned, 0.0).astype(placed.dtype)
        rest = jnp.where(near, 0.0, turned).astype(placed.dtype)
        rows = pl.ds(t * per_block, per_block)
        for b in range(blocks):
            genes_of = slice(b * per_block, (b + 1) * per_block)
            placed[b, rows, pl.ds(0, window)] = head[genes_of]
            placed[b, rows, pl.ds(window, window)] = rest[genes_of]


def reduced_sums(genotype, phenotype, residual, sign_flips, starts, ends, member, weights):
    samples, snps = genotype.shape
    tissues, genes, window = weights.shape
    count, ring = lax.axis_size("samp"), lax.axis_size("snp")
    blocks = snps // window
    per = share_of(window, count)
    owners = window // per
    half, wide = jnp.bfloat16, jnp.float32
    dma = pltpu.SemaphoreType.DMA
    vmem = pl.BlockSpec(memory_space=pltpu.VMEM)
    hbm = pl.BlockSpec(memory_space=pltpu.HBM)
    operands = (
        genotype, phenotype.reshape(-1, window), residual.reshape(-1, window), sign_flips,
        starts.reshape(1, genes), ends.reshape(1, genes), member, weights,
    )
    return pl.pallas_call(
        functools.partial(sums_kernel, count, ring, window),
        out_shape=(
            jax.ShapeDtypeStruct((blocks, owners, 2, per, window), half),
            jax.ShapeDtypeStruct((owners, 2, per, window), half),
            jax.ShapeDtypeStruct((window, window), half),
            jax.ShapeDtypeStruct((blocks, tissues * genes // blocks, 2 * window), half),
        ),
        in_specs=[hbm] * 8,
        out_specs=(vmem,) * 4,
        scratch_shapes=[pltpu.VMEM(x.shape, x.dtype) for x in operands[1:3] + operands[4:]] + [
            pltpu.VMEM((samples, snps + window), half),
            pltpu.VMEM(sign_flips.shape, jnp.int32),
            pltpu.VMEM((samples, window), half),
            pltpu.VMEM((samples - samples // HALVES, window), half),
            pltpu.VMEM((blocks, owners, 2, per, window), half),
            pltpu.VMEM((2, blocks, count, 2, per, window), half),
            pltpu.VMEM((2, blocks, 2, per, window), half),
            pltpu.VMEM((blocks, owners, 2, per, window), half),
            pltpu.VMEM((window // 2, window), half),
            pltpu.VMEM((count, window // 2, window), half),
            pltpu.VMEM((window // 2, window), half),
            pltpu.VMEM((count, window // 2, window), half),
            pltpu.VMEM((window // 2, window), wide),
            pltpu.VMEM((owners, 2, per, window), half),
            pltpu.VMEM((8, window), wide),
            pltpu.VMEM((2, count, 8, window), wide),
            pltpu.VMEM((2, 8, window), wide),
            pltpu.VMEM((2, window, window), wide),
            pltpu.VMEM((8, window), wide),
            pltpu.VMEM((8, window), wide),
            dma((1,)), dma((PARTS,)), dma((6,)), dma((HALVES,)), dma((HALVES,)),
            dma((blocks, count)), dma((2, blocks, count)), dma((2, blocks, count)), dma((blocks, count)),
            dma((count,)), dma((count,)), dma((count,)), dma((count,)), dma((count,)), dma((count,)),
            dma((count,)), dma((2, count)), dma((3,)), dma((3,)), dma((1,)), dma((1,)), dma((1,)), dma((1,)),
        ],
        compiler_params=pltpu.CompilerParams(
            collective_id=0, has_side_effects=True, vmem_limit_bytes=VMEM_LIMIT),
        name="sums",
    )(*(pltpu.with_memory_space_constraint(x, pltpu.HBM) for x in operands))


def scores_kernel(sample_total, near, far, corner, placed, out_hbm, out, sem):
    tissues, genes, window = out.shape
    blocks = placed.shape[0]
    per_block = genes // blocks
    row, col = iotas(window, window)
    root = 1.0 / (sample_total ** 0.5)

    def piece(b, kind):
        ref = near.at[b] if b < blocks else far
        return ref[:, kind].reshape(window, window)

    def masked(keep, value):
        return jnp.where(keep, value.astype(jnp.float32), 0.0).astype(jnp.bfloat16)

    labelled = [piece(b, 0) for b in range(blocks + 1)]
    banded = [piece(b, 1) for b in range(blocks + 1)]
    diagonal = [masked(col >= row, band) for band in banded]
    beside = [masked(col < row, band) for band in banded[:blocks - 1]] + [corner[...]]
    nothing = jnp.zeros((window, window), jnp.bfloat16)
    pairs, bands = [], []
    for b in range(blocks):
        pairs.append(jnp.concatenate([labelled[b], labelled[b + 1]], axis=0))
        bands.append(jnp.concatenate([
            jnp.concatenate([diagonal[b], beside[b]], axis=1),
            jnp.concatenate([nothing, diagonal[b + 1]], axis=1),
        ], axis=0))

    copies = []
    step = next(n for n in range(min(7, tissues), 0, -1) if tissues % n == 0)
    for t in range(0, tissues, step):
        for b in range(blocks):
            half = placed[b, pl.ds(t * per_block, step * per_block), :]
            top = jnp.dot(half, pairs[b], preferred_element_type=jnp.float32)
            square = jnp.dot(half, bands[b], preferred_element_type=jnp.float32)
            variance = jnp.sum(square * half.astype(jnp.float32), axis=1, keepdims=True)
            scale = lax.rsqrt(jnp.maximum(variance, 0.0) + 1e-06) * root
            out[pl.ds(t, step), pl.ds(b * per_block, per_block), :] = (top * scale).reshape(step, per_block, window)
        part = pl.ds(t, step)
        copies.append(pltpu.make_async_copy(out.at[part], out_hbm.at[part], sem.at[t // step]))
        copies[-1].start()
    for copy in copies:
        copy.wait()


def on_device(genotype, phenotype, residual, sign_flips, weights, member, gene_start, gene_end):
    by_tissue = weights.transpose(1, 0, 2)
    near, far, corner, placed = reduced_sums(
        genotype, phenotype, residual, sign_flips, gene_start, gene_end, member, by_tissue)
    vmem = pl.BlockSpec(memory_space=pltpu.VMEM)
    scores = pl.pallas_call(
        functools.partial(scores_kernel, genotype.shape[0] * lax.axis_size("samp")),
        out_shape=jax.ShapeDtypeStruct(by_tissue.shape, jnp.float32),
        in_specs=[vmem] * 4,
        out_specs=pl.BlockSpec(memory_space=pltpu.HBM),
        scratch_shapes=[
            pltpu.VMEM(by_tissue.shape, jnp.float32),
            pltpu.SemaphoreType.DMA((by_tissue.shape[0],)),
        ],
        compiler_params=pltpu.CompilerParams(vmem_limit_bytes=VMEM_LIMIT),
        name="scores",
    )(near, far, corner, placed)
    return scores.transpose(1, 0, 2)


def solution(mesh):
    return jax.shard_map(
        on_device,
        mesh=mesh,
        in_specs=(
            P("samp", "snp"),
            P("samp"),
            P("samp"),
            P("samp", None),
            P("snp", None, None),
            P("snp", None),
            P("snp"),
            P("snp"),
        ),
        out_specs=P("snp", None, None),
        check_vma=False,
    )
```

```python
import functools

import jax
import jax.numpy as jnp
from jax import lax
from jax.experimental import pallas as pl
from jax.experimental.pallas import tpu as pltpu
from jax.sharding import PartitionSpec as P

MESH = pl.DeviceIdType.MESH
TILE = 16
PARTS = 4
HALVES = 2
VMEM_LIMIT = 24 * 1024 * 1024


def across(left, right):
    return lax.dot_general(left, right, (((0,), (0,)), ((), ())), preferred_element_type=jnp.float32)


def iotas(rows, cols):
    return (
        lax.broadcasted_iota(jnp.int32, (rows, cols), 0),
        lax.broadcasted_iota(jnp.int32, (rows, cols), 1),
    )


def share_of(rows, count):
    per = -(-rows // (count * TILE)) * TILE
    while rows % per:
        per += TILE
    return per


def square_of(rows):
    tiles, width = rows.shape
    return jnp.concatenate([rows, jnp.zeros((width - tiles, width), jnp.float32)], axis=0)


def sums_kernel(
    count, ring, window,
    geno, phen, resid, flips, starts, ends, member, weights,
    near_out, far_out, corner_out, placed_out,
    phen_v, resid_v, starts_v, ends_v, member_v, weights_v,
    data_v, flips_v, halo_v, back_v,
    main_s, main_r, main_p, main_g,
    late_s, late_r, back_s, back_r, tail_v,
    sums_s, sums_r, sums_t, cols_v, next_v,
    load_sem, flip_sem, small_sem, halo_ss, halo_rs,
    ms_ss, ms_rs, mg_ss, mg_rs, lt_ss, lt_rs, bc_ss, bc_rs, td_ss, td_rs,
    sm_ss, sm_rs, st_ss, st_rs, bk_ss, bk_rs, fw_ss, fw_rs,
):
    me = lax.axis_index("samp")
    mine = lax.axis_index("snp")
    parity = lax.rem(mine, 2)
    odd, even = parity == 1, parity == 0
    has_before, has_after = mine > 0, mine < ring - 1
    before = jnp.maximum(mine - 1, 0)
    after = jnp.minimum(mine + 1, ring - 1)
    beyond = jnp.minimum(mine + 2, ring - 1)
    keeper = mine + 1 - parity
    partner = mine + 1 - 2 * parity
    slot = 1 - parity
    samples = data_v.shape[0]
    blocks, owners, _, per, _ = main_g.shape
    snps = blocks * window
    part = samples // PARTS
    split = samples // HALVES
    inverse = 1.0 / (samples * count)

    def peers(body, first=1):
        if count <= 16:
            for dist in range(first, count):
                body(dist)
        else:
            def step(dist, carry):
                body(dist)
                return carry
            lax.fori_loop(first, count, step, 0)

    def group(body):
        pl.when(even)(lambda: body(0))
        peers(body)

    def collect(wait, got, total, first=1):
        if count <= 16:
            for dist in range(first, count):
                wait(dist)
                total += got[dist].astype(jnp.float32)
            return total

        def step(dist, total):
            wait(dist)
            return total + got[dist].astype(jnp.float32)
        return lax.fori_loop(first, count, step, total)

    def ahead(dist):
        return lax.rem(me + dist, count)

    def behind(dist):
        return lax.rem(me + count - dist, count)

    small = [
        pltpu.make_async_copy(src, dst, small_sem.at[i])
        for i, (src, dst) in enumerate((
            (resid, resid_v), (phen, phen_v), (starts, starts_v), (ends, ends_v),
            (member, member_v), (weights, weights_v),
        ))
    ]
    flip_loads = []
    for copy in small[:2]:
        copy.start()
    for i in range(PARTS):
        rows = pl.ds(i * part, part)
        flip_loads.append(pltpu.make_async_copy(flips.at[rows], flips_v.at[rows], flip_sem.at[i]))
        flip_loads[i].start()
    load = pltpu.make_async_copy(geno, data_v.at[:, pl.ds(0, snps)], load_sem.at[0])
    load.start()

    barrier = pltpu.get_barrier_semaphore()

    def greet(dist, other):
        pl.semaphore_signal(barrier, inc=1, device_id=(ahead(dist), other), device_id_type=MESH)

    peers(lambda dist: greet(dist, mine))
    peers(lambda dist: greet(dist, partner), 0)
    pl.when(has_before & even)(lambda: greet(0, before))

    @pl.when(has_after & odd)
    def _():
        peers(lambda dist: greet(dist, after), 0)
        peers(lambda dist: greet(dist, beyond), 0)

    for copy in small[2:]:
        copy.start()

    for copy in small[:2]:
        copy.wait()
    phen_cols = square_of(phen_v[...]).T
    resid_cols = square_of(resid_v[...]).T
    lanes = phen_v.shape[1]
    for i in range(PARTS):
        flip_loads[i].wait()
        for t in range(i * part // lanes, (i + 1) * part // lanes):
            rows = pl.ds(t * lanes, lanes)
            signs = flips_v[rows, :].astype(jnp.float32)
            labels = jnp.concatenate([signs * resid_cols[:, t:t + 1], phen_cols[:, t:t + 1]], axis=1)
            data_v[rows, pl.ds(snps, window)] = labels.astype(jnp.bfloat16)

    load.wait()
    data = data_v[...]
    left = jnp.concatenate([data[:, :snps], jnp.ones((samples, 8), jnp.bfloat16)], axis=1)
    products = across(left, data)
    kinds = sums_s.shape[0]
    kind_of, _ = iotas(kinds, window)
    sums = jnp.zeros((kinds, window), jnp.float32)
    for b in range(blocks + 1):
        sums = jnp.where(kind_of == b, products[snps:snps + 1, b * window:(b + 1) * window], sums)
    sums_s[...] = sums
    row, col = iotas(window, window)
    for b in range(blocks):
        low, mid, high = b * window, (b + 1) * window, (b + 2) * window
        other = products[low:mid, mid:high] if b < blocks - 1 else 0.0
        band = jnp.where(col >= row, products[low:mid, low:mid], other)
        main_s[b, :, 0] = products[low:mid, snps:].astype(jnp.bfloat16).reshape(owners, per, window)
        main_s[b, :, 1] = band.astype(jnp.bfloat16).reshape(owners, per, window)

    def remote(src, dst, ss, rs, device):
        return pltpu.make_async_remote_copy(
            src_ref=src, dst_ref=dst, send_sem=ss, recv_sem=rs,
            device_id=device, device_id_type=MESH)

    halos = []
    for i in range(HALVES):
        rows = pl.ds(i * split, split)
        halos.append(remote(
            geno.at[rows, pl.ds(0, window)], halo_v.at[rows],
            halo_ss.at[i], halo_rs.at[i], (me, before)))
    back = remote(
        geno.at[pl.ds(split, samples - split), pl.ds(snps - window, window)], back_v,
        bk_ss.at[0], bk_rs.at[0], (me, after))

    def guarded(index, body):
        if owners == count:
            body()
        else:
            pl.when(index < owners)(body)

    def sums_copy(dist):
        return remote(
            sums_s, sums_r.at[slot, dist], sm_ss.at[dist], sm_rs.at[slot, dist], (ahead(dist), keeper))

    def scatter_copy(b, dist):
        return remote(
            main_s.at[b, ahead(dist)], main_r.at[slot, b, dist],
            ms_ss.at[b, dist], ms_rs.at[slot, b, dist], (ahead(dist), keeper))

    def gather_copy(s, b, dist, place):
        return remote(
            main_p.at[s, b], main_g.at[b, place], mg_ss.at[s, b, dist], mg_rs.at[b, dist],
            (ahead(dist), jnp.maximum(mine - s, 0)))

    def direct_copy(dist, place):
        return remote(
            main_p.at[1, 0], tail_v.at[place], td_ss.at[dist], td_rs.at[dist],
            (ahead(dist), jnp.maximum(mine - 2, 0)))

    forward = remote(main_g.at[0], tail_v, fw_ss.at[0], fw_rs.at[0], (me, before))

    def late_copy(dist):
        return remote(late_s, late_r.at[dist], lt_ss.at[dist], lt_rs.at[dist], (ahead(dist), mine))

    def back_copy(dist):
        return remote(back_s, back_r.at[dist], bc_ss.at[dist], bc_rs.at[dist], (ahead(dist), before))

    stats = remote(sums_t.at[1], next_v, st_ss.at[0], st_rs.at[0], (me, jnp.maximum(mine - 2, 0)))
    further = odd & (mine > 1)

    pl.semaphore_wait(
        barrier,
        2 * count - 1 + jnp.where(has_before & even, count, 0)
        + jnp.where(has_after & odd, 1, 0) + jnp.where(further, count, 0))
    pl.when(has_before)(halos[0].start)

    @pl.when(has_before & odd)
    def _():
        for copy in halos[1:]:
            copy.start()

    pl.when(has_after & odd)(back.start)
    group(lambda dist: sums_copy(dist).start())
    for b in range(blocks - 1):
        group(lambda dist: guarded(ahead(dist), lambda: scatter_copy(b, dist).start()))

    @pl.when(even)
    def _():
        for copy in halos:
            copy.wait_recv()
        beside = across(data_v[:, pl.ds(snps - window, window)], halo_v[...])
        band = jnp.where(col >= row, main_s[blocks - 1, :, 1].reshape(window, window).astype(jnp.float32), beside)
        main_s[blocks - 1, :, 1] = band.astype(jnp.bfloat16).reshape(owners, per, window)

    group(lambda dist: guarded(ahead(dist), lambda: scatter_copy(blocks - 1, dist).start()))

    half = window // 2
    half_row, half_col = iotas(half, window)

    def fold(product):
        turned = pltpu.roll(product, half, 1)[:half]
        folded = jnp.where(half_col - half > half_row, product.T[half:], turned)
        return jnp.where(half_col < half, product[half:], folded).astype(jnp.bfloat16)

    def corner():
        halos[0].wait_recv()
        rows = pl.ds(0, split)
        late_s[...] = fold(across(data_v[rows, pl.ds(snps - window, window)], halo_v[rows, :]))
        peers(lambda dist: late_copy(dist).start())

    for copy in small[2:]:
        copy.wait()
    place(mine * snps, starts_v, ends_v, member_v, weights_v, placed_out)

    @pl.when(has_before & even)
    def _():
        back.wait_recv()
        back_s[...] = fold(across(back_v[...], data_v[pl.ds(split, samples - split), pl.ds(0, window)]))
        peers(lambda dist: back_copy(dist).start(), 0)

    def settle(s):
        sums_t[s] = collect(
            lambda dist: remote(
                sums_s, sums_r.at[s, dist], sm_ss.at[dist], sm_rs.at[s, dist],
                (ahead(dist), partner)).wait_recv(),
            sums_r.at[s], sums_s[...] if s == 0 else jnp.zeros_like(sums_s), 1 - s)
        cols_v[s] = square_of(sums_t[s]).T

    def own(s, b):
        def body():
            total = collect(
                lambda dist: remote(
                    main_s.at[b, 0], main_r.at[s, b, dist], ms_ss.at[b, dist], ms_rs.at[s, b, dist],
                    (ahead(dist), partner)).wait_recv(),
                main_r.at[s, b],
                main_s[b, me].astype(jnp.float32) if s == 0 else jnp.zeros(main_p.shape[2:], jnp.float32), 1 - s)
            row_of, col_of = iotas(per, window)
            row_of = row_of + me * per
            at = cols_v[s, pl.ds(pl.multiple_of(me * per, per), per), :][:, b:b + 1] * inverse
            scored = total[0] - at * sums_t[s, blocks:blocks + 1, :]
            main_p[s, b, 0] = pltpu.roll(scored, 1, 1).astype(main_p.dtype)
            other = sums_t[s, b + 1:b + 2, :] if b < blocks - 1 else sums_t[0, 0:1, :]
            mean_row = jnp.where(col_of >= row_of, sums_t[s, b:b + 1, :], other) * inverse
            value = total[1] * inverse - at * mean_row
            value = jnp.where(col_of == row_of, value, 2.0 * value)
            main_p[s, b, 1] = value.astype(main_p.dtype)
            if s == 1 and b == 0:
                pl.when(further)(lambda: peers(lambda dist: direct_copy(dist, me).start(), 0))
            peers(lambda dist: gather_copy(s, b, dist, me).start(), 1 - s)
            if s == 0:
                main_g[b, me] = main_p[s, b]
        guarded(me, body)

    @pl.when(odd)
    def _():
        for s in range(2):
            settle(s)
        pl.when(further)(stats.start)
        for b in range(blocks - 1):
            own(1, b)
            own(0, b)
        own(0, blocks - 1)
        pl.when(has_after)(corner)
        own(1, blocks - 1)

    def gathered(b):
        group(lambda dist: guarded(
            behind(dist), lambda: gather_copy(0, b, dist, behind(dist)).wait_recv()))

    gathered(0)
    pl.when(odd)(forward.start)

    @pl.when(has_after & odd)
    def _():
        stats.wait_recv()
        folded = collect(
            lambda dist: late_copy(dist).wait_recv(), late_r, late_s[...].astype(jnp.float32))
        folded = collect(lambda dist: back_copy(dist).wait_recv(), back_r, folded, 0)
        mirrored = jnp.concatenate([folded, folded], axis=0).T
        product = jnp.concatenate([
            pltpu.roll(folded, half, 1), jnp.where(half_col < half, folded, mirrored[half:])], axis=0)
        mean_col = cols_v[0, :, blocks - 1:blocks] * inverse
        value = product * inverse - mean_col * (next_v[0:1, :] * inverse)
        corner_out[...] = jnp.where(col < row, 2.0 * value, 0.0).astype(corner_out.dtype)

    for b in range(1, blocks):
        gathered(b)
    near_out[...] = main_g[...]

    @pl.when(has_after)
    def _():
        @pl.when(even)
        def _():
            beside = main_g[blocks - 1, :, 1].reshape(window, window).astype(jnp.float32)
            corner_out[...] = jnp.where(col < row, beside, 0.0).astype(corner_out.dtype)
            forward.wait_recv()

        pl.when(odd)(lambda: peers(lambda dist: guarded(
            behind(dist), lambda: direct_copy(dist, behind(dist)).wait_recv()), 0))
        far_out[...] = tail_v[...]

    @pl.when(jnp.logical_not(has_after))
    def _():
        corner_out[...] = jnp.zeros_like(corner_out)
        far_out[...] = jnp.zeros_like(far_out)

    pl.when(has_before)(halos[0].wait_send)
    pl.when(has_before & even)(lambda: peers(lambda dist: back_copy(dist).wait_send(), 0))
    pl.when(has_after & odd)(back.wait_send)
    pl.when(has_after & odd)(lambda: peers(lambda dist: late_copy(dist).wait_send()))
    group(lambda dist: sums_copy(dist).wait_send())
    for b in range(blocks):
        group(lambda dist: guarded(ahead(dist), lambda: scatter_copy(b, dist).wait_send()))

    @pl.when(odd)
    def _():
        for copy in halos[1:]:
            copy.wait_send()
        pl.when(further)(stats.wait_send)

        forward.wait_send()

        def sent():
            for b in range(blocks):
                for s in range(2):
                    peers(lambda dist: gather_copy(s, b, dist, me).wait_send(), 1 - s)
            pl.when(further)(lambda: peers(lambda dist: direct_copy(dist, me).wait_send(), 0))
        guarded(me, sent)


def place(offset, starts, ends, member, weights, placed):
    tissues, genes, window = weights.shape
    blocks = placed.shape[0]
    per_block = genes // blocks
    gene_row, gene_col = iotas(genes, genes)

    def upright(row_ref):
        spread = jnp.broadcast_to(row_ref[...].astype(jnp.float32), (genes, genes))
        picked = jnp.where(gene_row == gene_col, spread, 0.0)
        return jnp.sum(picked, axis=1, keepdims=True).astype(jnp.int32)

    first, past = upright(starts), upright(ends)
    gene, lane = iotas(genes, window)
    inside = lane < past - first
    within = first - offset - (gene // per_block) * window
    owned = member[...]
    for t in range(tissues):
        kept = inside & (owned[:, t:t + 1] != 0)
        weights[t] = jnp.where(kept, weights[t].astype(jnp.float32), 0.0).astype(weights.dtype)
    near = lane >= within
    source = (lane - within) & (window - 1)
    for t in range(tissues):
        turned = jnp.take_along_axis(weights[t].astype(jnp.float32), source, axis=1)
        head = jnp.where(near, turned, 0.0).astype(placed.dtype)
        rest = jnp.where(near, 0.0, turned).astype(placed.dtype)
        rows = pl.ds(t * per_block, per_block)
        for b in range(blocks):
            genes_of = slice(b * per_block, (b + 1) * per_block)
            placed[b, rows, pl.ds(0, window)] = head[genes_of]
            placed[b, rows, pl.ds(window, window)] = rest[genes_of]


def reduced_sums(genotype, phenotype, residual, sign_flips, starts, ends, member, weights):
    samples, snps = genotype.shape
    tissues, genes, window = weights.shape
    count, ring = lax.axis_size("samp"), lax.axis_size("snp")
    blocks = snps // window
    per = share_of(window, count)
    owners = window // per
    kinds = -(-(blocks + 1) // 4) * 4
    half, wide = jnp.bfloat16, jnp.float32
    dma = pltpu.SemaphoreType.DMA
    vmem = pl.BlockSpec(memory_space=pltpu.VMEM)
    hbm = pl.BlockSpec(memory_space=pltpu.HBM)
    operands = (
        genotype, phenotype.reshape(-1, window), residual.reshape(-1, window), sign_flips,
        starts.reshape(1, genes), ends.reshape(1, genes), member, weights,
    )
    return pl.pallas_call(
        functools.partial(sums_kernel, count, ring, window),
        out_shape=(
            jax.ShapeDtypeStruct((blocks, owners, 2, per, window), half),
            jax.ShapeDtypeStruct((owners, 2, per, window), half),
            jax.ShapeDtypeStruct((window, window), half),
            jax.ShapeDtypeStruct((blocks, tissues * genes // blocks, 2 * window), half),
        ),
        in_specs=[hbm] * 8,
        out_specs=(vmem,) * 4,
        scratch_shapes=[pltpu.VMEM(x.shape, x.dtype) for x in operands[1:3] + operands[4:]] + [
            pltpu.VMEM((samples, snps + window), half),
            pltpu.VMEM(sign_flips.shape, jnp.int32),
            pltpu.VMEM((samples, window), half),
            pltpu.VMEM((samples - samples // HALVES, window), half),
            pltpu.VMEM((blocks, owners, 2, per, window), half),
            pltpu.VMEM((2, blocks, count, 2, per, window), half),
            pltpu.VMEM((2, blocks, 2, per, window), half),
            pltpu.VMEM((blocks, owners, 2, per, window), half),
            pltpu.VMEM((window // 2, window), half),
            pltpu.VMEM((count, window // 2, window), half),
            pltpu.VMEM((window // 2, window), half),
            pltpu.VMEM((count, window // 2, window), half),
            pltpu.VMEM((owners, 2, per, window), half),
            pltpu.VMEM((kinds, window), wide),
            pltpu.VMEM((2, count, kinds, window), wide),
            pltpu.VMEM((2, kinds, window), wide),
            pltpu.VMEM((2, window, window), wide),
            pltpu.VMEM((kinds, window), wide),
            dma((1,)), dma((PARTS,)), dma((6,)), dma((HALVES,)), dma((HALVES,)),
            dma((blocks, count)), dma((2, blocks, count)), dma((2, blocks, count)), dma((blocks, count)),
            dma((count,)), dma((count,)), dma((count,)), dma((count,)), dma((count,)), dma((count,)),
            dma((count,)), dma((2, count)), dma((1,)), dma((1,)), dma((1,)), dma((1,)), dma((1,)), dma((1,)),
        ],
        compiler_params=pltpu.CompilerParams(
            collective_id=0, has_side_effects=True, vmem_limit_bytes=VMEM_LIMIT),
        name="sums",
    )(*(pltpu.with_memory_space_constraint(x, pltpu.HBM) for x in operands))


def scores_kernel(sample_total, near, far, corner, placed, out_hbm, out, sem):
    tissues, genes, window = out.shape
    blocks = placed.shape[0]
    per_block = genes // blocks
    row, col = iotas(window, window)
    root = 1.0 / (sample_total ** 0.5)

    def piece(b, kind):
        ref = near.at[b] if b < blocks else far
        return ref[:, kind].reshape(window, window)

    def masked(keep, value):
        return jnp.where(keep, value.astype(jnp.float32), 0.0).astype(jnp.bfloat16)

    labelled = [piece(b, 0) for b in range(blocks + 1)]
    banded = [piece(b, 1) for b in range(blocks + 1)]
    diagonal = [masked(col >= row, band) for band in banded]
    beside = [masked(col < row, band) for band in banded[:blocks - 1]] + [corner[...]]
    nothing = jnp.zeros((window, window), jnp.bfloat16)
    pairs, bands = [], []
    for b in range(blocks):
        pairs.append(jnp.concatenate([labelled[b], labelled[b + 1]], axis=0))
        bands.append(jnp.concatenate([
            jnp.concatenate([diagonal[b], beside[b]], axis=1),
            jnp.concatenate([nothing, diagonal[b + 1]], axis=1),
        ], axis=0))

    copies = []
    step = next(n for n in range(min(7, tissues), 0, -1) if tissues % n == 0)
    for t in range(0, tissues, step):
        for b in range(blocks):
            half = placed[b, pl.ds(t * per_block, step * per_block), :]
            top = jnp.dot(half, pairs[b], preferred_element_type=jnp.float32)
            square = jnp.dot(half, bands[b], preferred_element_type=jnp.float32)
            variance = jnp.sum(square * half.astype(jnp.float32), axis=1, keepdims=True)
            scale = lax.rsqrt(jnp.maximum(variance, 0.0) + 1e-06) * root
            out[pl.ds(t, step), pl.ds(b * per_block, per_block), :] = (top * scale).reshape(step, per_block, window)
        part = pl.ds(t, step)
        copies.append(pltpu.make_async_copy(out.at[part], out_hbm.at[part], sem.at[t // step]))
        copies[-1].start()
    for copy in copies:
        copy.wait()


def on_device(genotype, phenotype, residual, sign_flips, weights, member, gene_start, gene_end):
    by_tissue = weights.transpose(1, 0, 2)
    near, far, corner, placed = reduced_sums(
        genotype, phenotype, residual, sign_flips, gene_start, gene_end, member, by_tissue)
    vmem = pl.BlockSpec(memory_space=pltpu.VMEM)
    scores = pl.pallas_call(
        functools.partial(scores_kernel, genotype.shape[0] * lax.axis_size("samp")),
        out_shape=jax.ShapeDtypeStruct(by_tissue.shape, jnp.float32),
        in_specs=[vmem] * 4,
        out_specs=pl.BlockSpec(memory_space=pltpu.HBM),
        scratch_shapes=[
            pltpu.VMEM(by_tissue.shape, jnp.float32),
            pltpu.SemaphoreType.DMA((by_tissue.shape[0],)),
        ],
        compiler_params=pltpu.CompilerParams(vmem_limit_bytes=VMEM_LIMIT),
        name="scores",
    )(near, far, corner, placed)
    return scores.transpose(1, 0, 2)


def solution(mesh):
    return jax.shard_map(
        on_device,
        mesh=mesh,
        in_specs=(
            P("samp", "snp"),
            P("samp"),
            P("samp"),
            P("samp", None),
            P("snp", None, None),
            P("snp", None),
            P("snp"),
            P("snp"),
        ),
        out_specs=P("snp", None, None),
        check_vma=False,
    )
```

```python
import functools

import jax
import jax.numpy as jnp
from jax import lax
from jax.experimental import pallas as pl
from jax.experimental.pallas import tpu as pltpu
from jax.sharding import PartitionSpec as P

MESH = pl.DeviceIdType.MESH
TILE = 16
PARTS = 4
HALVES = 2
VMEM_LIMIT = 24 * 1024 * 1024


def across(left, right):
    return lax.dot_general(left, right, (((0,), (0,)), ((), ())), preferred_element_type=jnp.float32)


def iotas(rows, cols):
    return (
        lax.broadcasted_iota(jnp.int32, (rows, cols), 0),
        lax.broadcasted_iota(jnp.int32, (rows, cols), 1),
    )


def share_of(rows, count):
    per = -(-rows // (count * TILE)) * TILE
    while rows % per:
        per += TILE
    return per


def square_of(rows):
    tiles, width = rows.shape
    return jnp.concatenate([rows, jnp.zeros((width - tiles, width), jnp.float32)], axis=0)


def sums_kernel(
    count, ring, window,
    geno, phen, resid, flips, starts, ends, member, weights,
    near_out, far_out, corner_out, placed_out,
    phen_v, resid_v, starts_v, ends_v, member_v, weights_v,
    data_v, flips_v, halo_v, back_v,
    main_s, main_r, main_p, main_g,
    late_s, late_r, back_s, back_r, tail_v,
    sums_s, sums_r, sums_t, cols_v, next_v,
    load_sem, flip_sem, small_sem, halo_ss, halo_rs,
    ms_ss, ms_rs, mg_ss, mg_rs, lt_ss, lt_rs, bc_ss, bc_rs, td_ss, td_rs,
    sm_ss, sm_rs, st_ss, st_rs, bk_ss, bk_rs, fw_ss, fw_rs,
):
    me = lax.axis_index("samp")
    mine = lax.axis_index("snp")
    parity = lax.rem(mine, 2)
    odd, even = parity == 1, parity == 0
    has_before, has_after = mine > 0, mine < ring - 1
    before = jnp.maximum(mine - 1, 0)
    after = jnp.minimum(mine + 1, ring - 1)
    beyond = jnp.minimum(mine + 2, ring - 1)
    keeper = mine + 1 - parity
    partner = mine + 1 - 2 * parity
    slot = 1 - parity
    samples = data_v.shape[0]
    blocks, owners, _, per, _ = main_g.shape
    snps = blocks * window
    part = samples // PARTS
    split = samples // HALVES
    inverse = 1.0 / (samples * count)

    def peers(body, first=1):
        if count <= 16:
            for dist in range(first, count):
                body(dist)
        else:
            def step(dist, carry):
                body(dist)
                return carry
            lax.fori_loop(first, count, step, 0)

    def group(body):
        pl.when(even)(lambda: body(0))
        peers(body)

    def collect(wait, got, total, first=1):
        if count <= 16:
            for dist in range(first, count):
                wait(dist)
                total += got[dist].astype(jnp.float32)
            return total

        def step(dist, total):
            wait(dist)
            return total + got[dist].astype(jnp.float32)
        return lax.fori_loop(first, count, step, total)

    def ahead(dist):
        return lax.rem(me + dist, count)

    def behind(dist):
        return lax.rem(me + count - dist, count)

    small = [
        pltpu.make_async_copy(src, dst, small_sem.at[i])
        for i, (src, dst) in enumerate((
            (resid, resid_v), (phen, phen_v), (starts, starts_v), (ends, ends_v),
            (member, member_v), (weights, weights_v),
        ))
    ]
    flip_loads = []
    for copy in small[:2]:
        copy.start()
    for i in range(PARTS):
        rows = pl.ds(i * part, part)
        flip_loads.append(pltpu.make_async_copy(flips.at[rows], flips_v.at[rows], flip_sem.at[i]))
        flip_loads[i].start()
    load = pltpu.make_async_copy(geno, data_v.at[:, pl.ds(0, snps)], load_sem.at[0])
    load.start()

    barrier = pltpu.get_barrier_semaphore()

    def greet(dist, other):
        pl.semaphore_signal(barrier, inc=1, device_id=(ahead(dist), other), device_id_type=MESH)

    peers(lambda dist: greet(dist, mine))
    peers(lambda dist: greet(dist, partner), 0)
    pl.when(has_before & even)(lambda: greet(0, before))

    @pl.when(has_after & odd)
    def _():
        peers(lambda dist: greet(dist, after), 0)
        peers(lambda dist: greet(dist, beyond), 0)

    for copy in small[2:]:
        copy.start()

    for copy in small[:2]:
        copy.wait()
    phen_cols = square_of(phen_v[...]).T
    resid_cols = square_of(resid_v[...]).T
    lanes = phen_v.shape[1]
    for i in range(PARTS):
        flip_loads[i].wait()
        for t in range(i * part // lanes, (i + 1) * part // lanes):
            rows = pl.ds(t * lanes, lanes)
            signs = flips_v[rows, :].astype(jnp.float32)
            labels = jnp.concatenate([signs * resid_cols[:, t:t + 1], phen_cols[:, t:t + 1]], axis=1)
            data_v[rows, pl.ds(snps, window)] = labels.astype(jnp.bfloat16)

    load.wait()
    data = data_v[...]
    left = jnp.concatenate([data[:, :snps], jnp.ones((samples, 8), jnp.bfloat16)], axis=1)
    products = across(left, data)
    kinds = sums_s.shape[0]
    kind_of, _ = iotas(kinds, window)
    sums = jnp.zeros((kinds, window), jnp.float32)
    for b in range(blocks + 1):
        sums = jnp.where(kind_of == b, products[snps:snps + 1, b * window:(b + 1) * window], sums)
    sums_s[...] = sums
    row, col = iotas(window, window)
    for b in range(blocks):
        low, mid, high = b * window, (b + 1) * window, (b + 2) * window
        other = products[low:mid, mid:high] if b < blocks - 1 else 0.0
        band = jnp.where(col >= row, products[low:mid, low:mid], other)
        main_s[b, :, 0] = products[low:mid, snps:].astype(jnp.bfloat16).reshape(owners, per, window)
        main_s[b, :, 1] = band.astype(jnp.bfloat16).reshape(owners, per, window)

    def remote(src, dst, ss, rs, device):
        return pltpu.make_async_remote_copy(
            src_ref=src, dst_ref=dst, send_sem=ss, recv_sem=rs,
            device_id=device, device_id_type=MESH)

    halos = []
    for i in range(HALVES):
        rows = pl.ds(i * split, split)
        halos.append(remote(
            geno.at[rows, pl.ds(0, window)], halo_v.at[rows],
            halo_ss.at[i], halo_rs.at[i], (me, before)))
    back = remote(
        geno.at[pl.ds(split, samples - split), pl.ds(snps - window, window)], back_v,
        bk_ss.at[0], bk_rs.at[0], (me, after))

    def guarded(index, body):
        if owners == count:
            body()
        else:
            pl.when(index < owners)(body)

    def sums_copy(dist):
        return remote(
            sums_s, sums_r.at[slot, dist], sm_ss.at[dist], sm_rs.at[slot, dist], (ahead(dist), keeper))

    def scatter_copy(b, dist):
        return remote(
            main_s.at[b, ahead(dist)], main_r.at[slot, b, dist],
            ms_ss.at[b, dist], ms_rs.at[slot, b, dist], (ahead(dist), keeper))

    def everyone(body, apart):
        def one(other):
            if apart is None:
                body(other)
            else:
                pl.when((other != me) | apart)(lambda: body(other))
        if count <= 16:
            for other in range(count):
                one(other)
        else:
            def step(other, carry):
                one(other)
                return carry
            lax.fori_loop(0, count, step, 0)

    def gather_copy(s, b, other, place, source):
        return remote(
            main_p.at[s, b], main_g.at[b, place], mg_ss.at[s, b, other], mg_rs.at[b, source],
            (other, jnp.maximum(mine - s, 0)))

    def direct_copy(dist, place):
        return remote(
            main_p.at[1, 0], tail_v.at[place], td_ss.at[dist], td_rs.at[dist],
            (ahead(dist), jnp.maximum(mine - 2, 0)))

    forward = remote(main_g.at[0], tail_v, fw_ss.at[0], fw_rs.at[0], (me, before))

    def late_copy(dist):
        return remote(late_s, late_r.at[dist], lt_ss.at[dist], lt_rs.at[dist], (ahead(dist), mine))

    def back_copy(dist):
        return remote(back_s, back_r.at[dist], bc_ss.at[dist], bc_rs.at[dist], (ahead(dist), before))

    stats = remote(sums_t.at[1], next_v, st_ss.at[0], st_rs.at[0], (me, jnp.maximum(mine - 2, 0)))
    further = odd & (mine > 1)

    pl.semaphore_wait(
        barrier,
        2 * count - 1 + jnp.where(has_before & even, count, 0)
        + jnp.where(has_after & odd, 1, 0) + jnp.where(further, count, 0))
    pl.when(has_before)(halos[0].start)

    @pl.when(has_before & odd)
    def _():
        for copy in halos[1:]:
            copy.start()

    pl.when(has_after & odd)(back.start)
    group(lambda dist: sums_copy(dist).start())
    for b in range(blocks - 1):
        group(lambda dist: guarded(ahead(dist), lambda: scatter_copy(b, dist).start()))

    @pl.when(even)
    def _():
        for copy in halos:
            copy.wait_recv()
        beside = across(data_v[:, pl.ds(snps - window, window)], halo_v[...])
        band = jnp.where(col >= row, main_s[blocks - 1, :, 1].reshape(window, window).astype(jnp.float32), beside)
        main_s[blocks - 1, :, 1] = band.astype(jnp.bfloat16).reshape(owners, per, window)

    group(lambda dist: guarded(ahead(dist), lambda: scatter_copy(blocks - 1, dist).start()))

    half = window // 2
    half_row, half_col = iotas(half, window)

    def fold(product):
        turned = pltpu.roll(product, half, 1)[:half]
        folded = jnp.where(half_col - half > half_row, product.T[half:], turned)
        return jnp.where(half_col < half, product[half:], folded).astype(jnp.bfloat16)

    def corner():
        halos[0].wait_recv()
        rows = pl.ds(0, split)
        late_s[...] = fold(across(data_v[rows, pl.ds(snps - window, window)], halo_v[rows, :]))
        peers(lambda dist: late_copy(dist).start())

    for copy in small[2:]:
        copy.wait()
    place(mine * snps, starts_v, ends_v, member_v, weights_v, placed_out)

    @pl.when(has_before & even)
    def _():
        back.wait_recv()
        back_s[...] = fold(across(back_v[...], data_v[pl.ds(split, samples - split), pl.ds(0, window)]))
        peers(lambda dist: back_copy(dist).start(), 0)

    def settle(s):
        sums_t[s] = collect(
            lambda dist: remote(
                sums_s, sums_r.at[s, dist], sm_ss.at[dist], sm_rs.at[s, dist],
                (ahead(dist), partner)).wait_recv(),
            sums_r.at[s], sums_s[...] if s == 0 else jnp.zeros_like(sums_s), 1 - s)
        cols_v[s] = square_of(sums_t[s]).T

    def own(s, b):
        def body():
            total = collect(
                lambda dist: remote(
                    main_s.at[b, 0], main_r.at[s, b, dist], ms_ss.at[b, dist], ms_rs.at[s, b, dist],
                    (ahead(dist), partner)).wait_recv(),
                main_r.at[s, b],
                main_s[b, me].astype(jnp.float32) if s == 0 else jnp.zeros(main_p.shape[2:], jnp.float32), 1 - s)
            row_of, col_of = iotas(per, window)
            row_of = row_of + me * per
            at = cols_v[s, pl.ds(pl.multiple_of(me * per, per), per), :][:, b:b + 1] * inverse
            scored = total[0] - at * sums_t[s, blocks:blocks + 1, :]
            main_p[s, b, 0] = pltpu.roll(scored, 1, 1).astype(main_p.dtype)
            other = sums_t[s, b + 1:b + 2, :] if b < blocks - 1 else sums_t[0, 0:1, :]
            mean_row = jnp.where(col_of >= row_of, sums_t[s, b:b + 1, :], other) * inverse
            value = total[1] * inverse - at * mean_row
            value = jnp.where(col_of == row_of, value, 2.0 * value)
            main_p[s, b, 1] = value.astype(main_p.dtype)
            if s == 1 and b == 0:
                pl.when(further)(lambda: peers(lambda dist: direct_copy(dist, me).start(), 0))
            everyone(lambda other: gather_copy(s, b, other, me, me).start(), None if s else False)
            if s == 0:
                main_g[b, me] = main_p[s, b]
        guarded(me, body)

    @pl.when(odd)
    def _():
        for s in range(2):
            settle(s)
        pl.when(further)(stats.start)
        for b in range(blocks - 1):
            own(1, b)
            own(0, b)
        own(0, blocks - 1)
        own(1, blocks - 1)
        pl.when(has_after)(corner)

    def gathered(b):
        everyone(lambda other: guarded(
            other, lambda: gather_copy(0, b, other, other, other).wait_recv()), even)
        near_out[b] = main_g[b]

    pl.when(has_before)(halos[0].wait_send)
    pl.when(has_before & even)(lambda: peers(lambda dist: back_copy(dist).wait_send(), 0))
    pl.when(has_after & odd)(back.wait_send)
    pl.when(has_after & odd)(lambda: peers(lambda dist: late_copy(dist).wait_send()))
    group(lambda dist: sums_copy(dist).wait_send())
    for b in range(blocks):
        group(lambda dist: guarded(ahead(dist), lambda: scatter_copy(b, dist).wait_send()))

    @pl.when(odd)
    def _():
        for copy in halos[1:]:
            copy.wait_send()
        pl.when(further)(stats.wait_send)

        def sent():
            for b in range(blocks):
                for s in range(2):
                    everyone(lambda other: gather_copy(s, b, other, me, me).wait_send(), None if s else False)
            pl.when(further)(lambda: peers(lambda dist: direct_copy(dist, me).wait_send(), 0))
        guarded(me, sent)

    gathered(0)
    pl.when(odd)(forward.start)

    @pl.when(has_after & odd)
    def _():
        stats.wait_recv()
        folded = collect(
            lambda dist: late_copy(dist).wait_recv(), late_r, late_s[...].astype(jnp.float32))
        folded = collect(lambda dist: back_copy(dist).wait_recv(), back_r, folded, 0)
        mirrored = jnp.concatenate([folded, folded], axis=0).T
        product = jnp.concatenate([
            pltpu.roll(folded, half, 1), jnp.where(half_col < half, folded, mirrored[half:])], axis=0)
        mean_col = cols_v[0, :, blocks - 1:blocks] * inverse
        value = product * inverse - mean_col * (next_v[0:1, :] * inverse)
        corner_out[...] = jnp.where(col < row, 2.0 * value, 0.0).astype(corner_out.dtype)

    for b in range(1, blocks):
        gathered(b)

    @pl.when(has_after)
    def _():
        @pl.when(even)
        def _():
            beside = main_g[blocks - 1, :, 1].reshape(window, window).astype(jnp.float32)
            corner_out[...] = jnp.where(col < row, beside, 0.0).astype(corner_out.dtype)
            forward.wait_recv()

        pl.when(odd)(lambda: peers(lambda dist: guarded(
            behind(dist), lambda: direct_copy(dist, behind(dist)).wait_recv()), 0))
        far_out[...] = tail_v[...]

    @pl.when(jnp.logical_not(has_after))
    def _():
        corner_out[...] = jnp.zeros_like(corner_out)
        far_out[...] = jnp.zeros_like(far_out)

    pl.when(odd)(forward.wait_send)


def place(offset, starts, ends, member, weights, placed):
    tissues, genes, window = weights.shape
    blocks = placed.shape[0]
    per_block = genes // blocks
    gene_row, gene_col = iotas(genes, genes)

    def upright(row_ref):
        spread = jnp.broadcast_to(row_ref[...].astype(jnp.float32), (genes, genes))
        picked = jnp.where(gene_row == gene_col, spread, 0.0)
        return jnp.sum(picked, axis=1, keepdims=True).astype(jnp.int32)

    first, past = upright(starts), upright(ends)
    gene, lane = iotas(genes, window)
    inside = lane < past - first
    within = first - offset - (gene // per_block) * window
    owned = member[...]
    for t in range(tissues):
        kept = inside & (owned[:, t:t + 1] != 0)
        weights[t] = jnp.where(kept, weights[t].astype(jnp.float32), 0.0).astype(weights.dtype)
    near = lane >= within
    source = (lane - within) & (window - 1)
    for t in range(tissues):
        turned = jnp.take_along_axis(weights[t].astype(jnp.float32), source, axis=1)
        head = jnp.where(near, turned, 0.0).astype(placed.dtype)
        rest = jnp.where(near, 0.0, turned).astype(placed.dtype)
        rows = pl.ds(t * per_block, per_block)
        for b in range(blocks):
            genes_of = slice(b * per_block, (b + 1) * per_block)
            placed[b, rows, pl.ds(0, window)] = head[genes_of]
            placed[b, rows, pl.ds(window, window)] = rest[genes_of]


def reduced_sums(genotype, phenotype, residual, sign_flips, starts, ends, member, weights):
    samples, snps = genotype.shape
    tissues, genes, window = weights.shape
    count, ring = lax.axis_size("samp"), lax.axis_size("snp")
    blocks = snps // window
    per = share_of(window, count)
    owners = window // per
    kinds = -(-(blocks + 1) // 4) * 4
    half, wide = jnp.bfloat16, jnp.float32
    dma = pltpu.SemaphoreType.DMA
    vmem = pl.BlockSpec(memory_space=pltpu.VMEM)
    hbm = pl.BlockSpec(memory_space=pltpu.HBM)
    operands = (
        genotype, phenotype.reshape(-1, window), residual.reshape(-1, window), sign_flips,
        starts.reshape(1, genes), ends.reshape(1, genes), member, weights,
    )
    return pl.pallas_call(
        functools.partial(sums_kernel, count, ring, window),
        out_shape=(
            jax.ShapeDtypeStruct((blocks, owners, 2, per, window), half),
            jax.ShapeDtypeStruct((owners, 2, per, window), half),
            jax.ShapeDtypeStruct((window, window), half),
            jax.ShapeDtypeStruct((blocks, tissues * genes // blocks, 2 * window), half),
        ),
        in_specs=[hbm] * 8,
        out_specs=(vmem,) * 4,
        scratch_shapes=[pltpu.VMEM(x.shape, x.dtype) for x in operands[1:3] + operands[4:]] + [
            pltpu.VMEM((samples, snps + window), half),
            pltpu.VMEM(sign_flips.shape, jnp.int32),
            pltpu.VMEM((samples, window), half),
            pltpu.VMEM((samples - samples // HALVES, window), half),
            pltpu.VMEM((blocks, owners, 2, per, window), half),
            pltpu.VMEM((2, blocks, count, 2, per, window), half),
            pltpu.VMEM((2, blocks, 2, per, window), half),
            pltpu.VMEM((blocks, owners, 2, per, window), half),
            pltpu.VMEM((window // 2, window), half),
            pltpu.VMEM((count, window // 2, window), half),
            pltpu.VMEM((window // 2, window), half),
            pltpu.VMEM((count, window // 2, window), half),
            pltpu.VMEM((owners, 2, per, window), half),
            pltpu.VMEM((kinds, window), wide),
            pltpu.VMEM((2, count, kinds, window), wide),
            pltpu.VMEM((2, kinds, window), wide),
            pltpu.VMEM((2, window, window), wide),
            pltpu.VMEM((kinds, window), wide),
            dma((1,)), dma((PARTS,)), dma((6,)), dma((HALVES,)), dma((HALVES,)),
            dma((blocks, count)), dma((2, blocks, count)), dma((2, blocks, count)), dma((blocks, count)),
            dma((count,)), dma((count,)), dma((count,)), dma((count,)), dma((count,)), dma((count,)),
            dma((count,)), dma((2, count)), dma((1,)), dma((1,)), dma((1,)), dma((1,)), dma((1,)), dma((1,)),
        ],
        compiler_params=pltpu.CompilerParams(
            collective_id=0, has_side_effects=True, vmem_limit_bytes=VMEM_LIMIT),
        name="sums",
    )(*(pltpu.with_memory_space_constraint(x, pltpu.HBM) for x in operands))


def scores_kernel(sample_total, near, far, corner, placed, out_hbm, out, sem):
    tissues, genes, window = out.shape
    blocks = placed.shape[0]
    per_block = genes // blocks
    row, col = iotas(window, window)
    root = 1.0 / (sample_total ** 0.5)

    def piece(b, kind):
        ref = near.at[b] if b < blocks else far
        return ref[:, kind].reshape(window, window)

    def masked(keep, value):
        return jnp.where(keep, value.astype(jnp.float32), 0.0).astype(jnp.bfloat16)

    labelled = [piece(b, 0) for b in range(blocks + 1)]
    banded = [piece(b, 1) for b in range(blocks + 1)]
    diagonal = [masked(col >= row, band) for band in banded]
    beside = [masked(col < row, band) for band in banded[:blocks - 1]] + [corner[...]]
    nothing = jnp.zeros((window, window), jnp.bfloat16)
    pairs, bands = [], []
    for b in range(blocks):
        pairs.append(jnp.concatenate([labelled[b], labelled[b + 1]], axis=0))
        bands.append(jnp.concatenate([
            jnp.concatenate([diagonal[b], beside[b]], axis=1),
            jnp.concatenate([nothing, diagonal[b + 1]], axis=1),
        ], axis=0))

    copies = []
    step = next(n for n in range(min(7, tissues), 0, -1) if tissues % n == 0)
    for t in range(0, tissues, step):
        for b in range(blocks):
            half = placed[b, pl.ds(t * per_block, step * per_block), :]
            top = jnp.dot(half, pairs[b], preferred_element_type=jnp.float32)
            square = jnp.dot(half, bands[b], preferred_element_type=jnp.float32)
            variance = jnp.sum(square * half.astype(jnp.float32), axis=1, keepdims=True)
            scale = lax.rsqrt(jnp.maximum(variance, 0.0) + 1e-06) * root
            out[pl.ds(t, step), pl.ds(b * per_block, per_block), :] = (top * scale).reshape(step, per_block, window)
        part = pl.ds(t, step)
        copies.append(pltpu.make_async_copy(out.at[part], out_hbm.at[part], sem.at[t // step]))
        copies[-1].start()
    for copy in copies:
        copy.wait()


def on_device(genotype, phenotype, residual, sign_flips, weights, member, gene_start, gene_end):
    by_tissue = weights.transpose(1, 0, 2)
    near, far, corner, placed = reduced_sums(
        genotype, phenotype, residual, sign_flips, gene_start, gene_end, member, by_tissue)
    vmem = pl.BlockSpec(memory_space=pltpu.VMEM)
    scores = pl.pallas_call(
        functools.partial(scores_kernel, genotype.shape[0] * lax.axis_size("samp")),
        out_shape=jax.ShapeDtypeStruct(by_tissue.shape, jnp.float32),
        in_specs=[vmem] * 4,
        out_specs=pl.BlockSpec(memory_space=pltpu.HBM),
        scratch_shapes=[
            pltpu.VMEM(by_tissue.shape, jnp.float32),
            pltpu.SemaphoreType.DMA((by_tissue.shape[0],)),
        ],
        compiler_params=pltpu.CompilerParams(vmem_limit_bytes=VMEM_LIMIT),
        name="scores",
    )(near, far, corner, placed)
    return scores.transpose(1, 0, 2)


def solution(mesh):
    return jax.shard_map(
        on_device,
        mesh=mesh,
        in_specs=(
            P("samp", "snp"),
            P("samp"),
            P("samp"),
            P("samp", None),
            P("snp", None, None),
            P("snp", None),
            P("snp"),
            P("snp"),
        ),
        out_specs=P("snp", None, None),
        check_vma=False,
    )
```

```python
import functools

import jax
import jax.numpy as jnp
from jax import lax
from jax.experimental import pallas as pl
from jax.experimental.pallas import tpu as pltpu
from jax.sharding import PartitionSpec as P

MESH = pl.DeviceIdType.MESH
TILE = 16
PARTS = 2
HALVES = 2
VMEM_LIMIT = 24 * 1024 * 1024


def across(left, right):
    return lax.dot_general(left, right, (((0,), (0,)), ((), ())), preferred_element_type=jnp.float32)


def iotas(rows, cols):
    return (
        lax.broadcasted_iota(jnp.int32, (rows, cols), 0),
        lax.broadcasted_iota(jnp.int32, (rows, cols), 1),
    )


def share_of(rows, count):
    per = -(-rows // (count * TILE)) * TILE
    while rows % per:
        per += TILE
    return per


def square_of(rows):
    tiles, width = rows.shape
    return jnp.concatenate([rows, jnp.zeros((width - tiles, width), jnp.float32)], axis=0)


def sums_kernel(
    count, ring, window,
    geno, phen, resid, flips, starts, ends, member, weights,
    near_out, far_out, corner_out, placed_out,
    phen_v, resid_v, starts_v, ends_v, member_v, weights_v,
    data_v, flips_v, halo_v, back_v,
    main_s, main_r, main_p, main_g,
    late_s, late_r, back_s, back_r, tail_v,
    sums_s, sums_r, sums_t, cols_v, next_v,
    load_sem, flip_sem, small_sem, halo_ss, halo_rs,
    ms_ss, ms_rs, mg_ss, mg_rs, lt_ss, lt_rs, bc_ss, bc_rs, td_ss, td_rs,
    sm_ss, sm_rs, st_ss, st_rs, bk_ss, bk_rs, fw_ss, fw_rs,
):
    me = lax.axis_index("samp")
    mine = lax.axis_index("snp")
    parity = lax.rem(mine, 2)
    odd, even = parity == 1, parity == 0
    has_before, has_after = mine > 0, mine < ring - 1
    before = jnp.maximum(mine - 1, 0)
    after = jnp.minimum(mine + 1, ring - 1)
    beyond = jnp.minimum(mine + 2, ring - 1)
    keeper = mine + 1 - parity
    partner = mine + 1 - 2 * parity
    slot = 1 - parity
    samples = data_v.shape[0]
    blocks, owners, _, per, _ = main_g.shape
    snps = blocks * window
    part = samples // PARTS
    split = samples // HALVES
    inverse = 1.0 / (samples * count)

    def peers(body, first=1):
        if count <= 16:
            for dist in range(first, count):
                body(dist)
        else:
            def step(dist, carry):
                body(dist)
                return carry
            lax.fori_loop(first, count, step, 0)

    def group(body):
        pl.when(even)(lambda: body(0))
        peers(body)

    def collect(wait, got, total, first=1):
        if count <= 16:
            for dist in range(first, count):
                wait(dist)
                total += got[dist].astype(jnp.float32)
            return total

        def step(dist, total):
            wait(dist)
            return total + got[dist].astype(jnp.float32)
        return lax.fori_loop(first, count, step, total)

    def ahead(dist):
        return lax.rem(me + dist, count)

    def behind(dist):
        return lax.rem(me + count - dist, count)

    small = [
        pltpu.make_async_copy(src, dst, small_sem.at[i])
        for i, (src, dst) in enumerate((
            (resid, resid_v), (phen, phen_v), (starts, starts_v), (ends, ends_v),
            (member, member_v), (weights, weights_v),
        ))
    ]
    flip_loads = []
    for i in range(PARTS):
        rows = pl.ds(i * part, part)
        flip_loads.append(pltpu.make_async_copy(flips.at[rows], flips_v.at[rows], flip_sem.at[i]))
    for copy in small[:2] + flip_loads:
        copy.start()
    load = pltpu.make_async_copy(geno, data_v.at[:, pl.ds(0, snps)], load_sem.at[0])
    load.start()

    class Behind:
        def __init__(self, ref):
            self.ref = ref

        def __getitem__(self, dist):
            return self.ref[behind(dist)]

    barrier = pltpu.get_barrier_semaphore()

    def greet(dist, other):
        pl.semaphore_signal(barrier, inc=1, device_id=(ahead(dist), other), device_id_type=MESH)

    peers(lambda dist: greet(dist, mine))
    peers(lambda dist: greet(dist, partner), 0)
    pl.when(has_before & even)(lambda: greet(0, before))

    @pl.when(has_after & odd)
    def _():
        peers(lambda dist: greet(dist, after), 0)
        peers(lambda dist: greet(dist, beyond), 0)

    for copy in small[2:]:
        copy.start()

    for copy in small[:2]:
        copy.wait()
    phen_cols = square_of(phen_v[...]).T
    resid_cols = square_of(resid_v[...]).T
    lanes = phen_v.shape[1]
    for i in range(PARTS):
        flip_loads[i].wait()
        for t in range(i * part // lanes, (i + 1) * part // lanes):
            rows = pl.ds(t * lanes, lanes)
            signs = flips_v[rows, :].astype(jnp.float32)
            labels = jnp.concatenate([signs * resid_cols[:, t:t + 1], phen_cols[:, t:t + 1]], axis=1)
            data_v[rows, pl.ds(snps, window)] = labels.astype(jnp.bfloat16)

    load.wait()
    row, col = iotas(window, window)

    def packed(b):
        left = data_v[:, pl.ds(b * window, window)]
        if b == 0:
            left = jnp.concatenate([left, jnp.ones((samples, 8), jnp.bfloat16)], axis=1)
        products = across(left, data_v[:, pl.ds(b * window, snps + window - b * window)])
        other = products[:window, window:2 * window] if b < blocks - 1 else 0.0
        band = jnp.where(col >= row, products[:window, :window], other)
        scored = products[:window, snps - b * window:]
        main_s[b, :, 0] = scored.astype(jnp.bfloat16).reshape(owners, per, window)
        main_s[b, :, 1] = band.astype(jnp.bfloat16).reshape(owners, per, window)
        if b == 0:
            kinds = sums_s.shape[0]
            kind_of, _ = iotas(kinds, window)
            sums = jnp.zeros((kinds, window), jnp.float32)
            for at in range(blocks + 1):
                total = products[window:window + 1, at * window:(at + 1) * window]
                sums = jnp.where(kind_of == at, total, sums)
            sums_s[...] = sums

    packed(0)

    def remote(src, dst, ss, rs, device):
        return pltpu.make_async_remote_copy(
            src_ref=src, dst_ref=dst, send_sem=ss, recv_sem=rs,
            device_id=device, device_id_type=MESH)

    halos = []
    for i in range(HALVES):
        rows = pl.ds(i * split, split)
        halos.append(remote(
            geno.at[rows, pl.ds(0, window)], halo_v.at[rows],
            halo_ss.at[i], halo_rs.at[i], (me, before)))
    back = remote(
        geno.at[pl.ds(split, samples - split), pl.ds(snps - window, window)], back_v,
        bk_ss.at[0], bk_rs.at[0], (me, after))

    def guarded(index, body):
        if owners == count:
            body()
        else:
            pl.when(index < owners)(body)

    def sums_copy(dist):
        return remote(
            sums_s, sums_r.at[slot, dist], sm_ss.at[dist], sm_rs.at[slot, dist], (ahead(dist), keeper))

    def scatter_copy(b, dist):
        return remote(
            main_s.at[b, ahead(dist)], main_r.at[slot, b, dist],
            ms_ss.at[b, dist], ms_rs.at[slot, b, dist], (ahead(dist), keeper))

    def everyone(body, apart):
        def one(other):
            if apart is None:
                body(other)
            else:
                pl.when((other != me) | apart)(lambda: body(other))
        if count <= 16:
            for other in range(count):
                one(other)
        else:
            def step(other, carry):
                one(other)
                return carry
            lax.fori_loop(0, count, step, 0)

    def gather_copy(s, b, other, place, source):
        return remote(
            main_p.at[s, b], main_g.at[b, place], mg_ss.at[s, b, other], mg_rs.at[b, source],
            (other, jnp.maximum(mine - s, 0)))

    def direct_copy(dist, place):
        return remote(
            main_p.at[1, 0], tail_v.at[place], td_ss.at[dist], td_rs.at[dist],
            (ahead(dist), jnp.maximum(mine - 2, 0)))

    forward = remote(main_g.at[0], tail_v, fw_ss.at[0], fw_rs.at[0], (me, before))

    def late_copy(other, source):
        return remote(late_s, late_r.at[source], lt_ss.at[other], lt_rs.at[source], (other, mine))

    def back_copy(other, source):
        return remote(back_s, back_r.at[source], bc_ss.at[other], bc_rs.at[source], (other, before))

    stats = remote(sums_t.at[1], next_v, st_ss.at[0], st_rs.at[0], (me, jnp.maximum(mine - 2, 0)))
    further = odd & (mine > 1)

    pl.semaphore_wait(
        barrier,
        2 * count - 1 + jnp.where(has_before & even, count, 0)
        + jnp.where(has_after & odd, 1, 0) + jnp.where(further, count, 0))
    pl.when(has_before)(halos[0].start)

    @pl.when(has_before & odd)
    def _():
        for copy in halos[1:]:
            copy.start()

    pl.when(has_after & odd)(back.start)
    group(lambda dist: sums_copy(dist).start())
    for b in range(blocks - 1):
        group(lambda dist: guarded(ahead(dist), lambda: scatter_copy(b, dist).start()))
        packed(b + 1)

    @pl.when(even)
    def _():
        for copy in halos:
            copy.wait_recv()
        beside = across(data_v[:, pl.ds(snps - window, window)], halo_v[...])
        band = jnp.where(col >= row, main_s[blocks - 1, :, 1].reshape(window, window).astype(jnp.float32), beside)
        main_s[blocks - 1, :, 1] = band.astype(jnp.bfloat16).reshape(owners, per, window)

    group(lambda dist: guarded(ahead(dist), lambda: scatter_copy(blocks - 1, dist).start()))

    half = window // 2
    half_row, half_col = iotas(half, window)

    def fold(product):
        turned = pltpu.roll(product, half, 1)[:half]
        folded = jnp.where(half_col - half > half_row, product.T[half:], turned)
        return jnp.where(half_col < half, product[half:], folded).astype(jnp.bfloat16)

    def corner():
        halos[0].wait_recv()
        rows = pl.ds(0, split)
        late_s[...] = fold(across(data_v[rows, pl.ds(snps - window, window)], halo_v[rows, :]))
        everyone(lambda other: late_copy(other, me).start(), False)

    for copy in small[2:]:
        copy.wait()
    place(mine * snps, starts_v, ends_v, member_v, weights_v, placed_out)

    @pl.when(has_before & even)
    def _():
        back.wait_recv()
        back_s[...] = fold(across(back_v[...], data_v[pl.ds(split, samples - split), pl.ds(0, window)]))
        everyone(lambda other: back_copy(other, me).start(), None)

    def settle(s):
        sums_t[s] = collect(
            lambda dist: remote(
                sums_s, sums_r.at[s, dist], sm_ss.at[dist], sm_rs.at[s, dist],
                (ahead(dist), partner)).wait_recv(),
            sums_r.at[s], sums_s[...] if s == 0 else jnp.zeros_like(sums_s), 1 - s)
        cols_v[s] = square_of(sums_t[s]).T

    def own(s, b):
        def body():
            total = collect(
                lambda dist: remote(
                    main_s.at[b, 0], main_r.at[s, b, dist], ms_ss.at[b, dist], ms_rs.at[s, b, dist],
                    (ahead(dist), partner)).wait_recv(),
                main_r.at[s, b],
                main_s[b, me].astype(jnp.float32) if s == 0 else jnp.zeros(main_p.shape[2:], jnp.float32), 1 - s)
            row_of, col_of = iotas(per, window)
            row_of = row_of + me * per
            at = cols_v[s, pl.ds(pl.multiple_of(me * per, per), per), :][:, b:b + 1] * inverse
            scored = total[0] - at * sums_t[s, blocks:blocks + 1, :]
            main_p[s, b, 0] = pltpu.roll(scored, 1, 1).astype(main_p.dtype)
            other = sums_t[s, b + 1:b + 2, :] if b < blocks - 1 else sums_t[0, 0:1, :]
            mean_row = jnp.where(col_of >= row_of, sums_t[s, b:b + 1, :], other) * inverse
            value = total[1] * inverse - at * mean_row
            value = jnp.where(col_of == row_of, value, 2.0 * value)
            main_p[s, b, 1] = value.astype(main_p.dtype)
            if s == 1 and b == 0:
                pl.when(further)(lambda: peers(lambda dist: direct_copy(dist, me).start(), 0))
            everyone(lambda other: gather_copy(s, b, other, me, me).start(), None if s else False)
            if s == 0:
                main_g[b, me] = main_p[s, b]
        guarded(me, body)

    @pl.when(odd)
    def _():
        for s in range(2):
            settle(s)
        pl.when(further)(stats.start)
        for b in range(blocks - 1):
            own(1, b)
            own(0, b)
        own(0, blocks - 1)
        own(1, blocks - 1)
        pl.when(has_after)(corner)

    def gathered(b):
        everyone(lambda other: guarded(
            other, lambda: gather_copy(0, b, other, other, other).wait_recv()), even)
        near_out[b] = main_g[b]

    pl.when(has_before)(halos[0].wait_send)
    pl.when(has_before & even)(lambda: everyone(lambda other: back_copy(other, me).wait_send(), None))
    pl.when(has_after & odd)(back.wait_send)
    pl.when(has_after & odd)(lambda: everyone(lambda other: late_copy(other, me).wait_send(), False))
    group(lambda dist: sums_copy(dist).wait_send())
    for b in range(blocks):
        group(lambda dist: guarded(ahead(dist), lambda: scatter_copy(b, dist).wait_send()))

    @pl.when(odd)
    def _():
        for copy in halos[1:]:
            copy.wait_send()
        pl.when(further)(stats.wait_send)

        def sent():
            for b in range(blocks):
                for s in range(2):
                    everyone(lambda other: gather_copy(s, b, other, me, me).wait_send(), None if s else False)
            pl.when(further)(lambda: peers(lambda dist: direct_copy(dist, me).wait_send(), 0))
        guarded(me, sent)

    gathered(0)
    pl.when(odd)(forward.start)

    @pl.when(has_after & odd)
    def _():
        stats.wait_recv()
        folded = collect(
            lambda dist: late_copy(behind(dist), behind(dist)).wait_recv(), Behind(late_r),
            late_s[...].astype(jnp.float32))
        folded = collect(lambda other: back_copy(other, other).wait_recv(), back_r, folded, 0)
        mirrored = jnp.concatenate([folded, folded], axis=0).T
        product = jnp.concatenate([
            pltpu.roll(folded, half, 1), jnp.where(half_col < half, folded, mirrored[half:])], axis=0)
        mean_col = cols_v[0, :, blocks - 1:blocks] * inverse
        value = product * inverse - mean_col * (next_v[0:1, :] * inverse)
        corner_out[...] = jnp.where(col < row, 2.0 * value, 0.0).astype(corner_out.dtype)

    for b in range(1, blocks):
        gathered(b)

    @pl.when(has_after)
    def _():
        @pl.when(even)
        def _():
            beside = main_g[blocks - 1, :, 1].reshape(window, window).astype(jnp.float32)
            corner_out[...] = jnp.where(col < row, beside, 0.0).astype(corner_out.dtype)
            forward.wait_recv()

        pl.when(odd)(lambda: peers(lambda dist: guarded(
            behind(dist), lambda: direct_copy(dist, behind(dist)).wait_recv()), 0))
        far_out[...] = tail_v[...]

    @pl.when(jnp.logical_not(has_after))
    def _():
        corner_out[...] = jnp.zeros_like(corner_out)
        far_out[...] = jnp.zeros_like(far_out)

    pl.when(odd)(forward.wait_send)


def place(offset, starts, ends, member, weights, placed):
    tissues, genes, window = weights.shape
    blocks = placed.shape[0]
    per_block = genes // blocks
    gene_row, gene_col = iotas(genes, genes)

    def upright(row_ref):
        spread = jnp.broadcast_to(row_ref[...].astype(jnp.float32), (genes, genes))
        picked = jnp.where(gene_row == gene_col, spread, 0.0)
        return jnp.sum(picked, axis=1, keepdims=True).astype(jnp.int32)

    first, past = upright(starts), upright(ends)
    gene, lane = iotas(genes, window)
    inside = lane < past - first
    within = first - offset - (gene // per_block) * window
    owned = member[...]
    for t in range(tissues):
        kept = inside & (owned[:, t:t + 1] != 0)
        weights[t] = jnp.where(kept, weights[t].astype(jnp.float32), 0.0).astype(weights.dtype)
    near = lane >= within
    source = (lane - within) & (window - 1)
    for t in range(tissues):
        turned = jnp.take_along_axis(weights[t].astype(jnp.float32), source, axis=1)
        head = jnp.where(near, turned, 0.0).astype(placed.dtype)
        rest = jnp.where(near, 0.0, turned).astype(placed.dtype)
        rows = pl.ds(t * per_block, per_block)
        for b in range(blocks):
            genes_of = slice(b * per_block, (b + 1) * per_block)
            placed[b, rows, pl.ds(0, window)] = head[genes_of]
            placed[b, rows, pl.ds(window, window)] = rest[genes_of]


def reduced_sums(genotype, phenotype, residual, sign_flips, starts, ends, member, weights):
    samples, snps = genotype.shape
    tissues, genes, window = weights.shape
    count, ring = lax.axis_size("samp"), lax.axis_size("snp")
    blocks = snps // window
    per = share_of(window, count)
    owners = window // per
    kinds = -(-(blocks + 1) // 4) * 4
    half, wide = jnp.bfloat16, jnp.float32
    dma = pltpu.SemaphoreType.DMA
    vmem = pl.BlockSpec(memory_space=pltpu.VMEM)
    hbm = pl.BlockSpec(memory_space=pltpu.HBM)
    operands = (
        genotype, phenotype.reshape(-1, window), residual.reshape(-1, window), sign_flips,
        starts.reshape(1, genes), ends.reshape(1, genes), member, weights,
    )
    return pl.pallas_call(
        functools.partial(sums_kernel, count, ring, window),
        out_shape=(
            jax.ShapeDtypeStruct((blocks, owners, 2, per, window), half),
            jax.ShapeDtypeStruct((owners, 2, per, window), half),
            jax.ShapeDtypeStruct((window, window), half),
            jax.ShapeDtypeStruct((blocks, tissues * genes // blocks, 2 * window), half),
        ),
        in_specs=[hbm] * 8,
        out_specs=(vmem,) * 4,
        scratch_shapes=[pltpu.VMEM(x.shape, x.dtype) for x in operands[1:3] + operands[4:]] + [
            pltpu.VMEM((samples, snps + window), half),
            pltpu.VMEM(sign_flips.shape, jnp.int32),
            pltpu.VMEM((samples, window), half),
            pltpu.VMEM((samples - samples // HALVES, window), half),
            pltpu.VMEM((blocks, owners, 2, per, window), half),
            pltpu.VMEM((2, blocks, count, 2, per, window), half),
            pltpu.VMEM((2, blocks, 2, per, window), half),
            pltpu.VMEM((blocks, owners, 2, per, window), half),
            pltpu.VMEM((window // 2, window), half),
            pltpu.VMEM((count, window // 2, window), half),
            pltpu.VMEM((window // 2, window), half),
            pltpu.VMEM((count, window // 2, window), half),
            pltpu.VMEM((owners, 2, per, window), half),
            pltpu.VMEM((kinds, window), wide),
            pltpu.VMEM((2, count, kinds, window), wide),
            pltpu.VMEM((2, kinds, window), wide),
            pltpu.VMEM((2, window, window), wide),
            pltpu.VMEM((kinds, window), wide),
            dma((1,)), dma((PARTS,)), dma((6,)), dma((HALVES,)), dma((HALVES,)),
            dma((blocks, count)), dma((2, blocks, count)), dma((2, blocks, count)), dma((blocks, count)),
            dma((count,)), dma((count,)), dma((count,)), dma((count,)), dma((count,)), dma((count,)),
            dma((count,)), dma((2, count)), dma((1,)), dma((1,)), dma((1,)), dma((1,)), dma((1,)), dma((1,)),
        ],
        compiler_params=pltpu.CompilerParams(
            collective_id=0, has_side_effects=True, vmem_limit_bytes=VMEM_LIMIT),
        name="sums",
    )(*(pltpu.with_memory_space_constraint(x, pltpu.HBM) for x in operands))


def scores_kernel(sample_total, near, far, corner, placed, out_hbm, out, sem):
    tissues, genes, window = out.shape
    blocks = placed.shape[0]
    per_block = genes // blocks
    row, col = iotas(window, window)
    root = 1.0 / (sample_total ** 0.5)

    def piece(b, kind):
        ref = near.at[b] if b < blocks else far
        return ref[:, kind].reshape(window, window)

    def masked(keep, value):
        return jnp.where(keep, value.astype(jnp.float32), 0.0).astype(jnp.bfloat16)

    labelled = [piece(b, 0) for b in range(blocks + 1)]
    banded = [piece(b, 1) for b in range(blocks + 1)]
    diagonal = [masked(col >= row, band) for band in banded]
    beside = [masked(col < row, band) for band in banded[:blocks - 1]] + [corner[...]]
    nothing = jnp.zeros((window, window), jnp.bfloat16)
    pairs, bands = [], []
    for b in range(blocks):
        pairs.append(jnp.concatenate([labelled[b], labelled[b + 1]], axis=0))
        bands.append(jnp.concatenate([
            jnp.concatenate([diagonal[b], beside[b]], axis=1),
            jnp.concatenate([nothing, diagonal[b + 1]], axis=1),
        ], axis=0))

    copies = []
    step = next(n for n in range(min(7, tissues), 0, -1) if tissues % n == 0)
    for t in range(0, tissues, step):
        for b in range(blocks):
            half = placed[b, pl.ds(t * per_block, step * per_block), :]
            top = jnp.dot(half, pairs[b], preferred_element_type=jnp.float32)
            square = jnp.dot(half, bands[b], preferred_element_type=jnp.float32)
            variance = jnp.sum(square * half.astype(jnp.float32), axis=1, keepdims=True)
            scale = lax.rsqrt(jnp.maximum(variance, 0.0) + 1e-06) * root
            out[pl.ds(t, step), pl.ds(b * per_block, per_block), :] = (top * scale).reshape(step, per_block, window)
        part = pl.ds(t, step)
        copies.append(pltpu.make_async_copy(out.at[part], out_hbm.at[part], sem.at[t // step]))
        copies[-1].start()
    for copy in copies:
        copy.wait()


def on_device(genotype, phenotype, residual, sign_flips, weights, member, gene_start, gene_end):
    by_tissue = weights.transpose(1, 0, 2)
    near, far, corner, placed = reduced_sums(
        genotype, phenotype, residual, sign_flips, gene_start, gene_end, member, by_tissue)
    vmem = pl.BlockSpec(memory_space=pltpu.VMEM)
    scores = pl.pallas_call(
        functools.partial(scores_kernel, genotype.shape[0] * lax.axis_size("samp")),
        out_shape=jax.ShapeDtypeStruct(by_tissue.shape, jnp.float32),
        in_specs=[vmem] * 4,
        out_specs=pl.BlockSpec(memory_space=pltpu.HBM),
        scratch_shapes=[
            pltpu.VMEM(by_tissue.shape, jnp.float32),
            pltpu.SemaphoreType.DMA((by_tissue.shape[0],)),
        ],
        compiler_params=pltpu.CompilerParams(vmem_limit_bytes=VMEM_LIMIT),
        name="scores",
    )(near, far, corner, placed)
    return scores.transpose(1, 0, 2)


def solution(mesh):
    return jax.shard_map(
        on_device,
        mesh=mesh,
        in_specs=(
            P("samp", "snp"),
            P("samp"),
            P("samp"),
            P("samp", None),
            P("snp", None, None),
            P("snp", None),
            P("snp"),
            P("snp"),
        ),
        out_specs=P("snp", None, None),
        check_vma=False,
    )
```

```python
import functools

import jax
import jax.numpy as jnp
from jax import lax
from jax.experimental import pallas as pl
from jax.experimental.pallas import tpu as pltpu
from jax.sharding import PartitionSpec as P

MESH = pl.DeviceIdType.MESH
TILE = 16
PARTS = 2
HALVES = 2
VMEM_LIMIT = 24 * 1024 * 1024


def across(left, right):
    return lax.dot_general(left, right, (((0,), (0,)), ((), ())), preferred_element_type=jnp.float32)


def iotas(rows, cols):
    return (
        lax.broadcasted_iota(jnp.int32, (rows, cols), 0),
        lax.broadcasted_iota(jnp.int32, (rows, cols), 1),
    )


def share_of(rows, count):
    per = -(-rows // (count * TILE)) * TILE
    while rows % per:
        per += TILE
    return per


def square_of(rows):
    tiles, width = rows.shape
    return jnp.concatenate([rows, jnp.zeros((width - tiles, width), jnp.float32)], axis=0)


def sums_kernel(
    count, ring, window,
    geno, phen, resid, flips, starts, ends, member, weights,
    near_out, far_out, corner_out, placed_out,
    phen_v, resid_v, starts_v, ends_v, member_v, weights_v,
    data_v, flips_v, halo_v, back_v,
    main_s, main_r, main_p, main_g,
    late_s, late_r, back_s, back_r, tail_v,
    sums_s, sums_r, sums_t, cols_v, near_v, next_v,
    load_sem, flip_sem, small_sem, halo_ss, halo_rs,
    ms_ss, ms_rs, mg_ss, mg_rs, lt_ss, lt_rs, bc_ss, bc_rs, td_ss, td_rs,
    sm_ss, sm_rs, st_ss, st_rs, nr_ss, nr_rs, bk_ss, bk_rs, fw_ss, fw_rs,
):
    me = lax.axis_index("samp")
    mine = lax.axis_index("snp")
    parity = lax.rem(mine, 2)
    odd, even = parity == 1, parity == 0
    has_before, has_after = mine > 0, mine < ring - 1
    before = jnp.maximum(mine - 1, 0)
    after = jnp.minimum(mine + 1, ring - 1)
    beyond = jnp.minimum(mine + 2, ring - 1)
    partner = mine + 1 - 2 * parity
    samples = data_v.shape[0]
    blocks, owners, _, per, _ = main_g.shape
    snps = blocks * window
    part = samples // PARTS
    split = samples // HALVES
    inverse = 1.0 / (samples * count)

    def peers(body, first=1):
        if count <= 16:
            for dist in range(first, count):
                body(dist)
        else:
            def step(dist, carry):
                body(dist)
                return carry
            lax.fori_loop(first, count, step, 0)

    def collect(wait, got, total, first=1):
        if count <= 16:
            for dist in range(first, count):
                wait(dist)
                total += got[dist].astype(jnp.float32)
            return total

        def step(dist, total):
            wait(dist)
            return total + got[dist].astype(jnp.float32)
        return lax.fori_loop(first, count, step, total)

    def ahead(dist):
        return lax.rem(me + dist, count)

    def behind(dist):
        return lax.rem(me + count - dist, count)

    small = [
        pltpu.make_async_copy(src, dst, small_sem.at[i])
        for i, (src, dst) in enumerate((
            (resid, resid_v), (phen, phen_v), (starts, starts_v), (ends, ends_v),
            (member, member_v), (weights, weights_v),
        ))
    ]
    flip_loads = []
    for i in range(PARTS):
        rows = pl.ds(i * part, part)
        flip_loads.append(pltpu.make_async_copy(flips.at[rows], flips_v.at[rows], flip_sem.at[i]))
    for copy in small[:2] + flip_loads:
        copy.start()
    load = pltpu.make_async_copy(geno, data_v.at[:, pl.ds(0, snps)], load_sem.at[0])
    load.start()

    class Behind:
        def __init__(self, ref):
            self.ref = ref

        def __getitem__(self, dist):
            return self.ref[behind(dist)]

    barrier = pltpu.get_barrier_semaphore()

    def greet(dist, other):
        pl.semaphore_signal(barrier, inc=1, device_id=(ahead(dist), other), device_id_type=MESH)

    peers(lambda dist: greet(dist, partner), 0)
    pl.when(has_before & even)(lambda: greet(0, before))

    @pl.when(has_after & odd)
    def _():
        peers(lambda dist: greet(dist, mine))
        peers(lambda dist: greet(dist, after), 0)
        peers(lambda dist: greet(dist, beyond), 0)

    for copy in small[2:]:
        copy.start()

    for copy in small[:2]:
        copy.wait()
    phen_cols = square_of(phen_v[...]).T
    resid_cols = square_of(resid_v[...]).T
    lanes = phen_v.shape[1]
    for i in range(PARTS):
        flip_loads[i].wait()
        for t in range(i * part // lanes, (i + 1) * part // lanes):
            rows = pl.ds(t * lanes, lanes)
            signs = flips_v[rows, :].astype(jnp.float32)
            labels = jnp.concatenate([signs * resid_cols[:, t:t + 1], phen_cols[:, t:t + 1]], axis=1)
            data_v[rows, pl.ds(snps, window)] = labels.astype(jnp.bfloat16)

    load.wait()
    row, col = iotas(window, window)

    def packed(b):
        left = data_v[:, pl.ds(b * window, window)]
        if b == 0:
            left = jnp.concatenate([left, jnp.ones((samples, 8), jnp.bfloat16)], axis=1)
        products = across(left, data_v[:, pl.ds(b * window, snps + window - b * window)])
        other = products[:window, window:2 * window] if b < blocks - 1 else 0.0
        band = jnp.where(col >= row, products[:window, :window], other)
        scored = products[:window, snps - b * window:]
        main_s[b, :, 0] = scored.astype(jnp.bfloat16).reshape(owners, per, window)
        main_s[b, :, 1] = band.astype(jnp.bfloat16).reshape(owners, per, window)
        if b == 0:
            kinds = sums_s.shape[0]
            kind_of, _ = iotas(kinds, window)
            sums = jnp.zeros((kinds, window), jnp.float32)
            for at in range(blocks + 1):
                total = products[window:window + 1, at * window:(at + 1) * window]
                sums = jnp.where(kind_of == at, total, sums)
            sums_s[...] = sums

    packed(0)

    def remote(src, dst, ss, rs, device):
        return pltpu.make_async_remote_copy(
            src_ref=src, dst_ref=dst, send_sem=ss, recv_sem=rs,
            device_id=device, device_id_type=MESH)

    halos = []
    for i in range(HALVES):
        rows = pl.ds(i * split, split)
        halos.append(remote(
            geno.at[rows, pl.ds(0, window)], halo_v.at[rows],
            halo_ss.at[i], halo_rs.at[i], (me, before)))
    back = remote(
        geno.at[pl.ds(split, samples - split), pl.ds(snps - window, window)], back_v,
        bk_ss.at[0], bk_rs.at[0], (me, after))

    def guarded(index, body):
        if owners == count:
            body()
        else:
            pl.when(index < owners)(body)

    def sums_copy(dist):
        return remote(sums_s, sums_r.at[dist], sm_ss.at[dist], sm_rs.at[dist], (ahead(dist), partner))

    def scatter_copy(b, dist):
        return remote(
            main_s.at[b, ahead(dist)], main_r.at[b, dist],
            ms_ss.at[b, dist], ms_rs.at[b, dist], (ahead(dist), partner))

    def everyone(body, apart):
        def one(other):
            if apart is None:
                body(other)
            else:
                pl.when((other != me) | apart)(lambda: body(other))
        if count <= 16:
            for other in range(count):
                one(other)
        else:
            def step(other, carry):
                one(other)
                return carry
            lax.fori_loop(0, count, step, 0)

    def gather_copy(b, other, place, source):
        return remote(
            main_p.at[b], main_g.at[b, place], mg_ss.at[b, other], mg_rs.at[b, source], (other, partner))

    def direct_copy(dist, place):
        return remote(
            main_p.at[0], tail_v.at[place], td_ss.at[dist], td_rs.at[dist],
            (ahead(dist), jnp.maximum(mine - 2, 0)))

    forward = remote(main_g.at[0], tail_v, fw_ss.at[0], fw_rs.at[0], (me, before))

    def late_copy(other, source):
        return remote(late_s, late_r.at[source], lt_ss.at[other], lt_rs.at[source], (other, mine))

    def back_copy(other, source):
        return remote(back_s, back_r.at[source], bc_ss.at[other], bc_rs.at[source], (other, before))

    stats = remote(sums_t, next_v, st_ss.at[0], st_rs.at[0], (me, jnp.maximum(mine - 2, 0)))
    near = remote(sums_t, near_v, nr_ss.at[0], nr_rs.at[0], (me, partner))
    further = odd & (mine > 1)

    pl.semaphore_wait(
        barrier,
        count + jnp.where(has_before & even, count, 0)
        + jnp.where(has_after & odd, count, 0) + jnp.where(further, count, 0))
    pl.when(has_before)(halos[0].start)

    @pl.when(has_before & odd)
    def _():
        for copy in halos[1:]:
            copy.start()

    pl.when(has_after & odd)(back.start)
    peers(lambda dist: sums_copy(dist).start(), 0)
    for b in range(blocks - 1):
        peers(lambda dist: guarded(ahead(dist), lambda: scatter_copy(b, dist).start()), 0)
        packed(b + 1)

    @pl.when(even)
    def _():
        for copy in halos:
            copy.wait_recv()
        beside = across(data_v[:, pl.ds(snps - window, window)], halo_v[...])
        band = jnp.where(col >= row, main_s[blocks - 1, :, 1].reshape(window, window).astype(jnp.float32), beside)
        main_s[blocks - 1, :, 1] = band.astype(jnp.bfloat16).reshape(owners, per, window)

    peers(lambda dist: guarded(ahead(dist), lambda: scatter_copy(blocks - 1, dist).start()), 0)

    half = window // 2
    half_row, half_col = iotas(half, window)

    def fold(product):
        turned = pltpu.roll(product, half, 1)[:half]
        folded = jnp.where(half_col - half > half_row, product.T[half:], turned)
        return jnp.where(half_col < half, product[half:], folded).astype(jnp.bfloat16)

    def corner():
        halos[0].wait_recv()
        rows = pl.ds(0, split)
        late_s[...] = fold(across(data_v[rows, pl.ds(snps - window, window)], halo_v[rows, :]))
        everyone(lambda other: late_copy(other, me).start(), False)

    for copy in small[2:]:
        copy.wait()
    place(mine * snps, starts_v, ends_v, member_v, weights_v, placed_out)

    @pl.when(has_before & even)
    def _():
        back.wait_recv()
        back_s[...] = fold(across(back_v[...], data_v[pl.ds(split, samples - split), pl.ds(0, window)]))
        everyone(lambda other: back_copy(other, me).start(), None)

    sums_t[...] = collect(
        lambda dist: sums_copy(dist).wait_recv(), sums_r, jnp.zeros(sums_t.shape, jnp.float32), 0)
    cols_v[...] = square_of(sums_t[...]).T
    pl.when(even)(near.start)
    pl.when(further)(stats.start)

    def own(b):
        def body():
            total = collect(
                lambda dist: scatter_copy(b, dist).wait_recv(), main_r.at[b],
                jnp.zeros(main_p.shape[1:], jnp.float32), 0)
            row_of, col_of = iotas(per, window)
            row_of = row_of + me * per
            at = cols_v[pl.ds(pl.multiple_of(me * per, per), per), :][:, b:b + 1] * inverse
            scored = total[0] - at * sums_t[blocks:blocks + 1, :]
            main_p[b, 0] = pltpu.roll(scored, 1, 1).astype(main_p.dtype)
            other = sums_t[b + 1:b + 2, :] if b < blocks - 1 else near_v[0:1, :]
            mean_row = jnp.where(col_of >= row_of, sums_t[b:b + 1, :], other) * inverse
            value = total[1] * inverse - at * mean_row
            value = jnp.where(col_of == row_of, value, 2.0 * value)
            main_p[b, 1] = value.astype(main_p.dtype)
            if b == 0:
                pl.when(further)(lambda: peers(lambda dist: direct_copy(dist, me).start(), 0))
            everyone(lambda other: gather_copy(b, other, me, me).start(), None)
        guarded(me, body)

    for b in range(blocks - 1):
        own(b)
    pl.when(has_after & odd)(corner)

    @pl.when(odd)
    def _():
        near.wait_recv()

    @pl.when(even)
    def _():
        near_v[...] = jnp.zeros_like(near_v)

    own(blocks - 1)

    def gathered(b):
        everyone(lambda other: guarded(
            other, lambda: gather_copy(b, other, other, other).wait_recv()), None)
        near_out[b] = main_g[b]

    pl.when(has_before)(halos[0].wait_send)
    pl.when(has_before & even)(lambda: everyone(lambda other: back_copy(other, me).wait_send(), None))
    pl.when(has_after & odd)(back.wait_send)
    pl.when(has_after & odd)(lambda: everyone(lambda other: late_copy(other, me).wait_send(), False))
    peers(lambda dist: sums_copy(dist).wait_send(), 0)
    for b in range(blocks):
        peers(lambda dist: guarded(ahead(dist), lambda: scatter_copy(b, dist).wait_send()), 0)

    @pl.when(odd)
    def _():
        for copy in halos[1:]:
            copy.wait_send()
        pl.when(further)(stats.wait_send)

    pl.when(even)(near.wait_send)

    def sent():
        for b in range(blocks):
            everyone(lambda other: gather_copy(b, other, me, me).wait_send(), None)
        pl.when(further)(lambda: peers(lambda dist: direct_copy(dist, me).wait_send(), 0))
    guarded(me, sent)

    gathered(0)
    pl.when(odd)(forward.start)

    @pl.when(has_after & odd)
    def _():
        stats.wait_recv()
        folded = collect(
            lambda dist: late_copy(behind(dist), behind(dist)).wait_recv(), Behind(late_r),
            late_s[...].astype(jnp.float32))
        folded = collect(lambda other: back_copy(other, other).wait_recv(), back_r, folded, 0)
        mirrored = jnp.concatenate([folded, folded], axis=0).T
        product = jnp.concatenate([
            pltpu.roll(folded, half, 1), jnp.where(half_col < half, folded, mirrored[half:])], axis=0)
        mean_col = square_of(near_v[...]).T[:, blocks - 1:blocks] * inverse
        value = product * inverse - mean_col * (next_v[0:1, :] * inverse)
        corner_out[...] = jnp.where(col < row, 2.0 * value, 0.0).astype(corner_out.dtype)

    for b in range(1, blocks):
        gathered(b)

    @pl.when(has_after)
    def _():
        @pl.when(even)
        def _():
            beside = main_g[blocks - 1, :, 1].reshape(window, window).astype(jnp.float32)
            corner_out[...] = jnp.where(col < row, beside, 0.0).astype(corner_out.dtype)
            forward.wait_recv()

        pl.when(odd)(lambda: peers(lambda dist: guarded(
            behind(dist), lambda: direct_copy(dist, behind(dist)).wait_recv()), 0))
        far_out[...] = tail_v[...]

    @pl.when(jnp.logical_not(has_after))
    def _():
        corner_out[...] = jnp.zeros_like(corner_out)
        far_out[...] = jnp.zeros_like(far_out)

    pl.when(odd)(forward.wait_send)


def place(offset, starts, ends, member, weights, placed):
    tissues, genes, window = weights.shape
    blocks = placed.shape[0]
    per_block = genes // blocks
    gene_row, gene_col = iotas(genes, genes)

    def upright(row_ref):
        spread = jnp.broadcast_to(row_ref[...].astype(jnp.float32), (genes, genes))
        picked = jnp.where(gene_row == gene_col, spread, 0.0)
        return jnp.sum(picked, axis=1, keepdims=True).astype(jnp.int32)

    first, past = upright(starts), upright(ends)
    gene, lane = iotas(genes, window)
    inside = lane < past - first
    within = first - offset - (gene // per_block) * window
    owned = member[...]
    for t in range(tissues):
        kept = inside & (owned[:, t:t + 1] != 0)
        weights[t] = jnp.where(kept, weights[t].astype(jnp.float32), 0.0).astype(weights.dtype)
    near = lane >= within
    source = (lane - within) & (window - 1)
    for t in range(tissues):
        turned = jnp.take_along_axis(weights[t].astype(jnp.float32), source, axis=1)
        head = jnp.where(near, turned, 0.0).astype(placed.dtype)
        rest = jnp.where(near, 0.0, turned).astype(placed.dtype)
        rows = pl.ds(t * per_block, per_block)
        for b in range(blocks):
            genes_of = slice(b * per_block, (b + 1) * per_block)
            placed[b, rows, pl.ds(0, window)] = head[genes_of]
            placed[b, rows, pl.ds(window, window)] = rest[genes_of]


def reduced_sums(genotype, phenotype, residual, sign_flips, starts, ends, member, weights):
    samples, snps = genotype.shape
    tissues, genes, window = weights.shape
    count, ring = lax.axis_size("samp"), lax.axis_size("snp")
    blocks = snps // window
    per = share_of(window, count)
    owners = window // per
    kinds = -(-(blocks + 1) // 4) * 4
    half, wide = jnp.bfloat16, jnp.float32
    dma = pltpu.SemaphoreType.DMA
    vmem = pl.BlockSpec(memory_space=pltpu.VMEM)
    hbm = pl.BlockSpec(memory_space=pltpu.HBM)
    operands = (
        genotype, phenotype.reshape(-1, window), residual.reshape(-1, window), sign_flips,
        starts.reshape(1, genes), ends.reshape(1, genes), member, weights,
    )
    return pl.pallas_call(
        functools.partial(sums_kernel, count, ring, window),
        out_shape=(
            jax.ShapeDtypeStruct((blocks, owners, 2, per, window), half),
            jax.ShapeDtypeStruct((owners, 2, per, window), half),
            jax.ShapeDtypeStruct((window, window), half),
            jax.ShapeDtypeStruct((blocks, tissues * genes // blocks, 2 * window), half),
        ),
        in_specs=[hbm] * 8,
        out_specs=(vmem,) * 4,
        scratch_shapes=[pltpu.VMEM(x.shape, x.dtype) for x in operands[1:3] + operands[4:]] + [
            pltpu.VMEM((samples, snps + window), half),
            pltpu.VMEM(sign_flips.shape, jnp.int32),
            pltpu.VMEM((samples, window), half),
            pltpu.VMEM((samples - samples // HALVES, window), half),
            pltpu.VMEM((blocks, owners, 2, per, window), half),
            pltpu.VMEM((blocks, count, 2, per, window), half),
            pltpu.VMEM((blocks, 2, per, window), half),
            pltpu.VMEM((blocks, owners, 2, per, window), half),
            pltpu.VMEM((window // 2, window), half),
            pltpu.VMEM((count, window // 2, window), half),
            pltpu.VMEM((window // 2, window), half),
            pltpu.VMEM((count, window // 2, window), half),
            pltpu.VMEM((owners, 2, per, window), half),
            pltpu.VMEM((kinds, window), wide),
            pltpu.VMEM((count, kinds, window), wide),
            pltpu.VMEM((kinds, window), wide),
            pltpu.VMEM((window, window), wide),
            pltpu.VMEM((kinds, window), wide),
            pltpu.VMEM((kinds, window), wide),
            dma((1,)), dma((PARTS,)), dma((6,)), dma((HALVES,)), dma((HALVES,)),
            dma((blocks, count)), dma((blocks, count)), dma((blocks, count)), dma((blocks, count)),
            dma((count,)), dma((count,)), dma((count,)), dma((count,)), dma((count,)), dma((count,)),
            dma((count,)), dma((count,)), dma((1,)), dma((1,)), dma((1,)), dma((1,)),
            dma((1,)), dma((1,)), dma((1,)), dma((1,)),
        ],
        compiler_params=pltpu.CompilerParams(
            collective_id=0, has_side_effects=True, vmem_limit_bytes=VMEM_LIMIT),
        name="sums",
    )(*(pltpu.with_memory_space_constraint(x, pltpu.HBM) for x in operands))


def scores_kernel(sample_total, near, far, corner, placed, out_hbm, out, sem):
    tissues, genes, window = out.shape
    blocks = placed.shape[0]
    per_block = genes // blocks
    row, col = iotas(window, window)
    root = 1.0 / (sample_total ** 0.5)

    def piece(b, kind):
        ref = near.at[b] if b < blocks else far
        return ref[:, kind].reshape(window, window)

    def masked(keep, value):
        return jnp.where(keep, value.astype(jnp.float32), 0.0).astype(jnp.bfloat16)

    labelled = [piece(b, 0) for b in range(blocks + 1)]
    banded = [piece(b, 1) for b in range(blocks + 1)]
    diagonal = [masked(col >= row, band) for band in banded]
    beside = [masked(col < row, band) for band in banded[:blocks - 1]] + [corner[...]]
    nothing = jnp.zeros((window, window), jnp.bfloat16)
    pairs, bands = [], []
    for b in range(blocks):
        pairs.append(jnp.concatenate([labelled[b], labelled[b + 1]], axis=0))
        bands.append(jnp.concatenate([
            jnp.concatenate([diagonal[b], beside[b]], axis=1),
            jnp.concatenate([nothing, diagonal[b + 1]], axis=1),
        ], axis=0))

    copies = []
    step = next(n for n in range(min(7, tissues), 0, -1) if tissues % n == 0)
    for t in range(0, tissues, step):
        for b in range(blocks):
            half = placed[b, pl.ds(t * per_block, step * per_block), :]
            top = jnp.dot(half, pairs[b], preferred_element_type=jnp.float32)
            square = jnp.dot(half, bands[b], preferred_element_type=jnp.float32)
            variance = jnp.sum(square * half.astype(jnp.float32), axis=1, keepdims=True)
            scale = lax.rsqrt(jnp.maximum(variance, 0.0) + 1e-06) * root
            out[pl.ds(t, step), pl.ds(b * per_block, per_block), :] = (top * scale).reshape(step, per_block, window)
        part = pl.ds(t, step)
        copies.append(pltpu.make_async_copy(out.at[part], out_hbm.at[part], sem.at[t // step]))
        copies[-1].start()
    for copy in copies:
        copy.wait()


def on_device(genotype, phenotype, residual, sign_flips, weights, member, gene_start, gene_end):
    by_tissue = weights.transpose(1, 0, 2)
    near, far, corner, placed = reduced_sums(
        genotype, phenotype, residual, sign_flips, gene_start, gene_end, member, by_tissue)
    vmem = pl.BlockSpec(memory_space=pltpu.VMEM)
    scores = pl.pallas_call(
        functools.partial(scores_kernel, genotype.shape[0] * lax.axis_size("samp")),
        out_shape=jax.ShapeDtypeStruct(by_tissue.shape, jnp.float32),
        in_specs=[vmem] * 4,
        out_specs=pl.BlockSpec(memory_space=pltpu.HBM),
        scratch_shapes=[
            pltpu.VMEM(by_tissue.shape, jnp.float32),
            pltpu.SemaphoreType.DMA((by_tissue.shape[0],)),
        ],
        compiler_params=pltpu.CompilerParams(vmem_limit_bytes=VMEM_LIMIT),
        name="scores",
    )(near, far, corner, placed)
    return scores.transpose(1, 0, 2)


def solution(mesh):
    return jax.shard_map(
        on_device,
        mesh=mesh,
        in_specs=(
            P("samp", "snp"),
            P("samp"),
            P("samp"),
            P("samp", None),
            P("snp", None, None),
            P("snp", None),
            P("snp"),
            P("snp"),
        ),
        out_specs=P("snp", None, None),
        check_vma=False,
    )
```

```python
import functools

import jax
import jax.numpy as jnp
from jax import lax
from jax.experimental import pallas as pl
from jax.experimental.pallas import tpu as pltpu
from jax.sharding import PartitionSpec as P

MESH = pl.DeviceIdType.MESH
TILE = 16
PARTS = 2
HALVES = 2
VMEM_LIMIT = 24 * 1024 * 1024


def across(left, right):
    return lax.dot_general(left, right, (((0,), (0,)), ((), ())), preferred_element_type=jnp.float32)


def iotas(rows, cols):
    return (
        lax.broadcasted_iota(jnp.int32, (rows, cols), 0),
        lax.broadcasted_iota(jnp.int32, (rows, cols), 1),
    )


def share_of(rows, count):
    per = -(-rows // (count * TILE)) * TILE
    while rows % per:
        per += TILE
    return per


def square_of(rows):
    tiles, width = rows.shape
    return jnp.concatenate([rows, jnp.zeros((width - tiles, width), jnp.float32)], axis=0)


def sums_kernel(
    count, ring, window,
    geno, phen, resid, flips, starts, ends, member, weights,
    near_out, far_out, corner_out, placed_out,
    phen_v, resid_v, starts_v, ends_v, member_v, weights_v,
    data_v, flips_v, halo_v, back_v,
    main_s, main_r, main_p, main_g,
    late_s, late_r, back_s, back_r, tail_v,
    sums_s, sums_r, sums_t, cols_v, near_v, next_v,
    load_sem, flip_sem, small_sem, halo_ss, halo_rs,
    ms_ss, ms_rs, mg_ss, mg_rs, lt_ss, lt_rs, bc_ss, bc_rs, td_ss, td_rs,
    sm_ss, sm_rs, st_ss, st_rs, nr_ss, nr_rs, bk_ss, bk_rs, fw_ss, fw_rs,
):
    me = lax.axis_index("samp")
    mine = lax.axis_index("snp")
    parity = lax.rem(mine, 2)
    odd, even = parity == 1, parity == 0
    has_before, has_after = mine > 0, mine < ring - 1
    before = jnp.maximum(mine - 1, 0)
    after = jnp.minimum(mine + 1, ring - 1)
    beyond = jnp.minimum(mine + 2, ring - 1)
    partner = mine + 1 - 2 * parity
    samples = data_v.shape[0]
    blocks, owners, _, per, _ = main_g.shape
    snps = blocks * window
    part = samples // PARTS
    split = samples // HALVES
    inverse = 1.0 / (samples * count)

    def peers(body, first=1):
        if count <= 16:
            for dist in range(first, count):
                body(dist)
        else:
            def step(dist, carry):
                body(dist)
                return carry
            lax.fori_loop(first, count, step, 0)

    def collect(wait, got, total, first=1):
        if count <= 16:
            for dist in range(first, count):
                wait(dist)
                total += got[dist].astype(jnp.float32)
            return total

        def step(dist, total):
            wait(dist)
            return total + got[dist].astype(jnp.float32)
        return lax.fori_loop(first, count, step, total)

    def ahead(dist):
        return lax.rem(me + dist, count)

    def behind(dist):
        return lax.rem(me + count - dist, count)

    small = [
        pltpu.make_async_copy(src, dst, small_sem.at[i])
        for i, (src, dst) in enumerate((
            (resid, resid_v), (phen, phen_v), (starts, starts_v), (ends, ends_v),
            (member, member_v), (weights, weights_v),
        ))
    ]
    flip_loads = []
    for i in range(PARTS):
        rows = pl.ds(i * part, part)
        flip_loads.append(pltpu.make_async_copy(flips.at[rows], flips_v.at[rows], flip_sem.at[i]))
    for copy in small[:2] + flip_loads:
        copy.start()
    load = pltpu.make_async_copy(geno, data_v.at[:, pl.ds(0, snps)], load_sem.at[0])
    load.start()

    class Behind:
        def __init__(self, ref):
            self.ref = ref

        def __getitem__(self, dist):
            return self.ref[behind(dist)]

    barrier = pltpu.get_barrier_semaphore()

    def greet(dist, other):
        pl.semaphore_signal(barrier, inc=1, device_id=(ahead(dist), other), device_id_type=MESH)

    peers(lambda dist: greet(dist, partner), 0)
    pl.when(has_before & even)(lambda: greet(0, before))

    @pl.when(has_after & odd)
    def _():
        peers(lambda dist: greet(dist, mine))
        peers(lambda dist: greet(dist, after), 0)
        peers(lambda dist: greet(dist, beyond), 0)

    for copy in small[2:]:
        copy.start()

    for copy in small[:2]:
        copy.wait()
    phen_cols = square_of(phen_v[...]).T
    resid_cols = square_of(resid_v[...]).T
    lanes = phen_v.shape[1]
    for i in range(PARTS):
        flip_loads[i].wait()
        for t in range(i * part // lanes, (i + 1) * part // lanes):
            rows = pl.ds(t * lanes, lanes)
            signs = flips_v[rows, :].astype(jnp.float32)
            labels = jnp.concatenate([signs * resid_cols[:, t:t + 1], phen_cols[:, t:t + 1]], axis=1)
            data_v[rows, pl.ds(snps, window)] = labels.astype(jnp.bfloat16)

    load.wait()
    row, col = iotas(window, window)

    def packed(b):
        left = data_v[:, pl.ds(b * window, window)]
        if b == 0:
            left = jnp.concatenate([left, jnp.ones((samples, 8), jnp.bfloat16)], axis=1)
        products = across(left, data_v[:, pl.ds(b * window, snps + window - b * window)])
        other = products[:window, window:2 * window] if b < blocks - 1 else 0.0
        band = jnp.where(col >= row, products[:window, :window], other)
        scored = products[:window, snps - b * window:]
        main_s[b, :, 0] = scored.astype(jnp.bfloat16).reshape(owners, per, window)
        main_s[b, :, 1] = band.astype(jnp.bfloat16).reshape(owners, per, window)
        if b == 0:
            kinds = sums_s.shape[0]
            kind_of, _ = iotas(kinds, window)
            sums = jnp.zeros((kinds, window), jnp.float32)
            for at in range(blocks + 1):
                total = products[window:window + 1, at * window:(at + 1) * window]
                sums = jnp.where(kind_of == at, total, sums)
            sums_s[...] = sums

    packed(0)

    def remote(src, dst, ss, rs, device):
        return pltpu.make_async_remote_copy(
            src_ref=src, dst_ref=dst, send_sem=ss, recv_sem=rs,
            device_id=device, device_id_type=MESH)

    halos = []
    for i in range(HALVES):
        rows = pl.ds(i * split, split)
        halos.append(remote(
            geno.at[rows, pl.ds(0, window)], halo_v.at[rows],
            halo_ss.at[i], halo_rs.at[i], (me, before)))
    back = remote(
        geno.at[pl.ds(split, samples - split), pl.ds(snps - window, window)], back_v,
        bk_ss.at[0], bk_rs.at[0], (me, after))

    def guarded(index, body):
        if owners == count:
            body()
        else:
            pl.when(index < owners)(body)

    def sums_copy(dist):
        return remote(sums_s, sums_r.at[dist], sm_ss.at[dist], sm_rs.at[dist], (ahead(dist), partner))

    def scatter_copy(b, dist):
        return remote(
            main_s.at[b, ahead(dist)], main_r.at[b, dist],
            ms_ss.at[b, dist], ms_rs.at[b, dist], (ahead(dist), partner))

    def everyone(body, apart, low=0, high=count):
        def one(other):
            if apart is None:
                body(other)
            else:
                pl.when((other != me) | apart)(lambda: body(other))
        if count <= 16:
            for other in range(low, high):
                one(other)
        else:
            def step(other, carry):
                one(other)
                return carry
            lax.fori_loop(low, high, step, 0)

    def gather_copy(b, other, place, source):
        return remote(
            main_p.at[b], main_g.at[b, place], mg_ss.at[b, other], mg_rs.at[b, source], (other, partner))

    def direct_copy(dist, place):
        return remote(
            main_p.at[0], tail_v.at[place], td_ss.at[dist], td_rs.at[dist],
            (ahead(dist), jnp.maximum(mine - 2, 0)))

    forward = remote(main_g.at[0], tail_v, fw_ss.at[0], fw_rs.at[0], (me, before))

    def late_copy(other, source):
        return remote(late_s, late_r.at[source], lt_ss.at[other], lt_rs.at[source], (other, mine))

    def back_copy(other, source):
        return remote(back_s, back_r.at[source], bc_ss.at[other], bc_rs.at[source], (other, before))

    stats = remote(sums_t, next_v, st_ss.at[0], st_rs.at[0], (me, jnp.maximum(mine - 2, 0)))
    near = remote(sums_t, near_v, nr_ss.at[0], nr_rs.at[0], (me, partner))
    further = odd & (mine > 1)

    pl.semaphore_wait(
        barrier,
        count + jnp.where(has_before & even, count, 0)
        + jnp.where(has_after & odd, count, 0) + jnp.where(further, count, 0))
    pl.when(has_before)(halos[0].start)

    @pl.when(has_before & odd)
    def _():
        for copy in halos[1:]:
            copy.start()

    pl.when(has_after & odd)(back.start)
    peers(lambda dist: sums_copy(dist).start(), 0)
    for b in range(blocks - 1):
        peers(lambda dist: guarded(ahead(dist), lambda: scatter_copy(b, dist).start()), 0)
        packed(b + 1)

    @pl.when(even)
    def _():
        for copy in halos:
            copy.wait_recv()
        beside = across(data_v[:, pl.ds(snps - window, window)], halo_v[...])
        band = jnp.where(col >= row, main_s[blocks - 1, :, 1].reshape(window, window).astype(jnp.float32), beside)
        main_s[blocks - 1, :, 1] = band.astype(jnp.bfloat16).reshape(owners, per, window)

    peers(lambda dist: guarded(ahead(dist), lambda: scatter_copy(blocks - 1, dist).start()), 0)

    soon = max(1, count // 8)
    half = window // 2
    half_row, half_col = iotas(half, window)

    def fold(product):
        turned = pltpu.roll(product, half, 1)[:half]
        folded = jnp.where(half_col - half > half_row, product.T[half:], turned)
        return jnp.where(half_col < half, product[half:], folded).astype(jnp.bfloat16)

    def corner():
        halos[0].wait_recv()
        rows = pl.ds(0, split)
        late_s[...] = fold(across(data_v[rows, pl.ds(snps - window, window)], halo_v[rows, :]))
        everyone(lambda other: late_copy(other, me).start(), False, 0, soon)

    for copy in small[2:]:
        copy.wait()
    place(mine * snps, starts_v, ends_v, member_v, weights_v, placed_out)

    @pl.when(has_before & even)
    def _():
        back.wait_recv()
        back_s[...] = fold(across(back_v[...], data_v[pl.ds(split, samples - split), pl.ds(0, window)]))
        everyone(lambda other: back_copy(other, me).start(), None)

    sums_t[...] = collect(
        lambda dist: sums_copy(dist).wait_recv(), sums_r, jnp.zeros(sums_t.shape, jnp.float32), 0)
    cols_v[...] = square_of(sums_t[...]).T
    pl.when(even)(near.start)
    pl.when(further)(stats.start)

    def own(b):
        def body():
            total = collect(
                lambda dist: scatter_copy(b, dist).wait_recv(), main_r.at[b],
                jnp.zeros(main_p.shape[1:], jnp.float32), 0)
            row_of, col_of = iotas(per, window)
            row_of = row_of + me * per
            at = cols_v[pl.ds(pl.multiple_of(me * per, per), per), :][:, b:b + 1] * inverse
            scored = total[0] - at * sums_t[blocks:blocks + 1, :]
            main_p[b, 0] = pltpu.roll(scored, 1, 1).astype(main_p.dtype)
            other = sums_t[b + 1:b + 2, :] if b < blocks - 1 else near_v[0:1, :]
            mean_row = jnp.where(col_of >= row_of, sums_t[b:b + 1, :], other) * inverse
            value = total[1] * inverse - at * mean_row
            value = jnp.where(col_of == row_of, value, 2.0 * value)
            main_p[b, 1] = value.astype(main_p.dtype)
            if b == 0:
                pl.when(further)(lambda: peers(lambda dist: direct_copy(dist, me).start(), 0))
            everyone(lambda other: gather_copy(b, other, me, me).start(), None)
        guarded(me, body)

    for b in range(blocks - 1):
        own(b)
    pl.when(has_after & odd)(corner)

    @pl.when(odd)
    def _():
        near.wait_recv()

    @pl.when(even)
    def _():
        near_v[...] = jnp.zeros_like(near_v)

    own(blocks - 1)
    pl.when(has_after & odd)(lambda: everyone(lambda other: late_copy(other, me).start(), False, soon))

    def gathered(b):
        everyone(lambda other: guarded(
            other, lambda: gather_copy(b, other, other, other).wait_recv()), None)
        near_out[b] = main_g[b]

    pl.when(has_before)(halos[0].wait_send)
    pl.when(has_before & even)(lambda: everyone(lambda other: back_copy(other, me).wait_send(), None))
    pl.when(has_after & odd)(back.wait_send)
    pl.when(has_after & odd)(lambda: everyone(lambda other: late_copy(other, me).wait_send(), False))
    peers(lambda dist: sums_copy(dist).wait_send(), 0)
    for b in range(blocks):
        peers(lambda dist: guarded(ahead(dist), lambda: scatter_copy(b, dist).wait_send()), 0)

    @pl.when(odd)
    def _():
        for copy in halos[1:]:
            copy.wait_send()
        pl.when(further)(stats.wait_send)

    pl.when(even)(near.wait_send)

    def sent():
        for b in range(blocks):
            everyone(lambda other: gather_copy(b, other, me, me).wait_send(), None)
        pl.when(further)(lambda: peers(lambda dist: direct_copy(dist, me).wait_send(), 0))
    guarded(me, sent)

    gathered(0)
    pl.when(odd)(forward.start)

    @pl.when(has_after & odd)
    def _():
        stats.wait_recv()
        folded = collect(
            lambda dist: late_copy(behind(dist), behind(dist)).wait_recv(), Behind(late_r),
            late_s[...].astype(jnp.float32))
        folded = collect(lambda other: back_copy(other, other).wait_recv(), back_r, folded, 0)
        mirrored = jnp.concatenate([folded, folded], axis=0).T
        product = jnp.concatenate([
            pltpu.roll(folded, half, 1), jnp.where(half_col < half, folded, mirrored[half:])], axis=0)
        mean_col = square_of(near_v[...]).T[:, blocks - 1:blocks] * inverse
        value = product * inverse - mean_col * (next_v[0:1, :] * inverse)
        corner_out[...] = jnp.where(col < row, 2.0 * value, 0.0).astype(corner_out.dtype)

    for b in range(1, blocks):
        gathered(b)

    @pl.when(has_after)
    def _():
        @pl.when(even)
        def _():
            beside = main_g[blocks - 1, :, 1].reshape(window, window).astype(jnp.float32)
            corner_out[...] = jnp.where(col < row, beside, 0.0).astype(corner_out.dtype)
            forward.wait_recv()

        pl.when(odd)(lambda: peers(lambda dist: guarded(
            behind(dist), lambda: direct_copy(dist, behind(dist)).wait_recv()), 0))
        far_out[...] = tail_v[...]

    @pl.when(jnp.logical_not(has_after))
    def _():
        corner_out[...] = jnp.zeros_like(corner_out)
        far_out[...] = jnp.zeros_like(far_out)

    pl.when(odd)(forward.wait_send)


def place(offset, starts, ends, member, weights, placed):
    tissues, genes, window = weights.shape
    blocks = placed.shape[0]
    per_block = genes // blocks
    gene_row, gene_col = iotas(genes, genes)

    def upright(row_ref):
        spread = jnp.broadcast_to(row_ref[...].astype(jnp.float32), (genes, genes))
        picked = jnp.where(gene_row == gene_col, spread, 0.0)
        return jnp.sum(picked, axis=1, keepdims=True).astype(jnp.int32)

    first, past = upright(starts), upright(ends)
    gene, lane = iotas(genes, window)
    inside = lane < past - first
    within = first - offset - (gene // per_block) * window
    owned = member[...]
    for t in range(tissues):
        kept = inside & (owned[:, t:t + 1] != 0)
        weights[t] = jnp.where(kept, weights[t].astype(jnp.float32), 0.0).astype(weights.dtype)
    near = lane >= within
    source = (lane - within) & (window - 1)
    for t in range(tissues):
        turned = jnp.take_along_axis(weights[t].astype(jnp.float32), source, axis=1)
        head = jnp.where(near, turned, 0.0).astype(placed.dtype)
        rest = jnp.where(near, 0.0, turned).astype(placed.dtype)
        rows = pl.ds(t * per_block, per_block)
        for b in range(blocks):
            genes_of = slice(b * per_block, (b + 1) * per_block)
            placed[b, rows, pl.ds(0, window)] = head[genes_of]
            placed[b, rows, pl.ds(window, window)] = rest[genes_of]


def reduced_sums(genotype, phenotype, residual, sign_flips, starts, ends, member, weights):
    samples, snps = genotype.shape
    tissues, genes, window = weights.shape
    count, ring = lax.axis_size("samp"), lax.axis_size("snp")
    blocks = snps // window
    per = share_of(window, count)
    owners = window // per
    kinds = -(-(blocks + 1) // 4) * 4
    half, wide = jnp.bfloat16, jnp.float32
    dma = pltpu.SemaphoreType.DMA
    vmem = pl.BlockSpec(memory_space=pltpu.VMEM)
    hbm = pl.BlockSpec(memory_space=pltpu.HBM)
    operands = (
        genotype, phenotype.reshape(-1, window), residual.reshape(-1, window), sign_flips,
        starts.reshape(1, genes), ends.reshape(1, genes), member, weights,
    )
    return pl.pallas_call(
        functools.partial(sums_kernel, count, ring, window),
        out_shape=(
            jax.ShapeDtypeStruct((blocks, owners, 2, per, window), half),
            jax.ShapeDtypeStruct((owners, 2, per, window), half),
            jax.ShapeDtypeStruct((window, window), half),
            jax.ShapeDtypeStruct((blocks, tissues * genes // blocks, 2 * window), half),
        ),
        in_specs=[hbm] * 8,
        out_specs=(vmem,) * 4,
        scratch_shapes=[pltpu.VMEM(x.shape, x.dtype) for x in operands[1:3] + operands[4:]] + [
            pltpu.VMEM((samples, snps + window), half),
            pltpu.VMEM(sign_flips.shape, jnp.int32),
            pltpu.VMEM((samples, window), half),
            pltpu.VMEM((samples - samples // HALVES, window), half),
            pltpu.VMEM((blocks, owners, 2, per, window), half),
            pltpu.VMEM((blocks, count, 2, per, window), half),
            pltpu.VMEM((blocks, 2, per, window), half),
            pltpu.VMEM((blocks, owners, 2, per, window), half),
            pltpu.VMEM((window // 2, window), half),
            pltpu.VMEM((count, window // 2, window), half),
            pltpu.VMEM((window // 2, window), half),
            pltpu.VMEM((count, window // 2, window), half),
            pltpu.VMEM((owners, 2, per, window), half),
            pltpu.VMEM((kinds, window), wide),
            pltpu.VMEM((count, kinds, window), wide),
            pltpu.VMEM((kinds, window), wide),
            pltpu.VMEM((window, window), wide),
            pltpu.VMEM((kinds, window), wide),
            pltpu.VMEM((kinds, window), wide),
            dma((1,)), dma((PARTS,)), dma((6,)), dma((HALVES,)), dma((HALVES,)),
            dma((blocks, count)), dma((blocks, count)), dma((blocks, count)), dma((blocks, count)),
            dma((count,)), dma((count,)), dma((count,)), dma((count,)), dma((count,)), dma((count,)),
            dma((count,)), dma((count,)), dma((1,)), dma((1,)), dma((1,)), dma((1,)),
            dma((1,)), dma((1,)), dma((1,)), dma((1,)),
        ],
        compiler_params=pltpu.CompilerParams(
            collective_id=0, has_side_effects=True, vmem_limit_bytes=VMEM_LIMIT),
        name="sums",
    )(*(pltpu.with_memory_space_constraint(x, pltpu.HBM) for x in operands))


def scores_kernel(sample_total, near, far, corner, placed, out_hbm, out, sem):
    tissues, genes, window = out.shape
    blocks = placed.shape[0]
    per_block = genes // blocks
    row, col = iotas(window, window)
    root = 1.0 / (sample_total ** 0.5)

    def piece(b, kind):
        ref = near.at[b] if b < blocks else far
        return ref[:, kind].reshape(window, window)

    def masked(keep, value):
        return jnp.where(keep, value.astype(jnp.float32), 0.0).astype(jnp.bfloat16)

    labelled = [piece(b, 0) for b in range(blocks + 1)]
    banded = [piece(b, 1) for b in range(blocks + 1)]
    diagonal = [masked(col >= row, band) for band in banded]
    beside = [masked(col < row, band) for band in banded[:blocks - 1]] + [corner[...]]
    nothing = jnp.zeros((window, window), jnp.bfloat16)
    pairs, bands = [], []
    for b in range(blocks):
        pairs.append(jnp.concatenate([labelled[b], labelled[b + 1]], axis=0))
        bands.append(jnp.concatenate([
            jnp.concatenate([diagonal[b], beside[b]], axis=1),
            jnp.concatenate([nothing, diagonal[b + 1]], axis=1),
        ], axis=0))

    copies = []
    step = next(n for n in range(min(7, tissues), 0, -1) if tissues % n == 0)
    for t in range(0, tissues, step):
        for b in range(blocks):
            half = placed[b, pl.ds(t * per_block, step * per_block), :]
            top = jnp.dot(half, pairs[b], preferred_element_type=jnp.float32)
            square = jnp.dot(half, bands[b], preferred_element_type=jnp.float32)
            variance = jnp.sum(square * half.astype(jnp.float32), axis=1, keepdims=True)
            scale = lax.rsqrt(jnp.maximum(variance, 0.0) + 1e-06) * root
            out[pl.ds(t, step), pl.ds(b * per_block, per_block), :] = (top * scale).reshape(step, per_block, window)
        part = pl.ds(t, step)
        copies.append(pltpu.make_async_copy(out.at[part], out_hbm.at[part], sem.at[t // step]))
        copies[-1].start()
    for copy in copies:
        copy.wait()


def on_device(genotype, phenotype, residual, sign_flips, weights, member, gene_start, gene_end):
    by_tissue = weights.transpose(1, 0, 2)
    near, far, corner, placed = reduced_sums(
        genotype, phenotype, residual, sign_flips, gene_start, gene_end, member, by_tissue)
    vmem = pl.BlockSpec(memory_space=pltpu.VMEM)
    scores = pl.pallas_call(
        functools.partial(scores_kernel, genotype.shape[0] * lax.axis_size("samp")),
        out_shape=jax.ShapeDtypeStruct(by_tissue.shape, jnp.float32),
        in_specs=[vmem] * 4,
        out_specs=pl.BlockSpec(memory_space=pltpu.HBM),
        scratch_shapes=[
            pltpu.VMEM(by_tissue.shape, jnp.float32),
            pltpu.SemaphoreType.DMA((by_tissue.shape[0],)),
        ],
        compiler_params=pltpu.CompilerParams(vmem_limit_bytes=VMEM_LIMIT),
        name="scores",
    )(near, far, corner, placed)
    return scores.transpose(1, 0, 2)


def solution(mesh):
    return jax.shard_map(
        on_device,
        mesh=mesh,
        in_specs=(
            P("samp", "snp"),
            P("samp"),
            P("samp"),
            P("samp", None),
            P("snp", None, None),
            P("snp", None),
            P("snp"),
            P("snp"),
        ),
        out_specs=P("snp", None, None),
        check_vma=False,
    )
```

```python
import functools

import jax
import jax.numpy as jnp
from jax import lax
from jax.experimental import pallas as pl
from jax.experimental.pallas import tpu as pltpu
from jax.sharding import PartitionSpec as P

MESH = pl.DeviceIdType.MESH
TILE = 16
PARTS = 2
HALVES = 2
VMEM_LIMIT = 24 * 1024 * 1024


def across(left, right):
    return lax.dot_general(left, right, (((0,), (0,)), ((), ())), preferred_element_type=jnp.float32)


def iotas(rows, cols):
    return (
        lax.broadcasted_iota(jnp.int32, (rows, cols), 0),
        lax.broadcasted_iota(jnp.int32, (rows, cols), 1),
    )


def share_of(rows, count):
    per = -(-rows // (count * TILE)) * TILE
    while rows % per:
        per += TILE
    return per


def square_of(rows):
    tiles, width = rows.shape
    return jnp.concatenate([rows, jnp.zeros((width - tiles, width), jnp.float32)], axis=0)


def sums_kernel(
    count, ring, window,
    geno, phen, resid, flips, starts, ends, member, weights,
    near_out, far_out, corner_out, placed_out,
    phen_v, resid_v, starts_v, ends_v, member_v, weights_v,
    data_v, flips_v, halo_v, back_v,
    main_s, main_r, main_p, main_g,
    late_s, late_r, back_s, back_r, tail_v,
    sums_s, sums_r, sums_t, cols_v, near_v, next_v,
    load_sem, flip_sem, small_sem, halo_ss, halo_rs,
    ms_ss, ms_rs, mg_ss, mg_rs, lt_ss, lt_rs, bc_ss, bc_rs, td_ss, td_rs,
    sm_ss, sm_rs, st_ss, st_rs, nr_ss, nr_rs, bk_ss, bk_rs, fw_ss, fw_rs,
):
    me = lax.axis_index("samp")
    mine = lax.axis_index("snp")
    parity = lax.rem(mine, 2)
    odd, even = parity == 1, parity == 0
    has_before, has_after = mine > 0, mine < ring - 1
    before = jnp.maximum(mine - 1, 0)
    after = jnp.minimum(mine + 1, ring - 1)
    beyond = jnp.minimum(mine + 2, ring - 1)
    partner = mine + 1 - 2 * parity
    samples = data_v.shape[0]
    blocks, owners, _, per, _ = main_g.shape
    snps = blocks * window
    part = samples // PARTS
    split = samples // HALVES
    inverse = 1.0 / (samples * count)

    def peers(body, first=1):
        if count <= 16:
            for dist in range(first, count):
                body(dist)
        else:
            def step(dist, carry):
                body(dist)
                return carry
            lax.fori_loop(first, count, step, 0)

    def collect(wait, got, total, first=1):
        if count <= 16:
            for dist in range(first, count):
                wait(dist)
                total += got[dist].astype(jnp.float32)
            return total

        def step(dist, total):
            wait(dist)
            return total + got[dist].astype(jnp.float32)
        return lax.fori_loop(first, count, step, total)

    def ahead(dist):
        return lax.rem(me + dist, count)

    def behind(dist):
        return lax.rem(me + count - dist, count)

    small = [
        pltpu.make_async_copy(src, dst, small_sem.at[i])
        for i, (src, dst) in enumerate((
            (resid, resid_v), (phen, phen_v), (starts, starts_v), (ends, ends_v),
            (member, member_v), (weights, weights_v),
        ))
    ]
    flip_loads = []
    for i in range(PARTS):
        rows = pl.ds(i * part, part)
        flip_loads.append(pltpu.make_async_copy(flips.at[rows], flips_v.at[rows], flip_sem.at[i]))
    for copy in small[:2] + flip_loads:
        copy.start()
    load = pltpu.make_async_copy(geno, data_v.at[:, pl.ds(0, snps)], load_sem.at[0])
    load.start()

    class Behind:
        def __init__(self, ref):
            self.ref = ref

        def __getitem__(self, dist):
            return self.ref[behind(dist)]

    barrier = pltpu.get_barrier_semaphore()

    def greet(dist, other):
        pl.semaphore_signal(barrier, inc=1, device_id=(ahead(dist), other), device_id_type=MESH)

    peers(lambda dist: greet(dist, partner), 0)
    pl.when(has_before & even)(lambda: greet(0, before))

    @pl.when(has_after & odd)
    def _():
        peers(lambda dist: greet(dist, mine))
        peers(lambda dist: greet(dist, after), 0)
        peers(lambda dist: greet(dist, beyond), 0)

    for copy in small[2:]:
        copy.start()

    for copy in small[:2]:
        copy.wait()
    phen_cols = square_of(phen_v[...]).T
    resid_cols = square_of(resid_v[...]).T
    lanes = phen_v.shape[1]
    for i in range(PARTS):
        flip_loads[i].wait()
        for t in range(i * part // lanes, (i + 1) * part // lanes):
            rows = pl.ds(t * lanes, lanes)
            signs = flips_v[rows, :].astype(jnp.float32)
            labels = jnp.concatenate([signs * resid_cols[:, t:t + 1], phen_cols[:, t:t + 1]], axis=1)
            data_v[rows, pl.ds(snps, window)] = labels.astype(jnp.bfloat16)

    load.wait()
    row, col = iotas(window, window)

    def packed(b):
        left = data_v[:, pl.ds(b * window, window)]
        if b == 0:
            left = jnp.concatenate([left, jnp.ones((samples, 8), jnp.bfloat16)], axis=1)
        products = across(left, data_v[:, pl.ds(b * window, snps + window - b * window)])
        other = products[:window, window:2 * window] if b < blocks - 1 else 0.0
        band = jnp.where(col >= row, products[:window, :window], other)
        scored = products[:window, snps - b * window:]
        main_s[b, :, 0] = scored.astype(jnp.bfloat16).reshape(owners, per, window)
        main_s[b, :, 1] = band.astype(jnp.bfloat16).reshape(owners, per, window)
        if b == 0:
            kinds = sums_s.shape[0]
            kind_of, _ = iotas(kinds, window)
            sums = jnp.zeros((kinds, window), jnp.float32)
            for at in range(blocks + 1):
                total = products[window:window + 1, at * window:(at + 1) * window]
                sums = jnp.where(kind_of == at, total, sums)
            sums_s[...] = sums

    packed(0)

    def remote(src, dst, ss, rs, device):
        return pltpu.make_async_remote_copy(
            src_ref=src, dst_ref=dst, send_sem=ss, recv_sem=rs,
            device_id=device, device_id_type=MESH)

    halos = []
    for i in range(HALVES):
        rows = pl.ds(i * split, split)
        halos.append(remote(
            geno.at[rows, pl.ds(0, window)], halo_v.at[rows],
            halo_ss.at[i], halo_rs.at[i], (me, before)))
    back = remote(
        geno.at[pl.ds(split, samples - split), pl.ds(snps - window, window)], back_v,
        bk_ss.at[0], bk_rs.at[0], (me, after))

    def guarded(index, body):
        if owners == count:
            body()
        else:
            pl.when(index < owners)(body)

    def sums_copy(dist):
        return remote(sums_s, sums_r.at[dist], sm_ss.at[dist], sm_rs.at[dist], (ahead(dist), partner))

    def scatter_copy(b, dist):
        return remote(
            main_s.at[b, ahead(dist)], main_r.at[b, dist],
            ms_ss.at[b, dist], ms_rs.at[b, dist], (ahead(dist), partner))

    def everyone(body, apart, low=0, high=count):
        def one(other):
            if apart is None:
                body(other)
            else:
                pl.when((other != me) | apart)(lambda: body(other))
        if count <= 16:
            for other in range(low, high):
                one(other)
        else:
            def step(other, carry):
                one(other)
                return carry
            lax.fori_loop(low, high, step, 0)

    def gather_copy(b, other, place, source):
        return remote(
            main_p.at[b], main_g.at[b, place], mg_ss.at[b, other], mg_rs.at[b, source], (other, partner))

    def direct_copy(other, place, source):
        return remote(
            main_p.at[0], tail_v.at[place], td_ss.at[other], td_rs.at[source],
            (other, jnp.maximum(mine - 2, 0)))

    forward = remote(main_g.at[0], tail_v, fw_ss.at[0], fw_rs.at[0], (me, before))

    def late_copy(other, source):
        return remote(late_s, late_r.at[source], lt_ss.at[other], lt_rs.at[source], (other, mine))

    def back_copy(other, source):
        return remote(back_s, back_r.at[source], bc_ss.at[other], bc_rs.at[source], (other, before))

    stats = remote(sums_t, next_v, st_ss.at[0], st_rs.at[0], (me, jnp.maximum(mine - 2, 0)))
    near = remote(sums_t, near_v, nr_ss.at[0], nr_rs.at[0], (me, partner))
    further = odd & (mine > 1)

    pl.semaphore_wait(
        barrier,
        count + jnp.where(has_before & even, count, 0)
        + jnp.where(has_after & odd, count, 0) + jnp.where(further, count, 0))
    pl.when(has_before)(halos[0].start)

    @pl.when(has_before & odd)
    def _():
        for copy in halos[1:]:
            copy.start()

    pl.when(has_after & odd)(back.start)
    peers(lambda dist: sums_copy(dist).start(), 0)
    for b in range(blocks - 1):
        peers(lambda dist: guarded(ahead(dist), lambda: scatter_copy(b, dist).start()), 0)
        packed(b + 1)

    @pl.when(even)
    def _():
        for copy in halos:
            copy.wait_recv()
        beside = across(data_v[:, pl.ds(snps - window, window)], halo_v[...])
        band = jnp.where(col >= row, main_s[blocks - 1, :, 1].reshape(window, window).astype(jnp.float32), beside)
        main_s[blocks - 1, :, 1] = band.astype(jnp.bfloat16).reshape(owners, per, window)

    peers(lambda dist: guarded(ahead(dist), lambda: scatter_copy(blocks - 1, dist).start()), 0)

    soon = max(1, count // 8)
    half = window // 2
    half_row, half_col = iotas(half, window)

    def fold(product):
        turned = pltpu.roll(product, half, 1)[:half]
        folded = jnp.where(half_col - half > half_row, product.T[half:], turned)
        return jnp.where(half_col < half, product[half:], folded).astype(jnp.bfloat16)

    def corner():
        halos[0].wait_recv()
        rows = pl.ds(0, split)
        late_s[...] = fold(across(data_v[rows, pl.ds(snps - window, window)], halo_v[rows, :]))
        everyone(lambda other: late_copy(other, me).start(), False, 0, soon)

    for copy in small[2:]:
        copy.wait()
    place(mine * snps, starts_v, ends_v, member_v, weights_v, placed_out)

    sums_t[...] = collect(
        lambda dist: sums_copy(dist).wait_recv(), sums_r, jnp.zeros(sums_t.shape, jnp.float32), 0)
    cols_v[...] = square_of(sums_t[...]).T
    pl.when(even)(near.start)
    pl.when(further)(stats.start)

    def direct(low, high):
        everyone(lambda other: direct_copy(other, me, me).start(), None, low, high)

    def own(b):
        def body():
            total = collect(
                lambda dist: scatter_copy(b, dist).wait_recv(), main_r.at[b],
                jnp.zeros(main_p.shape[1:], jnp.float32), 0)
            row_of, col_of = iotas(per, window)
            row_of = row_of + me * per
            at = cols_v[pl.ds(pl.multiple_of(me * per, per), per), :][:, b:b + 1] * inverse
            scored = total[0] - at * sums_t[blocks:blocks + 1, :]
            main_p[b, 0] = pltpu.roll(scored, 1, 1).astype(main_p.dtype)
            other = sums_t[b + 1:b + 2, :] if b < blocks - 1 else near_v[0:1, :]
            mean_row = jnp.where(col_of >= row_of, sums_t[b:b + 1, :], other) * inverse
            value = total[1] * inverse - at * mean_row
            value = jnp.where(col_of == row_of, value, 2.0 * value)
            main_p[b, 1] = value.astype(main_p.dtype)
            if b == 0:
                pl.when(further)(lambda: direct(0, soon))
            everyone(lambda other: gather_copy(b, other, me, me).start(), None)
        guarded(me, body)

    for b in range(blocks - 1):
        own(b)
    pl.when(has_after & odd)(corner)

    @pl.when(has_before & even)
    def _():
        back.wait_recv()
        back_s[...] = fold(across(back_v[...], data_v[pl.ds(split, samples - split), pl.ds(0, window)]))
        everyone(lambda other: back_copy(other, me).start(), None, 0, max(1, count // 2))

    @pl.when(odd)
    def _():
        near.wait_recv()

    @pl.when(even)
    def _():
        near_v[...] = jnp.zeros_like(near_v)

    own(blocks - 1)
    pl.when(further)(lambda: guarded(me, lambda: direct(soon, count)))
    pl.when(has_after & odd)(lambda: everyone(lambda other: late_copy(other, me).start(), False, soon))
    pl.when(has_before & even)(lambda: everyone(lambda other: back_copy(other, me).start(), None, max(1, count // 2)))

    def gathered(b):
        everyone(lambda other: guarded(
            other, lambda: gather_copy(b, other, other, other).wait_recv()), None)
        near_out[b] = main_g[b]

    pl.when(has_before)(halos[0].wait_send)
    pl.when(has_before & even)(lambda: everyone(lambda other: back_copy(other, me).wait_send(), None))
    pl.when(has_after & odd)(back.wait_send)
    pl.when(has_after & odd)(lambda: everyone(lambda other: late_copy(other, me).wait_send(), False))
    peers(lambda dist: sums_copy(dist).wait_send(), 0)
    for b in range(blocks):
        peers(lambda dist: guarded(ahead(dist), lambda: scatter_copy(b, dist).wait_send()), 0)

    @pl.when(odd)
    def _():
        for copy in halos[1:]:
            copy.wait_send()
        pl.when(further)(stats.wait_send)

    pl.when(even)(near.wait_send)

    def sent():
        for b in range(blocks):
            everyone(lambda other: gather_copy(b, other, me, me).wait_send(), None)
        pl.when(further)(lambda: everyone(lambda other: direct_copy(other, me, me).wait_send(), None))
    guarded(me, sent)

    gathered(0)
    pl.when(odd)(forward.start)

    @pl.when(has_after & odd)
    def _():
        stats.wait_recv()
        folded = collect(
            lambda dist: late_copy(behind(dist), behind(dist)).wait_recv(), Behind(late_r),
            late_s[...].astype(jnp.float32))
        folded = collect(lambda other: back_copy(other, other).wait_recv(), back_r, folded, 0)
        mirrored = jnp.concatenate([folded, folded], axis=0).T
        product = jnp.concatenate([
            pltpu.roll(folded, half, 1), jnp.where(half_col < half, folded, mirrored[half:])], axis=0)
        mean_col = square_of(near_v[...]).T[:, blocks - 1:blocks] * inverse
        value = product * inverse - mean_col * (next_v[0:1, :] * inverse)
        corner_out[...] = jnp.where(col < row, 2.0 * value, 0.0).astype(corner_out.dtype)

    for b in range(1, blocks):
        gathered(b)

    @pl.when(has_after)
    def _():
        @pl.when(even)
        def _():
            beside = main_g[blocks - 1, :, 1].reshape(window, window).astype(jnp.float32)
            corner_out[...] = jnp.where(col < row, beside, 0.0).astype(corner_out.dtype)
            forward.wait_recv()

        pl.when(odd)(lambda: everyone(lambda other: guarded(
            other, lambda: direct_copy(other, other, other).wait_recv()), None))
        far_out[...] = tail_v[...]

    @pl.when(jnp.logical_not(has_after))
    def _():
        corner_out[...] = jnp.zeros_like(corner_out)
        far_out[...] = jnp.zeros_like(far_out)

    pl.when(odd)(forward.wait_send)


def place(offset, starts, ends, member, weights, placed):
    tissues, genes, window = weights.shape
    blocks = placed.shape[0]
    per_block = genes // blocks
    gene_row, gene_col = iotas(genes, genes)

    def upright(row_ref):
        spread = jnp.broadcast_to(row_ref[...].astype(jnp.float32), (genes, genes))
        picked = jnp.where(gene_row == gene_col, spread, 0.0)
        return jnp.sum(picked, axis=1, keepdims=True).astype(jnp.int32)

    first, past = upright(starts), upright(ends)
    gene, lane = iotas(genes, window)
    inside = lane < past - first
    within = first - offset - (gene // per_block) * window
    owned = member[...]
    for t in range(tissues):
        kept = inside & (owned[:, t:t + 1] != 0)
        weights[t] = jnp.where(kept, weights[t].astype(jnp.float32), 0.0).astype(weights.dtype)
    near = lane >= within
    source = (lane - within) & (window - 1)
    for t in range(tissues):
        turned = jnp.take_along_axis(weights[t].astype(jnp.float32), source, axis=1)
        head = jnp.where(near, turned, 0.0).astype(placed.dtype)
        rest = jnp.where(near, 0.0, turned).astype(placed.dtype)
        rows = pl.ds(t * per_block, per_block)
        for b in range(blocks):
            genes_of = slice(b * per_block, (b + 1) * per_block)
            placed[b, rows, pl.ds(0, window)] = head[genes_of]
            placed[b, rows, pl.ds(window, window)] = rest[genes_of]


def reduced_sums(genotype, phenotype, residual, sign_flips, starts, ends, member, weights):
    samples, snps = genotype.shape
    tissues, genes, window = weights.shape
    count, ring = lax.axis_size("samp"), lax.axis_size("snp")
    blocks = snps // window
    per = share_of(window, count)
    owners = window // per
    kinds = -(-(blocks + 1) // 4) * 4
    half, wide = jnp.bfloat16, jnp.float32
    dma = pltpu.SemaphoreType.DMA
    vmem = pl.BlockSpec(memory_space=pltpu.VMEM)
    hbm = pl.BlockSpec(memory_space=pltpu.HBM)
    operands = (
        genotype, phenotype.reshape(-1, window), residual.reshape(-1, window), sign_flips,
        starts.reshape(1, genes), ends.reshape(1, genes), member, weights,
    )
    return pl.pallas_call(
        functools.partial(sums_kernel, count, ring, window),
        out_shape=(
            jax.ShapeDtypeStruct((blocks, owners, 2, per, window), half),
            jax.ShapeDtypeStruct((owners, 2, per, window), half),
            jax.ShapeDtypeStruct((window, window), half),
            jax.ShapeDtypeStruct((blocks, tissues * genes // blocks, 2 * window), half),
        ),
        in_specs=[hbm] * 8,
        out_specs=(vmem,) * 4,
        scratch_shapes=[pltpu.VMEM(x.shape, x.dtype) for x in operands[1:3] + operands[4:]] + [
            pltpu.VMEM((samples, snps + window), half),
            pltpu.VMEM(sign_flips.shape, jnp.int32),
            pltpu.VMEM((samples, window), half),
            pltpu.VMEM((samples - samples // HALVES, window), half),
            pltpu.VMEM((blocks, owners, 2, per, window), half),
            pltpu.VMEM((blocks, count, 2, per, window), half),
            pltpu.VMEM((blocks, 2, per, window), half),
            pltpu.VMEM((blocks, owners, 2, per, window), half),
            pltpu.VMEM((window // 2, window), half),
            pltpu.VMEM((count, window // 2, window), half),
            pltpu.VMEM((window // 2, window), half),
            pltpu.VMEM((count, window // 2, window), half),
            pltpu.VMEM((owners, 2, per, window), half),
            pltpu.VMEM((kinds, window), wide),
            pltpu.VMEM((count, kinds, window), wide),
            pltpu.VMEM((kinds, window), wide),
            pltpu.VMEM((window, window), wide),
            pltpu.VMEM((kinds, window), wide),
            pltpu.VMEM((kinds, window), wide),
            dma((1,)), dma((PARTS,)), dma((6,)), dma((HALVES,)), dma((HALVES,)),
            dma((blocks, count)), dma((blocks, count)), dma((blocks, count)), dma((blocks, count)),
            dma((count,)), dma((count,)), dma((count,)), dma((count,)), dma((count,)), dma((count,)),
            dma((count,)), dma((count,)), dma((1,)), dma((1,)), dma((1,)), dma((1,)),
            dma((1,)), dma((1,)), dma((1,)), dma((1,)),
        ],
        compiler_params=pltpu.CompilerParams(
            collective_id=0, has_side_effects=True, vmem_limit_bytes=VMEM_LIMIT),
        name="sums",
    )(*(pltpu.with_memory_space_constraint(x, pltpu.HBM) for x in operands))


def scores_kernel(sample_total, near, far, corner, placed, out_hbm, out, sem):
    tissues, genes, window = out.shape
    blocks = placed.shape[0]
    per_block = genes // blocks
    row, col = iotas(window, window)
    root = 1.0 / (sample_total ** 0.5)

    def piece(b, kind):
        ref = near.at[b] if b < blocks else far
        return ref[:, kind].reshape(window, window)

    def masked(keep, value):
        return jnp.where(keep, value.astype(jnp.float32), 0.0).astype(jnp.bfloat16)

    labelled = [piece(b, 0) for b in range(blocks + 1)]
    banded = [piece(b, 1) for b in range(blocks + 1)]
    diagonal = [masked(col >= row, band) for band in banded]
    beside = [masked(col < row, band) for band in banded[:blocks - 1]] + [corner[...]]
    nothing = jnp.zeros((window, window), jnp.bfloat16)
    pairs, bands = [], []
    for b in range(blocks):
        pairs.append(jnp.concatenate([labelled[b], labelled[b + 1]], axis=0))
        bands.append(jnp.concatenate([
            jnp.concatenate([diagonal[b], beside[b]], axis=1),
            jnp.concatenate([nothing, diagonal[b + 1]], axis=1),
        ], axis=0))

    copies = []
    step = next(n for n in range(min(7, tissues), 0, -1) if tissues % n == 0)
    for t in range(0, tissues, step):
        for b in range(blocks):
            half = placed[b, pl.ds(t * per_block, step * per_block), :]
            top = jnp.dot(half, pairs[b], preferred_element_type=jnp.float32)
            square = jnp.dot(half, bands[b], preferred_element_type=jnp.float32)
            variance = jnp.sum(square * half.astype(jnp.float32), axis=1, keepdims=True)
            scale = lax.rsqrt(jnp.maximum(variance, 0.0) + 1e-06) * root
            out[pl.ds(t, step), pl.ds(b * per_block, per_block), :] = (top * scale).reshape(step, per_block, window)
        part = pl.ds(t, step)
        copies.append(pltpu.make_async_copy(out.at[part], out_hbm.at[part], sem.at[t // step]))
        copies[-1].start()
    for copy in copies:
        copy.wait()


def on_device(genotype, phenotype, residual, sign_flips, weights, member, gene_start, gene_end):
    by_tissue = weights.transpose(1, 0, 2)
    near, far, corner, placed = reduced_sums(
        genotype, phenotype, residual, sign_flips, gene_start, gene_end, member, by_tissue)
    vmem = pl.BlockSpec(memory_space=pltpu.VMEM)
    scores = pl.pallas_call(
        functools.partial(scores_kernel, genotype.shape[0] * lax.axis_size("samp")),
        out_shape=jax.ShapeDtypeStruct(by_tissue.shape, jnp.float32),
        in_specs=[vmem] * 4,
        out_specs=pl.BlockSpec(memory_space=pltpu.HBM),
        scratch_shapes=[
            pltpu.VMEM(by_tissue.shape, jnp.float32),
            pltpu.SemaphoreType.DMA((by_tissue.shape[0],)),
        ],
        compiler_params=pltpu.CompilerParams(vmem_limit_bytes=VMEM_LIMIT),
        name="scores",
    )(near, far, corner, placed)
    return scores.transpose(1, 0, 2)


def solution(mesh):
    return jax.shard_map(
        on_device,
        mesh=mesh,
        in_specs=(
            P("samp", "snp"),
            P("samp"),
            P("samp"),
            P("samp", None),
            P("snp", None, None),
            P("snp", None),
            P("snp"),
            P("snp"),
        ),
        out_specs=P("snp", None, None),
        check_vma=False,
    )
```
